128 devices in a mesh: grp: 8 (over y_hi, z), gene: 16 (over y_lo, x, core).
Axes of the slice: x: 4, y: 4 (y_hi: 2, y_lo: 2; y = y_hi * 2 + y_lo), z: 4, core: 2. Of those that a mesh axis runs over, the one named last changes fastest.
Arguments:
- counts: int32 [2048, 15360], P('grp', 'gene'), may hold values from 0 to 12
- panels: int32 [15360], P('gene'), may hold values from 0 to 63
- membership: int32 [8, 256], P('grp'), may hold values from 0 to 3, never falling along the last dimension, each value on 1 to 128 neighbouring positions
- w_proj: bfloat16 [15360, 6400], P('gene'), may hold values from -0.0234375 to 0.0234375
- w_qkv_within: bfloat16 [1600, 32, 150], P(None, 'gene'), may hold values from -0.15625 to 0.15625
- w_out_within: bfloat16 [32, 50, 1600], P('gene'), may hold values from -0.4375 to 0.4375
- w_qkv_cross: bfloat16 [1600, 32, 150], P(None, 'gene'), may hold values from -0.15625 to 0.15625
- w_out_cross: bfloat16 [32, 50, 1600], P('gene'), may hold values from -0.4375 to 0.4375
- w_mean: bfloat16 [1600, 15360], P(None, 'gene'), may hold values from -0.25 to 0.25
- w_disp: bfloat16 [1600, 64], replicated, may hold values from -0.25 to 0.25
Outputs:
- cell_loss: float32 [2048], P('grp')
- grad_mean: float32 [1600, 15360], P('grp', 'gene')
- grad_disp: float32 [1600, 64], replicated
The draws below stay inside these ranges and needn't reach their ends.
Inputs may be any that keep to these rules, and one draw needn't show every extreme that they name: `membership`: group numbers never fall along a row; a group has at most 128 cells.
All inputs are finite; a program needn't handle non-finite values.
Results may differ from the reference program's by a relative error of at most 0.00055.
Values may be sent and summed in bfloat16 or wider, within the bound.
A program may use at most 128 MiB of HBM per device.

```python
import math
import jax
import jax.numpy as jnp
import numpy as np
from jax import lax

D = 1600
HEADS = 32
HD = 50
MODULES = 4
PANELS = 64
CELLS_DEV = 256
GROUPS_DEV = 4
GROUP_MOST = 128
GSHARDS = 8
CELLS = 2048
GENES = 15360


def draw_counts(key, part):
    cell_key, count_key = jax.random.split(jax.random.fold_in(key, 11))
    cell_rate = jax.random.randint(cell_key, (CELLS, 1), 1, 4)
    rising = 1 + 4 * jnp.arange(GENES, dtype=jnp.int32) // GENES
    upper = 1 + cell_rate * rising[None, :]
    return jax.random.randint(count_key, (CELLS, GENES), 0, upper).astype(jnp.int32)


def decoder_draw(key, columns):
    scale = D ** (-0.5)
    values = jnp.clip(jax.random.normal(key, (D, columns), jnp.float32), -4.0, 4.0) * scale
    values = jnp.clip(values, -0.25, 0.25)
    return values.astype(jnp.bfloat16)


def draw_w_mean(key, part):
    return decoder_draw(jax.random.fold_in(key, 23), GENES)


def draw_w_disp(key, part):
    return decoder_draw(jax.random.fold_in(key, 37), PANELS)


def plant(result, stream_key, least, top_value):
    shape = result.shape
    index_at = [jax.random.randint(jax.random.fold_in(stream_key, axis), (), 0, shape[axis]) for axis in range(len(shape))]
    result = result.at[tuple(index_at)].set(least)
    longest = shape.index(max(shape))
    index_at[longest] = (index_at[longest] + 1) % shape[longest]
    return result.at[tuple(index_at)].set(top_value)


def shard_levels(stream_key, extent, pieces, least, high):
    factor_of = 1.0
    for axis_at, parts in pieces:
        steps = jax.random.uniform(jax.random.fold_in(jax.random.fold_in(stream_key, 6), axis_at), (parts,), jnp.float32, least / len(pieces), high / len(pieces))
        factor_of = factor_of * jnp.repeat(jnp.exp(steps), extent[axis_at] // parts).reshape((-1,) + (1,) * (len(extent) - 1 - axis_at))
    return factor_of


def split_up(count, total, reach, slope):
    loads = [(1 << 20) // math.isqrt(rank ** slope) + 1 for rank in range(2, count + 1)]
    rest, holding = total - reach - (count - 1), [1] * (count - 1)
    while rest > 0:
        candidates = [i for i in range(count - 1) if holding[i] < reach]
        pool, remaining = sum([loads[i] for i in candidates]), rest
        for i in candidates:
            extra = min(reach - holding[i], max(1, remaining * loads[i] // pool), rest)
            holding[i] = holding[i] + extra
            rest = rest - extra
    return np.array([reach] + holding)


def ragged(stream_key, amount, total, reach, lean):
    if amount == 2:
        one = jax.random.randint(stream_key, (), max(1, total - reach), min(reach, total - 1) + 1)
        return jnp.stack([one, total - one])
    lengths = jnp.asarray(split_up(amount, total, reach, lean), jnp.int32)
    twos = (amount - 1) // 2
    donor, sink = lengths[1:1 + 2 * twos:2], lengths[2:2 + 2 * twos:2]
    margin = jnp.minimum(donor - 1, reach - sink)
    passed = jax.random.randint(jax.random.fold_in(stream_key, 1), (twos,), 0, 1 << 20) % (margin + 1)
    lengths = lengths.at[1:1 + 2 * twos:2].set(donor - passed).at[2:2 + 2 * twos:2].set(sink + passed)
    return lengths[jax.random.permutation(jax.random.fold_in(stream_key, 2), amount)]


def noise(stream_key, shape, deviation, limit, cuts=(), kind=jnp.bfloat16):
    loudness = shard_levels(stream_key, shape, cuts, -0.22, 0.18) if cuts else 1.0
    values = jax.random.normal(stream_key, shape, jnp.float32) * deviation * loudness
    return jnp.minimum(jnp.maximum(values, -limit), limit).astype(kind)


def setup_inputs(seed: int = 0) -> dict:
    key_of = jax.random.split(jax.random.key(seed), 11)
    return {
        "counts": draw_counts(jax.random.fold_in(key_of[10], 71), 0),
        "panels": plant(jax.random.randint(key_of[1], (GENES,), 0, PANELS), jax.random.fold_in(key_of[1], 1), 0, PANELS - 1).astype(jnp.int32),
        "membership": jax.vmap(lambda own: jnp.searchsorted(jnp.cumsum(ragged(own, GROUPS_DEV, CELLS_DEV, GROUP_MOST, 0)), jnp.arange(CELLS_DEV), side="right"))(jax.random.split(key_of[2], GSHARDS)).reshape((GSHARDS, CELLS_DEV)).astype(jnp.int32),
        "w_proj": noise(key_of[3], (GENES, MODULES * D), (4 * GENES) ** -0.5, 0.0234375, ((0, 16),)),
        "w_qkv_within": noise(key_of[4], (D, HEADS, 3 * HD), D ** -0.5, 0.15625, ((1, 16),)),
        "w_out_within": noise(key_of[5], (HEADS, HD, D), (4 * HD) ** -0.5, 0.4375, ((0, 16),)),
        "w_qkv_cross": noise(key_of[6], (D, HEADS, 3 * HD), D ** -0.5, 0.15625, ((1, 16),)),
        "w_out_cross": noise(key_of[7], (HEADS, HD, D), (4 * HD) ** -0.5, 0.4375, ((0, 16),)),
        "w_mean": draw_w_mean(jax.random.fold_in(key_of[10], 71), 0),
        "w_disp": draw_w_disp(jax.random.fold_in(key_of[10], 71), 0),
    }


EPS = 1e-06
FLOOR = 0.3
TARGET = 10000.0
DISP_BASE = 0.5

def rms_rows(values):
    return values * lax.rsqrt(lax.optimization_barrier(jnp.mean(values * values, axis=-1, keepdims=True)) + EPS)

def head_norm(values):
    return values * lax.rsqrt(jnp.maximum(lax.optimization_barrier(jnp.mean(values * values, axis=-1, keepdims=True)), FLOOR))

def split_heads(qkv, heads):
    qkv = qkv.reshape(qkv.shape[0], heads, 3, -1)
    query = head_norm(qkv[:, :, 0]).astype(jnp.bfloat16)
    keys = head_norm(qkv[:, :, 1]).astype(jnp.bfloat16)
    values = qkv[:, :, 2].astype(jnp.bfloat16)
    return (query, keys, values)

def within_cells(query, keys, values, modules):
    rows, heads, width = query.shape
    cells = rows // modules
    q_all = query.astype(jnp.float32).reshape(cells, modules, heads, width)
    k_all = keys.astype(jnp.float32).reshape(cells, modules, heads, width)
    v_all = values.astype(jnp.float32).reshape(cells, modules, heads, width)
    scores = jnp.einsum('cmhd,cnhd->chmn', q_all, k_all) * width ** (-0.5)
    weights = jnp.exp(scores)
    probs = (weights / lax.optimization_barrier(jnp.sum(weights, axis=-1, keepdims=True))).astype(jnp.bfloat16)
    mixed = jnp.einsum('chmn,cnhd->cmhd', probs.astype(jnp.float32), v_all)
    return mixed.astype(jnp.bfloat16).reshape(rows, heads * width)

def across_cells(query, keys, values, groups, modules):
    rows, heads, width = query.shape
    cells = rows // modules
    q_all = query.astype(jnp.float32).reshape(cells, modules, heads, width)
    k_all = keys.astype(jnp.float32).reshape(cells, modules, heads, width)
    v_all = values.astype(jnp.float32).reshape(cells, modules, heads, width)
    scores = jnp.einsum('cmhd,nmhd->mhcn', q_all, k_all) * width ** (-0.5)
    same = groups[:, None] == groups[None, :]
    weights = jnp.where(same[None, None], jnp.exp(scores), 0.0)
    probs = (weights / lax.optimization_barrier(jnp.sum(weights, axis=-1, keepdims=True))).astype(jnp.bfloat16)
    mixed = jnp.einsum('mhcn,nmhd->cmhd', probs.astype(jnp.float32), v_all)
    return mixed.astype(jnp.bfloat16).reshape(rows, heads * width)

def nb_terms(observed, rate, theta):
    total = theta + rate
    log_total = jnp.log(total)
    nll = -(lax.lgamma(observed + theta) - lax.lgamma(theta) - lax.lgamma(observed + 1.0) + theta * (jnp.log(theta) - log_total) + observed * (jnp.log(rate) - log_total))
    d_rate = (theta + observed) / total - observed / rate
    d_theta = -(lax.digamma(observed + theta) - lax.digamma(theta) + jnp.log(theta) + 1.0 - log_total - (theta + observed) / total)
    return (nll, d_rate, d_theta)

def reference(counts, panels, membership, w_proj, w_qkv_within, w_out_within, w_qkv_cross, w_out_cross, w_mean, w_disp):
    flat_within = w_qkv_within.reshape(D, -1)
    flat_cross = w_qkv_cross.reshape(D, -1)
    out_within = w_out_within.reshape(HEADS * HD, D)
    out_cross = w_out_cross.reshape(HEADS * HD, D)

    def encode(block):
        counts_block, groups = block
        observed = counts_block.astype(jnp.float32)
        library = 1.0 + lax.optimization_barrier(jnp.sum(observed, axis=1))
        scaled = jnp.log1p(observed * (TARGET / library)[:, None]).astype(jnp.bfloat16)
        tokens = jnp.dot(scaled, w_proj, preferred_element_type=jnp.float32).reshape(CELLS_DEV * MODULES, D)
        normed = rms_rows(tokens).astype(jnp.bfloat16)
        query, keys, values = split_heads(jnp.dot(normed, flat_within, preferred_element_type=jnp.float32), HEADS)
        mixed = within_cells(query, keys, values, MODULES)
        tokens = tokens + jnp.dot(mixed, out_within, preferred_element_type=jnp.float32)
        normed = rms_rows(tokens).astype(jnp.bfloat16)
        query, keys, values = split_heads(jnp.dot(normed, flat_cross, preferred_element_type=jnp.float32), HEADS)
        mixed = across_cells(query, keys, values, groups, MODULES)
        tokens = tokens + jnp.dot(mixed, out_cross, preferred_element_type=jnp.float32)
        pooled = lax.optimization_barrier(jnp.mean(tokens.reshape(CELLS_DEV, MODULES, D), axis=1))
        return (rms_rows(pooled).astype(jnp.bfloat16), library)
    hidden, library = lax.map(encode, (counts.reshape(GSHARDS, CELLS_DEV, GENES), membership))
    hidden = hidden.reshape(CELLS, D)
    library = library.reshape(CELLS)
    observed = counts.astype(jnp.float32)
    logit = jnp.dot(hidden, w_mean, preferred_element_type=jnp.float32)
    disp = jnp.dot(hidden, w_disp, preferred_element_type=jnp.float32)
    onehot = (panels[None, :] == jnp.arange(PANELS, dtype=jnp.int32)[:, None]).astype(jnp.float32)
    theta = jnp.dot(DISP_BASE + jax.nn.softplus(disp), onehot, precision=lax.Precision.HIGHEST)
    rate_scale = (library / GENES)[:, None]
    rate = rate_scale * jax.nn.softplus(logit)
    nll, d_rate, d_theta = nb_terms(observed, rate, theta)
    norm_scale = CELLS ** (-0.5)
    cell_loss = lax.optimization_barrier(jnp.sum(nll, axis=1)) / GENES
    d_logit = d_rate * rate_scale * jax.nn.sigmoid(logit) * norm_scale
    d_panel = jnp.dot(d_theta, onehot.T, precision=lax.Precision.HIGHEST)
    d_disp = d_panel * jax.nn.sigmoid(disp) * norm_scale
    hidden_f = hidden.astype(jnp.float32)
    dims = (((0,), (0,)), ((), ()))
    grad_mean = lax.dot_general(hidden_f, d_logit, dims, precision=lax.Precision.HIGHEST)
    grad_disp = lax.dot_general(hidden_f, d_disp, dims, precision=lax.Precision.HIGHEST)
    return (cell_loss, grad_mean, grad_disp)
```

```python
import functools
import math

import jax
import jax.numpy as jnp
from jax import lax
from jax.experimental import pallas as pl
from jax.experimental.pallas import tpu as pltpu
from jax.sharding import PartitionSpec as P

EPS = 1e-06
FLOOR = 0.3
TARGET = 10000.0
DISP_BASE = 0.5
MESH = pl.DeviceIdType.MESH
F32 = jnp.float32
BF16 = jnp.bfloat16

NX = 4
NY = 2
NG = 16
NCHIP = 8
NR = 8
NZ = 4
NM = 4
ROWS = 16
LIMIT = 64 * 1024 * 1024 - 256 * 1024
DN_T = (((1,), (1,)), ((), ()))
DN_0 = (((0,), (0,)), ((), ()))


def remote(src, dst, send, recv, axis, to):
    return pltpu.make_async_remote_copy(
        src_ref=src, dst_ref=dst, send_sem=send, recv_sem=recv, device_id={axis: to}, device_id_type=MESH
    )


class Place:
    def __init__(self):
        self.g = lax.axis_index("gene")
        self.core = lax.rem(self.g, 2)
        self.x = lax.rem(self.g // 2, NX)
        self.y = self.g // (2 * NX)
        self.right = self.at(self.y, self.shift(1), self.core)
        self.left = self.at(self.y, self.shift(3), self.core)
        self.other_y = self.at(1 - self.y, self.x, self.core)
        self.other_core = self.at(self.y, self.x, 1 - self.core)

    def shift(self, by):
        return lax.rem(self.x + by, NX)

    def at(self, y, x, core):
        return (y * NX + x) * 2 + core

    def chip(self, y, x):
        return y * NX + x


def greet(axis_peers):
    barrier = pltpu.get_barrier_semaphore()
    for axis, to in axis_peers:
        pl.semaphore_signal(barrier, inc=1, device_id={axis: to}, device_id_type=MESH)
    pl.semaphore_wait(barrier, len(axis_peers))


def near(place):
    return [("gene", t) for t in (place.right, place.left, place.other_y, place.other_core)]


def everyone(place):
    return [("gene", lax.rem(place.g + k, NG)) for k in range(1, NG)]


def rms(values):
    return values * lax.rsqrt(jnp.mean(values * values, axis=-1, keepdims=True) + EPS)


class Scatter:
    @staticmethod
    def scratch(width):
        return [
            pltpu.VMEM((NM, NCHIP, 2, ROWS, width), BF16),
            pltpu.VMEM((NM, NCHIP, ROWS, width), BF16),
            pltpu.VMEM((NM, NCHIP, ROWS, width), BF16),
            pltpu.VMEM((NM, 3, ROWS, width), BF16),
            pltpu.VMEM((NM, 3, ROWS, width), BF16),
            pltpu.VMEM((NM, 2, ROWS, width), BF16),
            pltpu.VMEM((NM, ROWS, width), BF16),
            pltpu.VMEM((NM, ROWS, width), BF16),
            pltpu.VMEM((NM, ROWS, width), F32),
            pltpu.SemaphoreType.DMA((NM, 8)),
            pltpu.SemaphoreType.DMA((NM, 8)),
        ]

    COUNT = 11

    def __init__(self, place, refs):
        (self.part, self.pair, self.chip, self.from_left, self.from_right, self.relay,
         self.y_out, self.y_in, self.mine, self.send, self.recv) = refs
        p = self.place = place
        x, y = p.x, p.y
        ahead, behind, across = p.shift(1), p.shift(3), p.shift(2)
        self.copies = []
        for m in range(NM):
            def go(slot, src, dst, to):
                return remote(src, dst, self.send.at[m, slot], self.recv.at[m, slot], "gene", to)
            self.copies.append([
                go(0, self.part.at[m, :, 1 - p.core], self.pair.at[m], p.other_core),
                go(1, self.chip.at[m, p.chip(0, across)], self.from_left.at[m, 0], p.right),
                go(2, self.chip.at[m, p.chip(1, across)], self.from_right.at[m, 0], p.left),
                go(3, self.chip.at[m, p.chip(1, ahead)], self.from_left.at[m, 2], p.right),
                go(4, self.chip.at[m, p.chip(0, behind)], self.from_right.at[m, 2], p.left),
                go(5, self.relay.at[m, 0], self.from_left.at[m, 1], p.right),
                go(6, self.relay.at[m, 1], self.from_right.at[m, 1], p.left),
                go(7, self.y_out.at[m], self.y_in.at[m], p.other_y),
            ])

    def give(self, m):
        self.copies[m][0].start()

    def spread(self, m):
        self.copies[m][0].wait_recv()
        for q in range(NCHIP):
            self.chip[m, q] = (self.part[m, q, self.place.core].astype(F32) + self.pair[m, q].astype(F32)).astype(BF16)
        for k in (1, 2, 3, 4):
            self.copies[m][k].start()

    def forward(self, m):
        p = self.place
        self.copies[m][1].wait_recv()
        self.relay[m, 0] = (
            self.chip[m, p.chip(0, p.shift(1))].astype(F32) + self.from_left[m, 0].astype(F32)
        ).astype(BF16)
        self.copies[m][5].start()
        self.copies[m][2].wait_recv()
        self.relay[m, 1] = (
            self.chip[m, p.chip(1, p.shift(3))].astype(F32) + self.from_right[m, 0].astype(F32)
        ).astype(BF16)
        self.copies[m][6].start()

    def cross(self, m):
        p = self.place
        for k in (3, 4, 5, 6):
            self.copies[m][k].wait_recv()
        self.y_out[m] = (
            self.chip[m, p.chip(1 - p.y, p.x)].astype(F32)
            + self.from_left[m, 2 - p.y].astype(F32)
            + self.from_right[m, 1 + p.y].astype(F32)
        ).astype(BF16)
        self.copies[m][7].start()
        self.mine[m] = (
            self.chip[m, p.chip(p.y, p.x)].astype(F32)
            + self.from_left[m, 1 + p.y].astype(F32)
            + self.from_right[m, 2 - p.y].astype(F32)
        )

    def take(self, m):
        self.copies[m][7].wait_recv()
        return self.mine[m] + self.y_in[m].astype(F32)

    def drain(self):
        for row in self.copies:
            for copy in row:
                copy.wait_send()


def run_scatter(scatter, produce, consume):
    steps = [produce, scatter.spread, scatter.forward, scatter.cross, consume]
    for t in range(NM + len(steps) - 1):
        for lag, step in enumerate(steps):
            if 0 <= t - lag < NM:
                step(t - lag)


class Gather:
    SLOTS = 15

    def __init__(self, place, block, send, recv, index):
        p = place
        ahead, behind, across = p.shift(1), p.shift(3), p.shift(2)
        y, z, c, x = p.y, 1 - p.y, p.core, p.x

        def go(slot, owner, to):
            ref = block(owner)
            return remote(ref, ref, send.at[index, slot], recv.at[index, slot], "gene", to)

        own, paired = p.at(y, x, c), p.at(z, x, c)
        held = [own, paired, p.at(y, behind, c), p.at(y, ahead, c), p.at(z, behind, c), p.at(z, ahead, c),
                p.at(y, across, c), p.at(z, across, c)]
        self.copies = [
            go(0, own, p.other_y),
            go(1, own, p.right),
            go(2, own, p.left),
            go(3, paired, p.right),
            go(4, paired, p.left),
            go(5, held[2], p.right),
            go(6, held[5], p.left),
        ] + [go(7 + k, held[k], p.other_core) for k in range(8)]
        self.c = self.copies

    def start(self):
        for k in (1, 2, 0, 7):
            self.c[k].start()

    def second(self):
        c = self.c
        c[1].wait_recv()
        c[5].start()
        c[9].start()
        c[0].wait_recv()
        c[3].start()
        c[4].start()
        c[8].start()
        c[2].wait_recv()
        c[10].start()

    def third(self):
        c = self.c
        c[4].wait_recv()
        c[6].start()
        c[12].start()
        c[3].wait_recv()
        c[11].start()

    def finish(self):
        c = self.c
        c[5].wait_recv()
        c[13].start()
        c[6].wait_recv()
        c[14].start()
        for k in range(7, 15):
            c[k].wait_recv()

    def drain(self):
        for copy in self.c:
            copy.wait_send()


def run_gather(gathers):
    for step in ("start", "second", "third", "finish", "drain"):
        for gather in gathers:
            getattr(gather, step)()


class Swap:
    def __init__(self, place, source, slots, send, recv, index):
        self.out, self.into = [], []
        for k in range(1, NG):
            to, frm = lax.rem(place.g + k, NG), lax.rem(place.g + NG - k, NG)
            self.out.append(remote(source(to), slots.at[place.g], send.at[index, k], recv.at[index, place.g], "gene", to))
            self.into.append(remote(source(frm), slots.at[frm], send.at[index, k], recv.at[index, frm], "gene", frm))

    def start(self):
        for copy in self.out:
            copy.start()

    def finish(self):
        for copy in self.into:
            copy.wait_recv()

    def drain(self):
        for copy in self.out:
            copy.wait_send()


def total_of(slots):
    total = slots[0]
    for k in range(1, NG):
        total = total + slots[k]
    return total


def encode_kernel(counts, w_hbm, normed, tokens, library, scaled, weights, tile, slots, w_sem, s_send, s_recv, a_send, a_recv, *refs):
    place = Place()
    width = tokens.shape[-1]
    wide = weights.shape[-1]
    greet(everyone(place))
    loads = [
        pltpu.make_async_copy(w_hbm.at[:, pl.ds((m * width) // 128 * 128, wide)], weights.at[m], w_sem.at[m])
        for m in range(NM)
    ]
    tile[...] = jnp.broadcast_to(jnp.sum(counts[...].astype(F32), axis=0, keepdims=True), tile.shape)
    swap = Swap(place, lambda t: tile, slots, s_send, s_recv, 0)
    swap.start()
    for load in loads:
        load.start()
    slots[place.g] = tile[...]
    swap.finish()
    total = 1.0 + total_of(slots)
    library[...] = total
    factor = TARGET / total[0:1]
    scaled[...] = jnp.log1p(counts[...].astype(F32) * factor).T.astype(BF16)
    scatter = Scatter(place, refs)
    gather = [
        Gather(place, lambda o, m=m: normed.at[m, pl.ds(pl.multiple_of(o * ROWS, ROWS), ROWS), :], a_send, a_recv, m)
        for m in range(NM)
    ]

    def produce(m):
        loads[m].wait()
        skip = (m * width) % 128
        out = jnp.dot(scaled[...], weights[m], preferred_element_type=F32)[:, skip:skip + width]
        scatter.part[m] = out.astype(BF16).reshape(NCHIP, 2, ROWS, width)
        scatter.give(m)

    def consume(m):
        value = scatter.take(m)
        tokens[m] = value
        normed[m, pl.ds(pl.multiple_of(place.g * ROWS, ROWS), ROWS), :] = rms(value).astype(BF16)
        gather[m].start()

    run_scatter(scatter, produce, consume)
    for step in ("second", "third", "finish", "drain"):
        for one in gather:
            getattr(one, step)()
    scatter.drain()
    swap.drain()


def half_sum(values):
    high = values.astype(BF16)
    low = (values - high.astype(F32)).astype(BF16)
    row = lax.broadcasted_iota(jnp.int32, (256, 128), 0)
    col = lax.broadcasted_iota(jnp.int32, (256, 128), 1)
    ones = ((lax.rem(row, 128) // 64) == (col // 64)).astype(BF16)
    return jnp.dot(jnp.concatenate([high, low], axis=1), ones, preferred_element_type=F32)


def heads_of(normed, w_qkv, query, keys, values, head):
    for m in range(NM):
        qkv = lax.dot_general(normed[m], w_qkv[...], DN_T, preferred_element_type=F32)
        for at, ref in ((0, query), (1, keys)):
            part = qkv[:, at * 128:(at + 1) * 128]
            mean = half_sum(part * part) / head
            ref[m] = (part * lax.rsqrt(jnp.maximum(mean, FLOOR))).astype(BF16)
        values[m] = qkv[:, 256:384].astype(BF16)


def within_mix(m, query, keys, values, head):
    q = query[m].astype(F32)
    weights = [jnp.exp(half_sum(q * keys[n].astype(F32)) * head ** (-0.5)) for n in range(NM)]
    total = weights[0] + weights[1] + weights[2] + weights[3]
    mixed = None
    for n in range(NM):
        term = (weights[n] / total).astype(BF16).astype(F32) * values[n].astype(F32)
        mixed = term if mixed is None else mixed + term
    return mixed.astype(BF16)


def cross_mix(m, query, keys, values, same, head):
    lane = lax.broadcasted_iota(jnp.int32, query.shape[1:], 1) // 64
    out = []
    for h in range(2):
        q = jnp.where(lane == h, query[m].astype(F32), 0.0).astype(BF16)
        scores = lax.dot_general(q, keys[m], DN_T, preferred_element_type=F32) * head ** (-0.5)
        weights = jnp.where(same, jnp.exp(scores), 0.0)
        probs = (weights / jnp.sum(weights, axis=-1, keepdims=True)).astype(BF16)
        out.append(jnp.dot(probs, values[m], preferred_element_type=F32))
    return jnp.where(lane == 0, out[0], out[1]).astype(BF16)


def within_kernel(head, normed_in, tokens, w_qkv, w_out, normed, resid, query, keys, values, a_send, a_recv, *refs):
    place = Place()
    width = tokens.shape[-1]
    greet(near(place))
    scatter = Scatter(place, refs)
    gather = [
        Gather(place, lambda o, m=m: normed.at[m, pl.ds(pl.multiple_of(o * ROWS, ROWS), ROWS), :], a_send, a_recv, m)
        for m in range(NM)
    ]
    heads_of(normed_in, w_qkv, query, keys, values, head)

    def produce(m):
        mixed = within_mix(m, query, keys, values, head)
        out = jnp.dot(mixed, w_out[...], preferred_element_type=F32)
        scatter.part[m] = out.astype(BF16).reshape(NCHIP, 2, ROWS, width)
        scatter.give(m)

    def consume(m):
        value = tokens[m] + scatter.take(m)
        resid[m] = value
        normed[m, pl.ds(pl.multiple_of(place.g * ROWS, ROWS), ROWS), :] = rms(value).astype(BF16)
        gather[m].start()

    run_scatter(scatter, produce, consume)
    for step in ("second", "third", "finish", "drain"):
        for one in gather:
            getattr(one, step)()
    scatter.drain()


def cross_kernel(head, normed_in, resid, w_qkv, w_out, groups, hidden, query, keys, values, a_send, a_recv, *refs):
    place = Place()
    width = resid.shape[-1]
    cells = hidden.shape[0]
    greet(near(place))
    scatter = Scatter(place, refs)
    gather = Gather(
        place, lambda o: hidden.at[pl.ds(pl.multiple_of(o * ROWS, ROWS), ROWS), :], a_send, a_recv, 0
    )
    heads_of(normed_in, w_qkv, query, keys, values, head)
    row = jnp.broadcast_to(groups[...].astype(F32), (cells, cells))
    same = row == row.T
    pool = []

    def produce(m):
        mixed = cross_mix(m, query, keys, values, same, head)
        out = jnp.dot(mixed, w_out[...], preferred_element_type=F32)
        scatter.part[m] = out.astype(BF16).reshape(NCHIP, 2, ROWS, width)
        scatter.give(m)

    def consume(m):
        pool.append(resid[m] + scatter.take(m))

    run_scatter(scatter, produce, consume)
    pooled = (pool[0] + pool[1] + pool[2] + pool[3]) * (1.0 / NM)
    hidden[pl.ds(pl.multiple_of(place.g * ROWS, ROWS), ROWS), :] = rms(pooled).astype(BF16)
    run_gather([gather])
    scatter.drain()


class GroupGather:
    SLOTS = 7

    def __init__(self, r, block, send, recv, index):
        z, h = lax.rem(r, NZ), r // NZ
        up, down = lax.rem(z + 1, NZ), lax.rem(z + 3, NZ)
        k = 1 - h

        def at(a, b):
            return a * NZ + b

        def go(slot, owner, to):
            ref = block(owner)
            return remote(ref, ref, send.at[index, slot], recv.at[index, slot], "grp", to)

        self.c = [
            go(0, at(h, z), at(k, z)),
            go(1, at(h, z), at(h, up)),
            go(2, at(h, z), at(h, down)),
            go(3, at(k, z), at(h, up)),
            go(4, at(k, z), at(h, down)),
            go(5, at(h, down), at(h, up)),
            go(6, at(k, up), at(h, down)),
        ]

    def start(self):
        for k in (1, 2, 0):
            self.c[k].start()

    def second(self):
        c = self.c
        c[1].wait_recv()
        c[5].start()
        c[0].wait_recv()
        c[3].start()
        c[4].start()

    def third(self):
        self.c[4].wait_recv()
        self.c[6].start()

    def finish(self):
        for k in (2, 3, 5, 6):
            self.c[k].wait_recv()

    def drain(self):
        for copy in self.c:
            copy.wait_send()


def log_factorials(count):
    return [math.log(math.factorial(k)) for k in range(count)]


def terms(x, theta, logit, rate_scale, norm_scale, most):
    tail = jnp.exp(-jnp.abs(logit))
    soft = jnp.maximum(logit, 0.0) + jnp.log1p(tail)
    sigmoid = jnp.where(logit >= 0, 1.0, tail) / (1.0 + tail)
    rate = rate_scale * soft
    product = jnp.ones_like(theta)
    slope = jnp.zeros_like(theta)
    log_factorial = jnp.zeros_like(theta)
    table = log_factorials(most + 1)
    for k in range(most):
        on = x > k
        term = theta + float(k)
        slope = jnp.where(on, slope * term + product, slope)
        product = jnp.where(on, product * term, product)
        if k:
            log_factorial = jnp.where(on, table[k + 1], log_factorial)
    total = theta + rate
    log_total = jnp.log(total)
    log_theta = jnp.log(theta)
    ratio = (theta + x) / total
    nll = -(
        jnp.log(product) - log_factorial
        + theta * (log_theta - log_total)
        + x * (jnp.log(rate) - log_total)
    )
    d_logit = (ratio - x / rate) * rate_scale * sigmoid * norm_scale
    d_theta = -(slope / product + log_theta + 1.0 - log_total - ratio)
    return nll, d_logit, d_theta


def decode_kernel(
    genes_all, cells_all, panel_count,
    counts, panel_row, panel_col, library, hidden, w_mean, w_disp,
    cell_loss, grad_mean, grad_disp,
    tile, slots, back, piece, columns, field, panel_part, loss, gradient, disp_block,
    s_send, s_recv, h_send, h_recv, v_send, v_recv, f_send, f_recv, o_send, o_recv,
):
    place = Place()
    r = lax.axis_index("grp")
    genes, cells = counts.shape
    width = hidden.shape[1]
    share = width // NR
    parts = 4
    step = genes // parts
    norm_scale = cells_all ** (-0.5)
    greet(everyone(place) + [("grp", lax.rem(r + k, NR)) for k in range(1, NR)])

    own = hidden[pl.ds(pl.multiple_of(place.g * ROWS, ROWS), ROWS), :].astype(F32)
    piece[...] = jnp.zeros_like(piece)
    for k in range(NR):
        piece[k, :, 0:share] = own[:, k * share:(k + 1) * share].astype(BF16)
    rows = pl.ds(pl.multiple_of(place.g * ROWS, ROWS), ROWS)
    out, into = [], []
    for k in range(1, NR):
        to, frm = lax.rem(r + k, NR), lax.rem(r + NR - k, NR)
        out.append(remote(piece.at[to], columns.at[r, rows], h_send.at[k], h_recv.at[r], "grp", to))
        into.append(remote(piece.at[frm], columns.at[frm, rows], h_send.at[k], h_recv.at[frm], "grp", frm))
    for copy in out:
        copy.start()
    columns[r, rows] = piece[r]

    disp = lax.dot_general(w_disp[...], hidden[...], DN_T, preferred_element_type=F32)
    table = DISP_BASE + (jnp.maximum(disp, 0.0) + jnp.log1p(jnp.exp(-jnp.abs(disp))))
    high = table.astype(BF16)
    rest = table - high.astype(F32)
    middle = rest.astype(BF16)
    low = (rest - middle.astype(F32)).astype(BF16)
    tables = jnp.concatenate([high, middle, low], axis=0)
    rate_scale = library[0:1] / genes_all
    panel_part[...] = jnp.zeros_like(panel_part)
    loss[...] = jnp.zeros_like(loss)

    v_gather = Gather(
        place, lambda o: columns.at[:, pl.ds(pl.multiple_of(o * ROWS, ROWS), ROWS), :], v_send, v_recv, 0
    )
    field_gather = [
        GroupGather(r, lambda o, p=p: field.at[o, pl.ds(p * step, step), :], f_send, f_recv, p) for p in range(parts)
    ]
    field_gather.append(
        GroupGather(r, lambda o: field.at[o, pl.ds(genes, panel_count), :], f_send, f_recv, parts)
    )

    def decode(p):
        at = pl.ds(p * step, step)
        x = counts[at, :].astype(F32)
        logit = lax.dot_general(w_mean[at, :], hidden[...], DN_T, preferred_element_type=F32)
        lane = lax.broadcasted_iota(jnp.int32, (step, 3 * panel_count), 1)
        pick = (panel_col[at, :] == lax.rem(lane, panel_count)).astype(F32).astype(BF16)
        theta = jnp.dot(pick, tables, preferred_element_type=F32)
        nll, d_logit, d_theta = terms(x, theta, logit, rate_scale, norm_scale, 12)
        field[r, at, :] = d_logit.astype(BF16)
        field_gather[p].start()
        loss[...] += jnp.sum(nll, axis=0, keepdims=True)
        row = lax.broadcasted_iota(jnp.int32, (step, 128), 1)
        wanted = jnp.where(lax.rem(row, 8) < 4, (row // 8) * 4 + lax.rem(row, 8), -1)
        pick_t = (panel_col[at, :] == wanted).astype(F32).astype(BF16)
        upper = d_theta.astype(BF16)
        lower = (d_theta - upper.astype(F32)).astype(BF16)
        panel_part[...] += lax.dot_general(pick_t, upper, DN_0, preferred_element_type=F32) + lax.dot_general(
            pick_t, lower, DN_0, preferred_element_type=F32
        )

    decode(0)
    for copy in into:
        copy.wait_recv()
    v_gather.start()
    decode(1)
    v_gather.second()
    field_gather[0].second()
    decode(2)
    v_gather.third()
    field_gather[0].third()
    field_gather[1].second()
    decode(3)

    row = lax.broadcasted_iota(jnp.int32, (128, cells), 0)
    both = jnp.where(lax.rem(row, 8) == 4, loss[...], panel_part[...])
    tile[...] = both.reshape(NG, 8, cells)
    first = Swap(place, lambda t: tile.at[t], slots, s_send, s_recv, 0)
    first.start()
    slots[place.g] = tile[place.g]
    v_gather.finish()
    field_gather[1].third()
    field_gather[2].second()
    first.finish()
    summed = total_of(slots)
    cell_loss[...] = summed[4:5] / genes_all
    back[place.g] = summed
    second = Swap(place, lambda t: back.at[place.g], back, s_send, s_recv, 1)
    second.start()
    field_gather[2].third()
    field_gather[3].second()
    second.finish()
    d_panel = jnp.concatenate([back[k, 0:4] for k in range(NG)], axis=0)
    tail = jnp.exp(-jnp.abs(disp))
    d_disp = d_panel * (jnp.where(disp >= 0, 1.0, tail) / (1.0 + tail)) * norm_scale
    field[r, pl.ds(genes, panel_count), :] = d_disp.astype(BF16)
    field_gather[parts].start()
    field_gather[3].third()
    field_gather[parts].second()
    field_gather[parts].third()

    def contract(at, size):
        total = jnp.zeros((size, columns.shape[2]), F32)
        for k in range(NR):
            total = total + jnp.dot(field[k, pl.ds(at, size), :], columns[k], preferred_element_type=F32)
        return total

    field_gather[parts].finish()
    part = contract(genes, panel_count)
    disp_block[r] = part
    spread, arrive = [], []
    for k in range(1, NR):
        to, frm = lax.rem(r + k, NR), lax.rem(r + NR - k, NR)
        spread.append(remote(disp_block.at[r], disp_block.at[r], o_send.at[k], o_recv.at[r], "grp", to))
        arrive.append(remote(disp_block.at[frm], disp_block.at[frm], o_send.at[k], o_recv.at[frm], "grp", frm))
    for copy in spread:
        copy.start()
    for p in range(parts):
        field_gather[p].finish()
        gradient[pl.ds(p * step, step), :] = contract(p * step, step)
    grad_mean[...] = gradient[...].T[0:share]
    for copy in arrive:
        copy.wait_recv()
    for k in range(NR):
        grad_disp[:, k * share:(k + 1) * share] = disp_block[k, :, 0:share]
    for copy in out + spread:
        copy.wait_send()
    for one in [v_gather, first, second] + field_gather:
        one.drain()


def whole():
    return pl.BlockSpec(memory_space=pltpu.VMEM)


def params(number):
    return pltpu.CompilerParams(collective_id=number, has_side_effects=True, vmem_limit_bytes=LIMIT)


def head_weights(w_qkv):
    width, heads, three = w_qkv.shape
    turned = jnp.transpose(w_qkv, (2, 1, 0)).reshape(3, three // 3, heads, width)
    turned = jnp.transpose(turned, (0, 2, 1, 3))
    turned = jnp.pad(turned, ((0, 0), (0, 0), (0, 64 - three // 3), (0, 0)))
    return turned.reshape(3 * heads * 64, width)


def out_weights(w_out):
    heads, head, width = w_out.shape
    return jnp.pad(w_out, ((0, 0), (0, 64 - head), (0, 0))).reshape(heads * 64, width)


def shards(counts, panels, membership, w_proj, w_qkv_within, w_out_within, w_qkv_cross, w_out_cross, w_mean, w_disp):
    cells, genes = counts.shape
    width = w_qkv_within.shape[0]
    head = w_out_within.shape[1]
    genes_all = genes * NG
    cells_all = cells * NR
    panel_count = w_disp.shape[1]
    counts_t = counts.T
    scatter = Scatter.scratch(width)
    gather_sems = [pltpu.SemaphoreType.DMA((NM, Gather.SLOTS))] * 2
    swap_sems = [pltpu.SemaphoreType.DMA((2, NG))] * 2
    block = jax.ShapeDtypeStruct((NM, cells, width), BF16)
    mine = jax.ShapeDtypeStruct((NM, ROWS, width), F32)
    normed, tokens, library = pl.pallas_call(
        encode_kernel,
        name="encode",
        out_shape=(block, mine, jax.ShapeDtypeStruct((8, cells), F32)),
        in_specs=[whole(), pl.BlockSpec(memory_space=pl.ANY)],
        out_specs=(whole(), whole(), whole()),
        scratch_shapes=[
            pltpu.VMEM((cells, genes), BF16),
            pltpu.VMEM((NM, genes, 1664), BF16),
            pltpu.VMEM((8, cells), F32),
            pltpu.VMEM((NG, 8, cells), F32),
            pltpu.SemaphoreType.DMA((NM,)),
        ] + swap_sems + gather_sems + scatter,
        compiler_params=params(0),
    )(counts_t, w_proj)
    heads_scratch = [pltpu.VMEM((NM, cells, 128), BF16)] * 3
    normed, resid = pl.pallas_call(
        functools.partial(within_kernel, head),
        name="within",
        out_shape=(block, mine),
        in_specs=[whole()] * 4,
        out_specs=(whole(), whole()),
        scratch_shapes=heads_scratch + gather_sems + scatter,
        compiler_params=params(1),
    )(normed, tokens, head_weights(w_qkv_within), out_weights(w_out_within))
    hidden = pl.pallas_call(
        functools.partial(cross_kernel, head),
        name="cross",
        out_shape=jax.ShapeDtypeStruct((cells, width), BF16),
        in_specs=[whole()] * 5,
        out_specs=whole(),
        scratch_shapes=heads_scratch + gather_sems + scatter,
        compiler_params=params(2),
    )(normed, resid, head_weights(w_qkv_cross), out_weights(w_out_cross), membership)
    cell_loss, grad_mean, grad_disp = pl.pallas_call(
        functools.partial(decode_kernel, genes_all, cells_all, panel_count),
        name="decode",
        out_shape=(
            jax.ShapeDtypeStruct((1, cells), F32),
            jax.ShapeDtypeStruct((width // NR, genes), F32),
            jax.ShapeDtypeStruct((panel_count, width), F32),
        ),
        in_specs=[whole()] * 7,
        out_specs=(whole(), whole(), whole()),
        scratch_shapes=[
            pltpu.VMEM((NG, 8, cells), F32),
            pltpu.VMEM((NG, 8, cells), F32),
            pltpu.VMEM((NG, 8, cells), F32),
            pltpu.VMEM((NR, ROWS, 256), BF16),
            pltpu.VMEM((NR, cells, 256), BF16),
            pltpu.VMEM((NR, genes + panel_count, cells), BF16),
            pltpu.VMEM((128, cells), F32),
            pltpu.VMEM((1, cells), F32),
            pltpu.VMEM((genes, 256), F32),
            pltpu.VMEM((NR, panel_count, 256), F32),
        ] + swap_sems + [
            pltpu.SemaphoreType.DMA((NR,)),
            pltpu.SemaphoreType.DMA((NR,)),
            pltpu.SemaphoreType.DMA((1, Gather.SLOTS)),
            pltpu.SemaphoreType.DMA((1, Gather.SLOTS)),
            pltpu.SemaphoreType.DMA((5, GroupGather.SLOTS)),
            pltpu.SemaphoreType.DMA((5, GroupGather.SLOTS)),
            pltpu.SemaphoreType.DMA((NR,)),
            pltpu.SemaphoreType.DMA((NR,)),
        ],
        compiler_params=params(3),
    )(counts_t, panels[None, :], panels[:, None], library, hidden, w_mean.T, w_disp.T)
    return cell_loss[0], grad_mean, grad_disp.T


def solution(mesh):
    return jax.shard_map(
        shards,
        mesh=mesh,
        in_specs=(
            P("grp", "gene"),
            P("gene"),
            P("grp", None),
            P("gene", None),
            P(None, "gene", None),
            P("gene", None, None),
            P(None, "gene", None),
            P("gene", None, None),
            P(None, "gene"),
            P(),
        ),
        out_specs=(P("grp"), P("grp", "gene"), P()),
        check_vma=False,
    )
```

```python
import functools
import math

import jax
import jax.numpy as jnp
from jax import lax
from jax.experimental import pallas as pl
from jax.experimental.pallas import tpu as pltpu
from jax.sharding import PartitionSpec as P

EPS = 1e-06
FLOOR = 0.3
TARGET = 10000.0
DISP_BASE = 0.5
MESH = pl.DeviceIdType.MESH
F32 = jnp.float32
BF16 = jnp.bfloat16

NX = 4
NY = 2
NG = 16
NCHIP = 8
NR = 8
NZ = 4
NM = 4
ROWS = 16
LIMIT = 64 * 1024 * 1024 - 256 * 1024
DN_T = (((1,), (1,)), ((), ()))
DN_0 = (((0,), (0,)), ((), ()))


def remote(src, dst, send, recv, axis, to):
    return pltpu.make_async_remote_copy(
        src_ref=src, dst_ref=dst, send_sem=send, recv_sem=recv, device_id={axis: to}, device_id_type=MESH
    )


class Place:
    def __init__(self):
        self.g = lax.axis_index("gene")
        self.core = lax.rem(self.g, 2)
        self.x = lax.rem(self.g // 2, NX)
        self.y = self.g // (2 * NX)
        self.right = self.at(self.y, self.shift(1), self.core)
        self.left = self.at(self.y, self.shift(3), self.core)
        self.other_y = self.at(1 - self.y, self.x, self.core)
        self.other_core = self.at(self.y, self.x, 1 - self.core)

    def shift(self, by):
        return lax.rem(self.x + by, NX)

    def at(self, y, x, core):
        return (y * NX + x) * 2 + core

    def chip(self, y, x):
        return y * NX + x


def greet(axis_peers):
    barrier = pltpu.get_barrier_semaphore()
    for axis, to in axis_peers:
        pl.semaphore_signal(barrier, inc=1, device_id={axis: to}, device_id_type=MESH)
    pl.semaphore_wait(barrier, len(axis_peers))


def near(place):
    return [("gene", t) for t in (place.right, place.left, place.other_y, place.other_core)]


def everyone(place):
    return [("gene", lax.rem(place.g + k, NG)) for k in range(1, NG)]


def rms(values):
    return values * lax.rsqrt(jnp.mean(values * values, axis=-1, keepdims=True) + EPS)


class Scatter:
    @staticmethod
    def scratch(width):
        return [
            pltpu.VMEM((NM, NCHIP, 2, ROWS, width), BF16),
            pltpu.VMEM((NM, NCHIP, ROWS, width), BF16),
            pltpu.VMEM((NM, NCHIP, ROWS, width), BF16),
            pltpu.VMEM((NM, 3, ROWS, width), BF16),
            pltpu.VMEM((NM, 3, ROWS, width), BF16),
            pltpu.VMEM((NM, 2, ROWS, width), BF16),
            pltpu.VMEM((NM, ROWS, width), BF16),
            pltpu.VMEM((NM, ROWS, width), BF16),
            pltpu.VMEM((NM, ROWS, width), F32),
            pltpu.SemaphoreType.DMA((NM, 8)),
            pltpu.SemaphoreType.DMA((NM, 8)),
        ]

    COUNT = 11

    def __init__(self, place, refs):
        (self.part, self.pair, self.chip, self.from_left, self.from_right, self.relay,
         self.y_out, self.y_in, self.mine, self.send, self.recv) = refs
        p = self.place = place
        x, y = p.x, p.y
        ahead, behind, across = p.shift(1), p.shift(3), p.shift(2)
        self.copies = []
        for m in range(NM):
            def go(slot, src, dst, to):
                return remote(src, dst, self.send.at[m, slot], self.recv.at[m, slot], "gene", to)
            self.copies.append([
                go(0, self.part.at[m, :, 1 - p.core], self.pair.at[m], p.other_core),
                go(1, self.chip.at[m, p.chip(0, across)], self.from_left.at[m, 0], p.right),
                go(2, self.chip.at[m, p.chip(1, across)], self.from_right.at[m, 0], p.left),
                go(3, self.chip.at[m, p.chip(1, ahead)], self.from_left.at[m, 2], p.right),
                go(4, self.chip.at[m, p.chip(0, behind)], self.from_right.at[m, 2], p.left),
                go(5, self.relay.at[m, 0], self.from_left.at[m, 1], p.right),
                go(6, self.relay.at[m, 1], self.from_right.at[m, 1], p.left),
                go(7, self.y_out.at[m], self.y_in.at[m], p.other_y),
            ])

    def give(self, m):
        self.copies[m][0].start()

    def spread(self, m):
        self.copies[m][0].wait_recv()
        for q in range(NCHIP):
            self.chip[m, q] = (self.part[m, q, self.place.core].astype(F32) + self.pair[m, q].astype(F32)).astype(BF16)
        for k in (1, 2, 3, 4):
            self.copies[m][k].start()

    def forward(self, m):
        p = self.place
        self.copies[m][1].wait_recv()
        self.relay[m, 0] = (
            self.chip[m, p.chip(0, p.shift(1))].astype(F32) + self.from_left[m, 0].astype(F32)
        ).astype(BF16)
        self.copies[m][5].start()
        self.copies[m][2].wait_recv()
        self.relay[m, 1] = (
            self.chip[m, p.chip(1, p.shift(3))].astype(F32) + self.from_right[m, 0].astype(F32)
        ).astype(BF16)
        self.copies[m][6].start()

    def cross(self, m):
        p = self.place
        for k in (3, 4, 5, 6):
            self.copies[m][k].wait_recv()
        self.y_out[m] = (
            self.chip[m, p.chip(1 - p.y, p.x)].astype(F32)
            + self.from_left[m, 2 - p.y].astype(F32)
            + self.from_right[m, 1 + p.y].astype(F32)
        ).astype(BF16)
        self.copies[m][7].start()
        self.mine[m] = (
            self.chip[m, p.chip(p.y, p.x)].astype(F32)
            + self.from_left[m, 1 + p.y].astype(F32)
            + self.from_right[m, 2 - p.y].astype(F32)
        )

    def take(self, m):
        self.copies[m][7].wait_recv()
        return self.mine[m] + self.y_in[m].astype(F32)

    def drain(self):
        for row in self.copies:
            for copy in row:
                copy.wait_send()


def run_scatter(scatter, produce, consume):
    steps = [produce, scatter.spread, scatter.forward, scatter.cross, consume]
    for t in range(NM + len(steps) - 1):
        for lag, step in enumerate(steps):
            if 0 <= t - lag < NM:
                step(t - lag)


class Gather:
    SLOTS = 15

    def __init__(self, place, block, send, recv, index):
        p = place
        ahead, behind, across = p.shift(1), p.shift(3), p.shift(2)
        y, z, c, x = p.y, 1 - p.y, p.core, p.x

        def go(slot, owner, to):
            ref = block(owner)
            return remote(ref, ref, send.at[index, slot], recv.at[index, slot], "gene", to)

        own, paired = p.at(y, x, c), p.at(z, x, c)
        held = [own, paired, p.at(y, behind, c), p.at(y, ahead, c), p.at(z, behind, c), p.at(z, ahead, c),
                p.at(y, across, c), p.at(z, across, c)]
        self.copies = [
            go(0, own, p.other_y),
            go(1, own, p.right),
            go(2, own, p.left),
            go(3, paired, p.right),
            go(4, paired, p.left),
            go(5, held[2], p.right),
            go(6, held[5], p.left),
        ] + [go(7 + k, held[k], p.other_core) for k in range(8)]
        self.c = self.copies

    def start(self):
        for k in (1, 2, 0, 7):
            self.c[k].start()

    def second(self):
        c = self.c
        c[1].wait_recv()
        c[5].start()
        c[9].start()
        c[0].wait_recv()
        c[3].start()
        c[4].start()
        c[8].start()
        c[2].wait_recv()
        c[10].start()

    def third(self):
        c = self.c
        c[4].wait_recv()
        c[6].start()
        c[12].start()
        c[3].wait_recv()
        c[11].start()

    def finish(self):
        c = self.c
        c[5].wait_recv()
        c[13].start()
        c[6].wait_recv()
        c[14].start()
        for k in range(7, 15):
            c[k].wait_recv()

    def drain(self):
        for copy in self.c:
            copy.wait_send()


class Direct:
    def __init__(self, place, block, send, recv, index):
        p = place
        chip = p.chip(p.y, p.x)
        own = block(p.g)
        self.out, self.pair = [], []
        for k in range(NCHIP):
            to, frm = lax.rem(chip + k, NCHIP) * 2 + p.core, lax.rem(chip + NCHIP - k, NCHIP) * 2 + p.core
            ref = block(frm)
            if k:
                self.out.append(remote(own, own, send.at[index, k], recv.at[index, k], "gene", to))
            self.pair.append(remote(ref, ref, send.at[index, 7 + k if k else 0], recv.at[index, 7 + k if k else 0], "gene", p.other_core))

    def start(self):
        for copy in self.out + self.pair[:1]:
            copy.start()

    def finish(self):
        for k in range(1, NCHIP):
            self.out[k - 1].wait_recv()
            self.pair[k].start()
        for copy in self.pair:
            copy.wait_recv()

    def drain(self):
        for copy in self.out + self.pair:
            copy.wait_send()


class Swap:
    def __init__(self, place, source, slots, send, recv, index):
        self.out, self.into = [], []
        for k in range(1, NG):
            to, frm = lax.rem(place.g + k, NG), lax.rem(place.g + NG - k, NG)
            self.out.append(remote(source(to), slots.at[place.g], send.at[index, k], recv.at[index, place.g], "gene", to))
            self.into.append(remote(source(frm), slots.at[frm], send.at[index, k], recv.at[index, frm], "gene", frm))

    def start(self):
        for copy in self.out:
            copy.start()

    def finish(self):
        for copy in self.into:
            copy.wait_recv()

    def drain(self):
        for copy in self.out:
            copy.wait_send()


def total_of(slots):
    total = slots[0]
    for k in range(1, NG):
        total = total + slots[k]
    return total


def encode_kernel(counts, w_hbm, normed, tokens, library, scaled, weights, tile, slots, w_sem, s_send, s_recv, a_send, a_recv, *refs):
    place = Place()
    width = tokens.shape[-1]
    wide = weights.shape[-1]
    greet(everyone(place))
    loads = [
        pltpu.make_async_copy(w_hbm.at[:, pl.ds((m * width) // 128 * 128, wide)], weights.at[m], w_sem.at[m])
        for m in range(NM)
    ]
    tile[...] = jnp.broadcast_to(jnp.sum(counts[...].astype(F32), axis=0, keepdims=True), tile.shape)
    swap = Swap(place, lambda t: tile, slots, s_send, s_recv, 0)
    swap.start()
    for load in loads:
        load.start()
    slots[place.g] = tile[...]
    swap.finish()
    total = 1.0 + total_of(slots)
    library[...] = total
    factor = TARGET / total[0:1]
    scaled[...] = jnp.log1p(counts[...].astype(F32) * factor).T.astype(BF16)
    scatter = Scatter(place, refs)
    gather = [
        Gather(place, lambda o, m=m: normed.at[m, pl.ds(pl.multiple_of(o * ROWS, ROWS), ROWS), :], a_send, a_recv, m)
        for m in range(NM)
    ]

    def produce(m):
        loads[m].wait()
        skip = (m * width) % 128
        out = jnp.dot(scaled[...], weights[m], preferred_element_type=F32)[:, skip:skip + width]
        scatter.part[m] = out.astype(BF16).reshape(NCHIP, 2, ROWS, width)
        scatter.give(m)

    def consume(m):
        value = scatter.take(m)
        tokens[m] = value
        normed[m, pl.ds(pl.multiple_of(place.g * ROWS, ROWS), ROWS), :] = rms(value).astype(BF16)
        gather[m].start()

    run_scatter(scatter, produce, consume)
    for step in ("second", "third", "finish", "drain"):
        for one in gather:
            getattr(one, step)()
    scatter.drain()
    swap.drain()


def half_sum(values):
    high = values.astype(BF16)
    low = (values - high.astype(F32)).astype(BF16)
    row = lax.broadcasted_iota(jnp.int32, (256, 128), 0)
    col = lax.broadcasted_iota(jnp.int32, (256, 128), 1)
    ones = ((lax.rem(row, 128) // 64) == (col // 64)).astype(BF16)
    return jnp.dot(jnp.concatenate([high, low], axis=1), ones, preferred_element_type=F32)


def heads_of(m, normed, w_qkv, query, keys, values, head):
    qkv = lax.dot_general(normed[m], w_qkv[...], DN_T, preferred_element_type=F32)
    for at, ref in ((0, query), (1, keys)):
        part = qkv[:, at * 128:(at + 1) * 128]
        mean = half_sum(part * part) / head
        ref[m] = (part * lax.rsqrt(jnp.maximum(mean, FLOOR))).astype(BF16)
    values[m] = qkv[:, 256:384].astype(BF16)


def within_mix(m, query, keys, values, head):
    q = query[m].astype(F32)
    weights = [jnp.exp(half_sum(q * keys[n].astype(F32)) * head ** (-0.5)) for n in range(NM)]
    total = weights[0] + weights[1] + weights[2] + weights[3]
    mixed = None
    for n in range(NM):
        term = (weights[n] / total).astype(BF16).astype(F32) * values[n].astype(F32)
        mixed = term if mixed is None else mixed + term
    return mixed.astype(BF16)


def cross_mix(m, query, keys, values, same, head):
    lane = lax.broadcasted_iota(jnp.int32, query.shape[1:], 1) // 64
    out = []
    for h in range(2):
        q = jnp.where(lane == h, query[m].astype(F32), 0.0).astype(BF16)
        scores = lax.dot_general(q, keys[m], DN_T, preferred_element_type=F32) * head ** (-0.5)
        weights = jnp.where(same, jnp.exp(scores), 0.0)
        probs = (weights / jnp.sum(weights, axis=-1, keepdims=True)).astype(BF16)
        out.append(jnp.dot(probs, values[m], preferred_element_type=F32))
    return jnp.where(lane == 0, out[0], out[1]).astype(BF16)


def within_kernel(head, normed_in, tokens, w_qkv, w_out, normed, resid, query, keys, values, a_send, a_recv, *refs):
    place = Place()
    width = tokens.shape[-1]
    greet(near(place))
    scatter = Scatter(place, refs)
    gather = [
        Gather(place, lambda o, m=m: normed.at[m, pl.ds(pl.multiple_of(o * ROWS, ROWS), ROWS), :], a_send, a_recv, m)
        for m in range(NM)
    ]
    for m in range(NM):
        heads_of(m, normed_in, w_qkv, query, keys, values, head)

    def produce(m):
        mixed = within_mix(m, query, keys, values, head)
        out = jnp.dot(mixed, w_out[...], preferred_element_type=F32)
        scatter.part[m] = out.astype(BF16).reshape(NCHIP, 2, ROWS, width)
        scatter.give(m)

    def consume(m):
        value = tokens[m] + scatter.take(m)
        resid[m] = value
        normed[m, pl.ds(pl.multiple_of(place.g * ROWS, ROWS), ROWS), :] = rms(value).astype(BF16)
        gather[m].start()

    run_scatter(scatter, produce, consume)
    for step in ("second", "third", "finish", "drain"):
        for one in gather:
            getattr(one, step)()
    scatter.drain()


def cross_kernel(head, normed_in, resid, w_qkv, w_out, groups, hidden, query, keys, values, a_send, a_recv, *refs):
    place = Place()
    width = resid.shape[-1]
    cells = hidden.shape[0]
    greet(everyone(place))
    scatter = Scatter(place, refs)
    gather = Direct(
        place, lambda o: hidden.at[pl.ds(pl.multiple_of(o * ROWS, ROWS), ROWS), :], a_send, a_recv, 0
    )
    row = jnp.broadcast_to(groups[...].astype(F32), (cells, cells))
    same = row == row.T
    pool = []

    def produce(m):
        heads_of(m, normed_in, w_qkv, query, keys, values, head)
        mixed = cross_mix(m, query, keys, values, same, head)
        out = jnp.dot(mixed, w_out[...], preferred_element_type=F32)
        scatter.part[m] = out.astype(BF16).reshape(NCHIP, 2, ROWS, width)
        scatter.give(m)

    def consume(m):
        pool.append(resid[m] + scatter.take(m))

    run_scatter(scatter, produce, consume)
    pooled = (pool[0] + pool[1] + pool[2] + pool[3]) * (1.0 / NM)
    hidden[pl.ds(pl.multiple_of(place.g * ROWS, ROWS), ROWS), :] = rms(pooled).astype(BF16)
    gather.start()
    gather.finish()
    gather.drain()
    scatter.drain()


class GroupGather:
    SLOTS = 7

    def __init__(self, r, block, send, recv, index):
        z, h = lax.rem(r, NZ), r // NZ
        up, down = lax.rem(z + 1, NZ), lax.rem(z + 3, NZ)
        k = 1 - h

        def at(a, b):
            return a * NZ + b

        def go(slot, owner, to):
            ref = block(owner)
            return remote(ref, ref, send.at[index, slot], recv.at[index, slot], "grp", to)

        self.c = [
            go(0, at(h, z), at(k, z)),
            go(1, at(h, z), at(h, up)),
            go(2, at(h, z), at(h, down)),
            go(3, at(k, z), at(h, up)),
            go(4, at(k, z), at(h, down)),
            go(5, at(h, down), at(h, up)),
            go(6, at(k, up), at(h, down)),
        ]

    def start(self):
        for k in (1, 2, 0):
            self.c[k].start()

    def second(self):
        c = self.c
        c[1].wait_recv()
        c[5].start()
        c[0].wait_recv()
        c[3].start()
        c[4].start()

    def third(self):
        self.c[4].wait_recv()
        self.c[6].start()

    def finish(self):
        for k in (2, 3, 5, 6):
            self.c[k].wait_recv()

    def drain(self):
        for copy in self.c:
            copy.wait_send()


class GroupDirect:
    def __init__(self, r, block, send, recv):
        self.out, self.into = [], []
        for k in range(1, NR):
            to, frm = lax.rem(r + k, NR), lax.rem(r + NR - k, NR)
            self.out.append(remote(block(r), block(r), send.at[k], recv.at[k], "grp", to))
            self.into.append(remote(block(r), block(frm), send.at[k], recv.at[k], "grp", frm))

    def start(self):
        for copy in self.out:
            copy.start()

    def finish(self):
        for copy in self.into:
            copy.wait_recv()

    def drain(self):
        for copy in self.out:
            copy.wait_send()


def log_factorials(count):
    return [math.log(math.factorial(k)) for k in range(count)]


def terms(x, theta, logit, rate_scale, norm_scale, most):
    tail = jnp.exp(-jnp.abs(logit))
    soft = jnp.maximum(logit, 0.0) + jnp.log1p(tail)
    sigmoid = jnp.where(logit >= 0, 1.0, tail) / (1.0 + tail)
    rate = rate_scale * soft
    product = jnp.ones_like(theta)
    slope = jnp.zeros_like(theta)
    log_factorial = jnp.zeros_like(theta)
    table = log_factorials(most + 1)
    for k in range(most):
        on = x > k
        term = theta + float(k)
        slope = jnp.where(on, slope * term + product, slope)
        product = jnp.where(on, product * term, product)
        if k:
            log_factorial = jnp.where(on, table[k + 1], log_factorial)
    total = theta + rate
    log_total = jnp.log(total)
    log_theta = jnp.log(theta)
    ratio = (theta + x) / total
    nll = -(
        jnp.log(product) - log_factorial
        + theta * (log_theta - log_total)
        + x * (jnp.log(rate) - log_total)
    )
    d_logit = (ratio - x / rate) * rate_scale * sigmoid * norm_scale
    d_theta = -(slope / product + log_theta + 1.0 - log_total - ratio)
    return nll, d_logit, d_theta


def decode_kernel(
    genes_all, cells_all, panel_count,
    counts, panel_row, panel_col, library, hidden, w_mean, w_disp,
    cell_loss, gradient, disp_block,
    tile, slots, back, piece, columns, field, panel_part, loss,
    s_send, s_recv, h_send, h_recv, v_send, v_recv, f_send, f_recv, d_send, d_recv, o_send, o_recv,
):
    place = Place()
    r = lax.axis_index("grp")
    genes, cells = counts.shape
    width = hidden.shape[1]
    share = width // NR
    parts = 4
    step = genes // parts
    norm_scale = cells_all ** (-0.5)
    greet(everyone(place) + [("grp", lax.rem(r + k, NR)) for k in range(1, NR)])

    own = hidden[pl.ds(pl.multiple_of(place.g * ROWS, ROWS), ROWS), :].astype(F32)
    piece[...] = jnp.zeros_like(piece)
    for k in range(NR):
        piece[k, :, 0:share] = own[:, k * share:(k + 1) * share].astype(BF16)
    rows = pl.ds(pl.multiple_of(place.g * ROWS, ROWS), ROWS)
    out, into = [], []
    for k in range(1, NR):
        to, frm = lax.rem(r + k, NR), lax.rem(r + NR - k, NR)
        out.append(remote(piece.at[to], columns.at[r, rows], h_send.at[k], h_recv.at[r], "grp", to))
        into.append(remote(piece.at[frm], columns.at[frm, rows], h_send.at[k], h_recv.at[frm], "grp", frm))
    for copy in out:
        copy.start()
    columns[r, rows] = piece[r]

    disp = lax.dot_general(w_disp[...], hidden[...], DN_T, preferred_element_type=F32)
    table = DISP_BASE + (jnp.maximum(disp, 0.0) + jnp.log1p(jnp.exp(-jnp.abs(disp))))
    high = table.astype(BF16)
    rest = table - high.astype(F32)
    middle = rest.astype(BF16)
    low = (rest - middle.astype(F32)).astype(BF16)
    tables = jnp.concatenate([high, middle, low], axis=0)
    rate_scale = library[0:1] / genes_all
    panel_part[...] = jnp.zeros_like(panel_part)
    loss[...] = jnp.zeros_like(loss)

    v_gather = Gather(
        place, lambda o: columns.at[:, pl.ds(pl.multiple_of(o * ROWS, ROWS), ROWS), :], v_send, v_recv, 0
    )
    field_gather = [
        GroupGather(r, lambda o, p=p: field.at[o, pl.ds(p * step, step), :], f_send, f_recv, p) for p in range(parts)
    ]
    disp_gather = GroupDirect(r, lambda o: field.at[o, pl.ds(genes, panel_count), :], d_send, d_recv)
    spread = GroupDirect(r, lambda o: disp_block.at[o], o_send, o_recv)

    def decode(p):
        at = pl.ds(p * step, step)
        x = counts[at, :].astype(F32)
        logit = lax.dot_general(w_mean[at, :], hidden[...], DN_T, preferred_element_type=F32)
        lane = lax.broadcasted_iota(jnp.int32, (step, 3 * panel_count), 1)
        pick = (panel_col[at, :] == lax.rem(lane, panel_count)).astype(F32).astype(BF16)
        theta = jnp.dot(pick, tables, preferred_element_type=F32)
        nll, d_logit, d_theta = terms(x, theta, logit, rate_scale, norm_scale, 12)
        field[r, at, :] = d_logit.astype(BF16)
        field_gather[p].start()
        loss[...] += jnp.sum(nll, axis=0, keepdims=True)
        row = lax.broadcasted_iota(jnp.int32, (step, 128), 1)
        wanted = jnp.where(lax.rem(row, 8) < 4, (row // 8) * 4 + lax.rem(row, 8), -1)
        pick_t = (panel_col[at, :] == wanted).astype(F32).astype(BF16)
        upper = d_theta.astype(BF16)
        lower = (d_theta - upper.astype(F32)).astype(BF16)
        panel_part[...] += lax.dot_general(pick_t, upper, DN_0, preferred_element_type=F32) + lax.dot_general(
            pick_t, lower, DN_0, preferred_element_type=F32
        )

    decode(0)
    for copy in into:
        copy.wait_recv()
    v_gather.start()
    decode(1)
    v_gather.second()
    field_gather[0].second()
    decode(2)
    v_gather.third()
    decode(3)

    row = lax.broadcasted_iota(jnp.int32, (128, cells), 0)
    both = jnp.where(lax.rem(row, 8) == 4, loss[...], panel_part[...])
    tile[...] = both.reshape(NG, 8, cells)
    first = Swap(place, lambda t: tile.at[t], slots, s_send, s_recv, 0)
    first.start()
    slots[place.g] = tile[place.g]
    field_gather[0].third()
    field_gather[1].second()
    first.finish()
    summed = total_of(slots)
    cell_loss[...] = summed[4:5] / genes_all
    back[place.g] = summed
    second = Swap(place, lambda t: back.at[place.g], back, s_send, s_recv, 1)
    second.start()
    v_gather.finish()
    field_gather[1].third()
    second.finish()
    d_panel = jnp.concatenate([back[k, 0:4] for k in range(NG)], axis=0)
    tail = jnp.exp(-jnp.abs(disp))
    d_disp = d_panel * (jnp.where(disp >= 0, 1.0, tail) / (1.0 + tail)) * norm_scale
    field[r, pl.ds(genes, panel_count), :] = d_disp.astype(BF16)
    disp_gather.start()
    field_gather[2].second()
    field_gather[2].third()
    field_gather[3].second()

    def contract(at, size):
        total = jnp.zeros((size, columns.shape[2]), F32)
        for k in range(NR):
            total = total + jnp.dot(field[k, pl.ds(at, size), :], columns[k], preferred_element_type=F32)
        return total

    disp_gather.finish()
    disp_block[r] = contract(genes, panel_count)
    spread.start()
    field_gather[3].third()
    for p in range(parts):
        field_gather[p].finish()
        gradient[pl.ds(p * step, step), :] = contract(p * step, step)
    spread.finish()
    for copy in out:
        copy.wait_send()
    for one in [v_gather, first, second, disp_gather, spread] + field_gather:
        one.drain()


def finish_kernel(gradient, disp_block, loss, cell_loss, grad_mean, grad_disp):
    share = grad_mean.shape[0]
    cell_loss[...] = loss[...]
    grad_mean[...] = gradient[...].T[0:share]
    for k in range(NR):
        grad_disp[:, k * share:(k + 1) * share] = disp_block[k, :, 0:share]


def whole():
    return pl.BlockSpec(memory_space=pltpu.VMEM)


def params(number):
    return pltpu.CompilerParams(collective_id=number, has_side_effects=True, vmem_limit_bytes=LIMIT)


def head_weights(w_qkv):
    width, heads, three = w_qkv.shape
    turned = jnp.transpose(w_qkv, (2, 1, 0)).reshape(3, three // 3, heads, width)
    turned = jnp.transpose(turned, (0, 2, 1, 3))
    turned = jnp.pad(turned, ((0, 0), (0, 0), (0, 64 - three // 3), (0, 0)))
    return turned.reshape(3 * heads * 64, width)


def out_weights(w_out):
    heads, head, width = w_out.shape
    return jnp.pad(w_out, ((0, 0), (0, 64 - head), (0, 0))).reshape(heads * 64, width)


def shards(counts, panels, membership, w_proj, w_qkv_within, w_out_within, w_qkv_cross, w_out_cross, w_mean, w_disp):
    cells, genes = counts.shape
    width = w_qkv_within.shape[0]
    head = w_out_within.shape[1]
    genes_all = genes * NG
    cells_all = cells * NR
    panel_count = w_disp.shape[1]
    counts_t = counts.T
    scatter = Scatter.scratch(width)
    gather_sems = [pltpu.SemaphoreType.DMA((NM, Gather.SLOTS))] * 2
    swap_sems = [pltpu.SemaphoreType.DMA((2, NG))] * 2
    block = jax.ShapeDtypeStruct((NM, cells, width), BF16)
    mine = jax.ShapeDtypeStruct((NM, ROWS, width), F32)
    normed, tokens, library = pl.pallas_call(
        encode_kernel,
        name="encode",
        out_shape=(block, mine, jax.ShapeDtypeStruct((8, cells), F32)),
        in_specs=[whole(), pl.BlockSpec(memory_space=pl.ANY)],
        out_specs=(whole(), whole(), whole()),
        scratch_shapes=[
            pltpu.VMEM((cells, genes), BF16),
            pltpu.VMEM((NM, genes, 1664), BF16),
            pltpu.VMEM((8, cells), F32),
            pltpu.VMEM((NG, 8, cells), F32),
            pltpu.SemaphoreType.DMA((NM,)),
        ] + swap_sems + gather_sems + scatter,
        compiler_params=params(0),
    )(counts_t, w_proj)
    heads_scratch = [pltpu.VMEM((NM, cells, 128), BF16)] * 3
    normed, resid = pl.pallas_call(
        functools.partial(within_kernel, head),
        name="within",
        out_shape=(block, mine),
        in_specs=[whole()] * 4,
        out_specs=(whole(), whole()),
        scratch_shapes=heads_scratch + gather_sems + scatter,
        compiler_params=params(1),
    )(normed, tokens, head_weights(w_qkv_within), out_weights(w_out_within))
    hidden = pl.pallas_call(
        functools.partial(cross_kernel, head),
        name="cross",
        out_shape=jax.ShapeDtypeStruct((cells, width), BF16),
        in_specs=[whole()] * 5,
        out_specs=whole(),
        scratch_shapes=heads_scratch + gather_sems + scatter,
        compiler_params=params(2),
    )(normed, resid, head_weights(w_qkv_cross), out_weights(w_out_cross), membership)
    cell_loss, gradient, disp_block = pl.pallas_call(
        functools.partial(decode_kernel, genes_all, cells_all, panel_count),
        name="decode",
        out_shape=(
            jax.ShapeDtypeStruct((1, cells), F32),
            jax.ShapeDtypeStruct((genes, 256), F32),
            jax.ShapeDtypeStruct((NR, panel_count, 256), F32),
        ),
        in_specs=[whole()] * 7,
        out_specs=(whole(), whole(), whole()),
        scratch_shapes=[
            pltpu.VMEM((NG, 8, cells), F32),
            pltpu.VMEM((NG, 8, cells), F32),
            pltpu.VMEM((NG, 8, cells), F32),
            pltpu.VMEM((NR, ROWS, 256), BF16),
            pltpu.VMEM((NR, cells, 256), BF16),
            pltpu.VMEM((NR, genes + panel_count, cells), BF16),
            pltpu.VMEM((128, cells), F32),
            pltpu.VMEM((1, cells), F32),
        ] + swap_sems + [
            pltpu.SemaphoreType.DMA((NR,)),
            pltpu.SemaphoreType.DMA((NR,)),
            pltpu.SemaphoreType.DMA((1, Gather.SLOTS)),
            pltpu.SemaphoreType.DMA((1, Gather.SLOTS)),
            pltpu.SemaphoreType.DMA((4, GroupGather.SLOTS)),
            pltpu.SemaphoreType.DMA((4, GroupGather.SLOTS)),
            pltpu.SemaphoreType.DMA((NR,)),
            pltpu.SemaphoreType.DMA((NR,)),
            pltpu.SemaphoreType.DMA((NR,)),
            pltpu.SemaphoreType.DMA((NR,)),
        ],
        compiler_params=params(3),
    )(counts_t, panels[None, :], panels[:, None], library, hidden, w_mean.T, w_disp.T)
    cell_loss, grad_mean, grad_disp = pl.pallas_call(
        finish_kernel,
        name="finish",
        out_shape=(
            jax.ShapeDtypeStruct((1, cells), F32),
            jax.ShapeDtypeStruct((width // NR, genes), F32),
            jax.ShapeDtypeStruct((panel_count, width), F32),
        ),
        in_specs=[whole()] * 3,
        out_specs=(whole(), whole(), whole()),
    )(gradient, disp_block, cell_loss)
    return cell_loss[0], grad_mean, grad_disp.T


def solution(mesh):
    return jax.shard_map(
        shards,
        mesh=mesh,
        in_specs=(
            P("grp", "gene"),
            P("gene"),
            P("grp", None),
            P("gene", None),
            P(None, "gene", None),
            P("gene", None, None),
            P(None, "gene", None),
            P("gene", None, None),
            P(None, "gene"),
            P(),
        ),
        out_specs=(P("grp"), P("grp", "gene"), P()),
        check_vma=False,
    )
```

```python
import functools
import math

import jax
import jax.numpy as jnp
from jax import lax
from jax.experimental import pallas as pl
from jax.experimental.pallas import tpu as pltpu
from jax.sharding import PartitionSpec as P

EPS = 1e-06
FLOOR = 0.3
TARGET = 10000.0
DISP_BASE = 0.5
MESH = pl.DeviceIdType.MESH
F32 = jnp.float32
BF16 = jnp.bfloat16

NX = 4
NY = 2
NG = 16
NCHIP = 8
NR = 8
NZ = 4
NM = 4
ROWS = 16
LIMIT = 64 * 1024 * 1024 - 256 * 1024
DN_T = (((1,), (1,)), ((), ()))
DN_0 = (((0,), (0,)), ((), ()))


def remote(src, dst, send, recv, axis, to):
    return pltpu.make_async_remote_copy(
        src_ref=src, dst_ref=dst, send_sem=send, recv_sem=recv, device_id={axis: to}, device_id_type=MESH
    )


class Place:
    def __init__(self):
        self.g = lax.axis_index("gene")
        self.core = lax.rem(self.g, 2)
        self.x = lax.rem(self.g // 2, NX)
        self.y = self.g // (2 * NX)
        self.right = self.at(self.y, self.shift(1), self.core)
        self.left = self.at(self.y, self.shift(3), self.core)
        self.other_y = self.at(1 - self.y, self.x, self.core)
        self.other_core = self.at(self.y, self.x, 1 - self.core)

    def shift(self, by):
        return lax.rem(self.x + by, NX)

    def at(self, y, x, core):
        return (y * NX + x) * 2 + core

    def chip(self, y, x):
        return y * NX + x


def greet(axis_peers):
    barrier = pltpu.get_barrier_semaphore()
    for axis, to in axis_peers:
        pl.semaphore_signal(barrier, inc=1, device_id={axis: to}, device_id_type=MESH)
    pl.semaphore_wait(barrier, len(axis_peers))


def everyone(place):
    return [("gene", lax.rem(place.g + k, NG)) for k in range(1, NG)]


def rms(values):
    return values * lax.rsqrt(jnp.mean(values * values, axis=-1, keepdims=True) + EPS)


class Scatter:
    @staticmethod
    def scratch(width):
        return [
            pltpu.VMEM((NM, NCHIP, ROWS, width), BF16),
            pltpu.VMEM((NM, 3, ROWS, width), BF16),
            pltpu.VMEM((NM, 3, ROWS, width), BF16),
            pltpu.VMEM((NM, 2, ROWS, width), BF16),
            pltpu.VMEM((NM, ROWS, width), BF16),
            pltpu.VMEM((NM, ROWS, width), BF16),
            pltpu.VMEM((NM, ROWS, width), F32),
            pltpu.SemaphoreType.DMA((NM, 7)),
            pltpu.SemaphoreType.DMA((NM, 7)),
        ]

    def __init__(self, place, refs):
        (self.chip, self.from_left, self.from_right, self.relay, self.y_out, self.y_in, self.mine, send, recv) = refs
        p = self.place = place
        ahead, behind, across = p.shift(1), p.shift(3), p.shift(2)
        self.copies = []
        for m in range(NM):
            def go(slot, src, dst, to):
                return remote(src, dst, send.at[m, slot], recv.at[m, slot], "gene", to)
            self.copies.append([
                go(0, self.chip.at[m, p.chip(0, across)], self.from_left.at[m, 0], p.right),
                go(1, self.chip.at[m, p.chip(1, across)], self.from_right.at[m, 0], p.left),
                go(2, self.chip.at[m, p.chip(1, ahead)], self.from_left.at[m, 2], p.right),
                go(3, self.chip.at[m, p.chip(0, behind)], self.from_right.at[m, 2], p.left),
                go(4, self.relay.at[m, 0], self.from_left.at[m, 1], p.right),
                go(5, self.relay.at[m, 1], self.from_right.at[m, 1], p.left),
                go(6, self.y_out.at[m], self.y_in.at[m], p.other_y),
            ])

    def spread(self, m):
        for k in (0, 1, 2, 3):
            self.copies[m][k].start()

    def forward(self, m):
        p = self.place
        self.copies[m][0].wait_recv()
        self.relay[m, 0] = (
            self.chip[m, p.chip(0, p.shift(1))].astype(F32) + self.from_left[m, 0].astype(F32)
        ).astype(BF16)
        self.copies[m][4].start()
        self.copies[m][1].wait_recv()
        self.relay[m, 1] = (
            self.chip[m, p.chip(1, p.shift(3))].astype(F32) + self.from_right[m, 0].astype(F32)
        ).astype(BF16)
        self.copies[m][5].start()

    def cross(self, m):
        p = self.place
        for k in (2, 3, 4, 5):
            self.copies[m][k].wait_recv()
        self.y_out[m] = (
            self.chip[m, p.chip(1 - p.y, p.x)].astype(F32)
            + self.from_left[m, 2 - p.y].astype(F32)
            + self.from_right[m, 1 + p.y].astype(F32)
        ).astype(BF16)
        self.copies[m][6].start()
        self.mine[m] = (
            self.chip[m, p.chip(p.y, p.x)].astype(F32)
            + self.from_left[m, 1 + p.y].astype(F32)
            + self.from_right[m, 2 - p.y].astype(F32)
        )

    def take(self, m):
        self.copies[m][6].wait_recv()
        return self.mine[m] + self.y_in[m].astype(F32)

    def drain(self):
        for row in self.copies:
            for copy in row:
                copy.wait_send()


def run_pipeline(steps, count=NM):
    for t in range(count + len(steps) - 1):
        for lag, step in enumerate(steps):
            if 0 <= t - lag < count:
                step(t - lag)


class Gather:
    SLOTS = 7

    def __init__(self, place, block, send, recv, index):
        p = place
        ahead, behind, across = p.shift(1), p.shift(3), p.shift(2)
        y, z, x = p.y, 1 - p.y, p.x

        def go(slot, owner, to):
            ref = block(owner)
            return remote(ref, ref, send.at[index, slot], recv.at[index, slot], "gene", to)

        own, paired = p.chip(y, x), p.chip(z, x)
        self.c = [
            go(0, own, p.other_y),
            go(1, own, p.right),
            go(2, own, p.left),
            go(3, paired, p.right),
            go(4, paired, p.left),
            go(5, p.chip(y, behind), p.right),
            go(6, p.chip(z, ahead), p.left),
        ]

    def start(self):
        for k in (1, 2, 0):
            self.c[k].start()

    def second(self):
        c = self.c
        c[1].wait_recv()
        c[5].start()
        c[0].wait_recv()
        c[3].start()
        c[4].start()

    def third(self):
        self.c[4].wait_recv()
        self.c[6].start()

    def finish(self):
        for k in (2, 3, 5, 6):
            self.c[k].wait_recv()

    def drain(self):
        for copy in self.c:
            copy.wait_send()


class Direct:
    def __init__(self, place, block, send, recv, index):
        p = place
        chip = p.chip(p.y, p.x)
        own = block(p.g)
        self.out, self.pair = [], []
        for k in range(NCHIP):
            to, frm = lax.rem(chip + k, NCHIP) * 2 + p.core, lax.rem(chip + NCHIP - k, NCHIP) * 2 + p.core
            ref = block(frm)
            if k:
                self.out.append(remote(own, own, send.at[index, k], recv.at[index, k], "gene", to))
            self.pair.append(remote(ref, ref, send.at[index, 7 + k if k else 0], recv.at[index, 7 + k if k else 0], "gene", p.other_core))

    def start(self):
        for copy in self.out + self.pair[:1]:
            copy.start()

    def finish(self):
        for k in range(1, NCHIP):
            self.out[k - 1].wait_recv()
            self.pair[k].start()
        for copy in self.pair:
            copy.wait_recv()

    def drain(self):
        for copy in self.out + self.pair:
            copy.wait_send()


class Swap:
    def __init__(self, place, source, slots, send, recv, index):
        self.out, self.into = [], []
        for k in range(1, NG):
            to, frm = lax.rem(place.g + k, NG), lax.rem(place.g + NG - k, NG)
            self.out.append(remote(source(to), slots.at[place.g], send.at[index, k], recv.at[index, place.g], "gene", to))
            self.into.append(remote(source(frm), slots.at[frm], send.at[index, k], recv.at[index, frm], "gene", frm))

    def start(self):
        for copy in self.out:
            copy.start()

    def finish(self):
        for copy in self.into:
            copy.wait_recv()

    def drain(self):
        for copy in self.out:
            copy.wait_send()


def total_of(slots):
    total = slots[0]
    for k in range(1, NG):
        total = total + slots[k]
    return total


def group_sum(values):
    high = values.astype(BF16)
    low = (values - high.astype(F32)).astype(BF16)
    shape = (values.shape[1], values.shape[1])
    row = lax.broadcasted_iota(jnp.int32, shape, 0) // 64
    col = lax.broadcasted_iota(jnp.int32, shape, 1) // 64
    ones = (row == col).astype(F32).astype(BF16)
    return jnp.dot(high, ones, preferred_element_type=F32) + jnp.dot(low, ones, preferred_element_type=F32)


def heads_of(rows, weights, head):
    parts = [jnp.dot(rows, weights[k], preferred_element_type=F32) for k in range(3)]
    for k in range(2):
        mean = group_sum(parts[k] * parts[k]) / head
        parts[k] = (parts[k] * lax.rsqrt(jnp.maximum(mean, FLOOR))).astype(BF16)
    parts[2] = parts[2].astype(BF16)
    return parts


def turned(values, by):
    if by == 0:
        return values
    row = lax.rem(lax.broadcasted_iota(jnp.int32, values.shape, 0), ROWS)
    count = values.shape[0]
    return jnp.where(row < by, pltpu.roll(values, count - ROWS + by, 0), pltpu.roll(values, by, 0))


def within_mix(query, keys, values, head):
    q, k, v = (part.astype(F32) for part in (query, keys, values))
    count = q.shape[0]
    scores = group_sum(jnp.concatenate([q * turned(k, 4 * d) for d in range(NM)], axis=0))
    weights = [jnp.exp(scores[d * count:(d + 1) * count] * head ** (-0.5)) for d in range(NM)]
    total = weights[0] + weights[1] + weights[2] + weights[3]
    mixed = None
    for d in range(NM):
        term = (weights[d] / total).astype(BF16).astype(F32) * turned(v, 4 * d)
        mixed = term if mixed is None else mixed + term
    return mixed.astype(BF16)


def cross_mix(query, keys, values, same, head):
    lane = lax.broadcasted_iota(jnp.int32, query.shape, 1) // 64
    q = query.astype(F32)
    mixed = jnp.zeros(query.shape, F32)
    for h in range(query.shape[1] // 64):
        one = jnp.where(lane == h, q, 0.0).astype(BF16)
        scores = lax.dot_general(one, keys, DN_T, preferred_element_type=F32) * head ** (-0.5)
        weights = jnp.where(same, jnp.exp(scores), 0.0)
        probs = (weights / jnp.sum(weights, axis=-1, keepdims=True)).astype(BF16)
        mixed = jnp.where(lane == h, jnp.dot(probs, values, preferred_element_type=F32), mixed)
    return mixed.astype(BF16)


def encoder_scratch(width, genes, cells, head):
    half = cells // 2
    raw = [pltpu.VMEM((3, 2, head, width), BF16), pltpu.VMEM((2, head, width), BF16)]
    layer = [
        pltpu.VMEM((3, width, 256), BF16),
        pltpu.VMEM((256, width), BF16),
        pltpu.VMEM((NM, NCHIP, ROWS, width), BF16),
    ]
    return (
        [
            pltpu.VMEM((cells, genes), BF16),
            pltpu.VMEM((NM, genes, 1664), BF16),
            pltpu.VMEM((8, cells), F32),
            pltpu.VMEM((NG, 8, cells), F32),
            pltpu.VMEM((NM, NCHIP, 2, ROWS, width), BF16),
            pltpu.VMEM((NM, NCHIP, ROWS, width), BF16),
            pltpu.VMEM((128, width), F32),
            pltpu.VMEM((NM, ROWS, width), F32),
            pltpu.VMEM((NM, ROWS, width), F32),
            pltpu.VMEM((NM, 2, 2, half, 256), BF16),
            pltpu.VMEM((NM, half, 256), BF16),
            pltpu.VMEM((cells, 128), F32),
            pltpu.SemaphoreType.DMA((NM + 4,)),
        ]
        + raw * 2
        + layer * 2
        + [pltpu.SemaphoreType.DMA((1, NG))] * 2
        + [pltpu.SemaphoreType.DMA((NM,))] * 2
        + [pltpu.SemaphoreType.DMA((NM,))] * 2
        + [pltpu.SemaphoreType.DMA((NM, NM))] * 2
        + [pltpu.SemaphoreType.DMA((2 * NM, Gather.SLOTS))] * 2
        + [pltpu.SemaphoreType.DMA((1, 16))] * 2
        + Scatter.scratch(width) * 3
    )


def encoder_kernel(head, counts, groups, w_hbm, q1_hbm, q2_hbm, o1_hbm, o2_hbm, hidden, library, *refs):
    (scaled, w_proj, tile, slots, halves, pair, padded, tokens, resid, kv, queries, spot, load_sem) = refs[:13]
    raws, layers = refs[13:17], refs[17:23]
    (s_send, s_recv, w_send, w_recv, p_send, p_recv, k_send, k_recv, a_send, a_recv, d_send, d_recv) = refs[23:35]
    sums = refs[35:]
    place = Place()
    width = resid.shape[-1]
    wide = w_proj.shape[-1]
    core, here = place.core, place.chip(place.y, place.x)
    scatter = [Scatter(place, sums[9 * k:9 * k + 9]) for k in range(3)]
    weights, outs, blocks = layers[0::3], layers[1::3], layers[2::3]

    greet(everyone(place))
    tile[...] = jnp.broadcast_to(jnp.sum(counts[...].astype(F32), axis=0, keepdims=True), tile.shape)
    swap = Swap(place, lambda t: tile, slots, s_send, s_recv, 0)
    swap.start()
    small = [
        pltpu.make_async_copy(src, dst, load_sem.at[NM + k])
        for k, (src, dst) in enumerate(zip((q1_hbm, o1_hbm, q2_hbm, o2_hbm), raws))
    ]
    loads = [
        pltpu.make_async_copy(w_hbm.at[:, pl.ds((m * width) // 128 * 128, wide)], w_proj.at[m], load_sem.at[m])
        for m in range(NM)
    ]
    for load in small[:2] + loads + small[2:]:
        load.start()
    slots[place.g] = tile[...]

    lanes = pl.ds(pl.multiple_of(core * 128, 128), 128)
    share = []
    for k in range(2):
        share.append([
            remote(weights[k].at[:, :, lanes], weights[k].at[:, :, lanes], w_send.at[2 * k], w_recv.at[2 * k], "gene", place.other_core),
            remote(outs[k].at[lanes, :], outs[k].at[lanes, :], w_send.at[2 * k + 1], w_recv.at[2 * k + 1], "gene", place.other_core),
        ])

    def prepare(k):
        padded[...] = jnp.zeros_like(padded)
        small[2 * k].wait()
        for a in range(3):
            for h in range(2):
                padded[64 * h:64 * h + head, :] = raws[2 * k][a, h].astype(F32)
            weights[k][a, :, lanes] = padded[...].T.astype(BF16)
        share[k][0].start()
        small[2 * k + 1].wait()
        for h in range(2):
            padded[64 * h:64 * h + head, :] = raws[2 * k + 1][h].astype(F32)
        outs[k][lanes, :] = padded[...].astype(BF16)
        share[k][1].start()

    prepare(0)
    swap.finish()
    total = 1.0 + total_of(slots)
    library[...] = total
    scaled[...] = jnp.log1p(counts[...].astype(F32) * (TARGET / total[0:1])).T.astype(BF16)

    pairs = [
        remote(halves.at[m, :, 1 - core], pair.at[m], p_send.at[m], p_recv.at[m], "gene", place.other_core)
        for m in range(NM)
    ]

    def project(m):
        loads[m].wait()
        skip = (m * width) % 128
        out = jnp.dot(scaled[...], w_proj[m], preferred_element_type=F32)[:, skip:skip + width]
        halves[m] = out.astype(BF16).reshape(NCHIP, 2, ROWS, width)
        pairs[m].start()

    def join(m):
        pairs[m].wait_recv()
        for q in range(NCHIP):
            scatter[0].chip[m, q] = (halves[m, q, core].astype(F32) + pair[m, q].astype(F32)).astype(BF16)
        scatter[0].spread(m)

    def keep(m):
        scatter[0].mine[m] = scatter[0].take(m)

    run_pipeline([project, join, scatter[0].forward, scatter[0].cross, keep])

    gathers = [
        [Gather(place, lambda q, k=k, m=m: blocks[k].at[m, q], a_send, a_recv, k * NM + m) for m in range(NM)]
        for k in range(2)
    ]
    for s in range(NM):
        for m in range(NM):
            tokens[s, 4 * m:4 * m + 4, :] = scatter[0].mine[m, 4 * s:4 * s + 4, :]
        blocks[0][s, here] = rms(tokens[s]).astype(BF16)
        gathers[0][s].start()

    prepare(1)
    cells = 2 * kv.shape[3]
    at = lax.broadcasted_iota(jnp.int32, (cells, cells), 1)
    source = 32 * (lax.rem(at, 128) // ROWS) + ROWS * (at // 128) + lax.rem(at, ROWS)
    order = (lax.broadcasted_iota(jnp.int32, (cells, cells), 0) == source).astype(F32).astype(BF16)
    row = jnp.dot(
        jnp.broadcast_to(groups[...].astype(F32), (128, cells)).astype(BF16), order, preferred_element_type=F32
    )
    spot[...] = row.T
    same = jnp.broadcast_to(spot[lanes, 0:1], (128, cells)) == row
    for copy in share[0]:
        copy.wait_recv()

    def within(s):
        gathers[0][s].finish()
        rows = blocks[0][s].reshape(NCHIP * ROWS, width)
        mixed = within_mix(*heads_of(rows, weights[0], head), head)
        out = jnp.dot(mixed, outs[0][...], preferred_element_type=F32)
        scatter[1].chip[s] = out.astype(BF16).reshape(NCHIP, ROWS, width)
        scatter[1].spread(s)

    def add_within(s):
        tokens[s] = tokens[s] + scatter[1].take(s)

    run_pipeline([
        lambda s: gathers[0][s].second(), lambda s: gathers[0][s].third(), within,
        scatter[1].forward, scatter[1].cross, add_within,
    ])

    for m in range(NM):
        for s in range(NM):
            resid[m, 4 * s:4 * s + 4, :] = tokens[s, 4 * m:4 * m + 4, :]
        blocks[1][m, here] = rms(resid[m]).astype(BF16)
        gathers[1][m].start()
    for copy in share[1]:
        copy.wait_recv()
    trade = [
        remote(kv.at[m, core], kv.at[m, core], k_send.at[m, 0], k_recv.at[m, 0], "gene", place.other_core)
        for m in range(NM)
    ]

    def look(m):
        gathers[1][m].finish()
        rows = blocks[1][m].reshape(NCHIP * ROWS, width)
        queries[m], kv[m, core, 0], kv[m, core, 1] = heads_of(rows, weights[1], head)
        trade[m].start()

    def attend(m):
        trade[m].wait_recv()
        keys = jnp.concatenate([kv[m, 0, 0], kv[m, 1, 0]], axis=0)
        values = jnp.concatenate([kv[m, 0, 1], kv[m, 1, 1]], axis=0)
        mixed = cross_mix(queries[m], keys, values, same, head)
        out = jnp.dot(mixed, outs[1][...], preferred_element_type=F32)
        scatter[2].chip[m] = out.astype(BF16).reshape(NCHIP, ROWS, width)
        scatter[2].spread(m)

    def add_cross(m):
        resid[m] = resid[m] + scatter[2].take(m)

    run_pipeline([
        lambda m: gathers[1][m].second(), lambda m: gathers[1][m].third(), look, attend,
        scatter[2].forward, scatter[2].cross, add_cross,
    ])

    pooled = (resid[0] + resid[1] + resid[2] + resid[3]) * (1.0 / NM)
    hidden[pl.ds(pl.multiple_of(place.g * ROWS, ROWS), ROWS), :] = rms(pooled).astype(BF16)
    last = Direct(
        place, lambda o: hidden.at[pl.ds(pl.multiple_of(o * ROWS, ROWS), ROWS), :], d_send, d_recv, 0
    )
    last.start()
    last.finish()
    for one in scatter + gathers[0] + gathers[1] + [swap, last]:
        one.drain()
    for copy in share[0] + share[1] + pairs + trade:
        copy.wait_send()


class GroupGather:
    SLOTS = 7

    def __init__(self, r, block, send, recv, index):
        z, h = lax.rem(r, NZ), r // NZ
        up, down = lax.rem(z + 1, NZ), lax.rem(z + 3, NZ)
        k = 1 - h

        def at(a, b):
            return a * NZ + b

        def go(slot, owner, to):
            ref = block(owner)
            return remote(ref, ref, send.at[index, slot], recv.at[index, slot], "grp", to)

        self.c = [
            go(0, at(h, z), at(k, z)),
            go(1, at(h, z), at(h, up)),
            go(2, at(h, z), at(h, down)),
            go(3, at(k, z), at(h, up)),
            go(4, at(k, z), at(h, down)),
            go(5, at(h, down), at(h, up)),
            go(6, at(k, up), at(h, down)),
        ]

    def start(self):
        for k in (1, 2, 0):
            self.c[k].start()

    def second(self):
        c = self.c
        c[1].wait_recv()
        c[5].start()
        c[0].wait_recv()
        c[3].start()
        c[4].start()

    def third(self):
        self.c[4].wait_recv()
        self.c[6].start()

    def finish(self):
        for k in (2, 3, 5, 6):
            self.c[k].wait_recv()

    def drain(self):
        for copy in self.c:
            copy.wait_send()


class GroupGatherZ:
    def __init__(self, r, block, send, recv, index, upward):
        z, h = lax.rem(r, NZ), r // NZ
        up, down, across = lax.rem(z + 1, NZ), lax.rem(z + 3, NZ), lax.rem(z + 2, NZ)
        k = 1 - h
        self.upward = upward

        def at(a, b):
            return a * NZ + b

        def go(slot, owner, to):
            ref = block(owner)
            return remote(ref, ref, send.at[index, slot], recv.at[index, slot], "grp", to)

        self.c = [
            go(0, at(h, z), at(h, up)),
            go(1, at(h, z), at(h, down)),
            go(2, at(h, down), at(h, up)) if upward else go(2, at(h, up), at(h, down)),
            go(3, at(h, z), at(k, z)),
            go(4, at(h, down), at(k, z)),
            go(5, at(h, up), at(k, z)),
            go(6, at(h, across), at(k, z)),
        ]

    def start(self):
        for k in (0, 1, 3):
            self.c[k].start()

    def second(self):
        c = self.c
        for k in (0, 1):
            c[k].wait_recv()
            if self.upward == (k == 0):
                c[2].start()
            c[4 + k].start()

    def third(self):
        self.c[2].wait_recv()
        self.c[6].start()

    def finish(self):
        for k in (3, 4, 5, 6):
            self.c[k].wait_recv()

    def drain(self):
        for copy in self.c:
            copy.wait_send()


class GroupDirect:
    def __init__(self, r, block, send, recv):
        self.out, self.into = [], []
        for k in range(1, NR):
            to, frm = lax.rem(r + k, NR), lax.rem(r + NR - k, NR)
            self.out.append(remote(block(r), block(r), send.at[k], recv.at[k], "grp", to))
            self.into.append(remote(block(r), block(frm), send.at[k], recv.at[k], "grp", frm))

    def start(self):
        for copy in self.out:
            copy.start()

    def finish(self):
        for copy in self.into:
            copy.wait_recv()

    def drain(self):
        for copy in self.out:
            copy.wait_send()


def log_factorials(count):
    return [math.log(math.factorial(k)) for k in range(count)]


def terms(x, theta, logit, rate_scale, norm_scale, most):
    tail = jnp.exp(-jnp.abs(logit))
    soft = jnp.maximum(logit, 0.0) + jnp.log1p(tail)
    sigmoid = jnp.where(logit >= 0, 1.0, tail) / (1.0 + tail)
    rate = rate_scale * soft
    product = jnp.ones_like(theta)
    slope = jnp.zeros_like(theta)
    log_factorial = jnp.zeros_like(theta)
    table = log_factorials(most + 1)
    for k in range(most):
        on = x > k
        term = theta + float(k)
        slope = jnp.where(on, slope * term + product, slope)
        product = jnp.where(on, product * term, product)
        if k:
            log_factorial = jnp.where(on, table[k + 1], log_factorial)
    total = theta + rate
    log_total = jnp.log(total)
    log_theta = jnp.log(theta)
    ratio = (theta + x) / total
    nll = -(
        jnp.log(product) - log_factorial
        + theta * (log_theta - log_total)
        + x * (jnp.log(rate) - log_total)
    )
    d_logit = (ratio - x / rate) * rate_scale * sigmoid * norm_scale
    d_theta = -(slope / product + log_theta + 1.0 - log_total - ratio)
    return nll, d_logit, d_theta


def decode_kernel(
    genes_all, cells_all, panel_count,
    counts, panel_row, panel_col, library, hidden, w_mean, w_disp,
    cell_loss, gradient, disp_block,
    tile, slots, back, piece, columns, field, panel_part, loss,
    s_send, s_recv, h_send, h_recv, v_send, v_recv, f_send, f_recv, d_send, d_recv, o_send, o_recv,
):
    place = Place()
    r = lax.axis_index("grp")
    genes, cells = counts.shape
    width = hidden.shape[1]
    share = width // NR
    parts = 4
    step = genes // parts
    norm_scale = cells_all ** (-0.5)
    greet(everyone(place) + [("grp", lax.rem(r + k, NR)) for k in range(1, NR)])

    own = hidden[pl.ds(pl.multiple_of(place.g * ROWS, ROWS), ROWS), :].astype(F32)
    piece[...] = jnp.zeros_like(piece)
    for k in range(NR):
        piece[k, :, 0:share] = own[:, k * share:(k + 1) * share].astype(BF16)
    rows = pl.ds(pl.multiple_of(place.g * ROWS, ROWS), ROWS)
    out, into = [], []
    for k in range(1, NR):
        to, frm = lax.rem(r + k, NR), lax.rem(r + NR - k, NR)
        out.append(remote(piece.at[to], columns.at[r, rows], h_send.at[k], h_recv.at[r], "grp", to))
        into.append(remote(piece.at[frm], columns.at[frm, rows], h_send.at[k], h_recv.at[frm], "grp", frm))
    for copy in out:
        copy.start()
    columns[r, rows] = piece[r]

    disp = lax.dot_general(w_disp[...], hidden[...], DN_T, preferred_element_type=F32)
    table = DISP_BASE + (jnp.maximum(disp, 0.0) + jnp.log1p(jnp.exp(-jnp.abs(disp))))
    high = table.astype(BF16)
    rest = table - high.astype(F32)
    middle = rest.astype(BF16)
    low = (rest - middle.astype(F32)).astype(BF16)
    tables = jnp.concatenate([high, middle, low], axis=0)
    rate_scale = library[0:1] / genes_all
    panel_part[...] = jnp.zeros_like(panel_part)
    loss[...] = jnp.zeros_like(loss)

    v_gather = Direct(
        place, lambda o: columns.at[:, pl.ds(pl.multiple_of(o * ROWS, ROWS), ROWS), :], v_send, v_recv, 0
    )
    field_gather = []
    for p in range(parts):
        block = lambda o, p=p: field.at[o, pl.ds(p * step, step), :]
        field_gather.append(
            GroupGatherZ(r, block, f_send, f_recv, p, p == 1) if p % 2 else GroupGather(r, block, f_send, f_recv, p)
        )
    disp_gather = GroupDirect(r, lambda o: field.at[o, pl.ds(genes, panel_count), :], d_send, d_recv)
    spread = GroupDirect(r, lambda o: disp_block.at[o], o_send, o_recv)

    def decode(p):
        at = pl.ds(p * step, step)
        x = counts[at, :].astype(F32)
        logit = lax.dot_general(w_mean[at, :], hidden[...], DN_T, preferred_element_type=F32)
        lane = lax.broadcasted_iota(jnp.int32, (step, 3 * panel_count), 1)
        pick = (panel_col[at, :] == lax.rem(lane, panel_count)).astype(F32).astype(BF16)
        theta = jnp.dot(pick, tables, preferred_element_type=F32)
        nll, d_logit, d_theta = terms(x, theta, logit, rate_scale, norm_scale, 12)
        field[r, at, :] = d_logit.astype(BF16)
        field_gather[p].start()
        loss[...] += jnp.sum(nll, axis=0, keepdims=True)
        row = lax.broadcasted_iota(jnp.int32, (step, 128), 1)
        wanted = jnp.where(lax.rem(row, 8) < 4, (row // 8) * 4 + lax.rem(row, 8), -1)
        pick_t = (panel_col[at, :] == wanted).astype(F32).astype(BF16)
        upper = d_theta.astype(BF16)
        lower = (d_theta - upper.astype(F32)).astype(BF16)
        panel_part[...] += lax.dot_general(pick_t, upper, DN_0, preferred_element_type=F32) + lax.dot_general(
            pick_t, lower, DN_0, preferred_element_type=F32
        )

    decode(0)
    for copy in into:
        copy.wait_recv()
    v_gather.start()
    decode(1)
    field_gather[0].second()
    decode(2)
    field_gather[1].second()
    field_gather[0].third()
    decode(3)

    row = lax.broadcasted_iota(jnp.int32, (128, cells), 0)
    both = jnp.where(lax.rem(row, 8) == 4, loss[...], panel_part[...])
    tile[...] = both.reshape(NG, 8, cells)
    first = Swap(place, lambda t: tile.at[t], slots, s_send, s_recv, 0)
    first.start()
    slots[place.g] = tile[place.g]
    field_gather[2].second()
    field_gather[1].third()
    first.finish()
    summed = total_of(slots)
    cell_loss[...] = summed[4:5] / genes_all
    back[place.g] = summed
    second = Swap(place, lambda t: back.at[place.g], back, s_send, s_recv, 1)
    second.start()
    v_gather.finish()
    field_gather[2].third()
    field_gather[3].second()
    second.finish()
    d_panel = jnp.concatenate([back[k, 0:4] for k in range(NG)], axis=0)
    tail = jnp.exp(-jnp.abs(disp))
    d_disp = d_panel * (jnp.where(disp >= 0, 1.0, tail) / (1.0 + tail)) * norm_scale
    field[r, pl.ds(genes, panel_count), :] = d_disp.astype(BF16)
    disp_gather.start()
    field_gather[3].third()

    def contract(at, size):
        total = jnp.zeros((size, columns.shape[2]), F32)
        for k in range(NR):
            total = total + jnp.dot(field[k, pl.ds(at, size), :], columns[k], preferred_element_type=F32)
        return total

    def gradient_of(p):
        field_gather[p].finish()
        gradient[pl.ds(p * step, step), :] = contract(p * step, step)

    gradient_of(0)
    gradient_of(1)
    disp_gather.finish()
    disp_block[r] = contract(genes, panel_count)
    spread.start()
    gradient_of(2)
    gradient_of(3)
    spread.finish()
    for copy in out:
        copy.wait_send()
    for one in [v_gather, first, second, disp_gather, spread] + field_gather:
        one.drain()


def finish_kernel(gradient, disp_block, loss, cell_loss, grad_mean, grad_disp):
    share = grad_mean.shape[0]
    cell_loss[...] = loss[...]
    grad_mean[...] = gradient[...].T[0:share]
    for k in range(NR):
        grad_disp[:, k * share:(k + 1) * share] = disp_block[k, :, 0:share]


def whole():
    return pl.BlockSpec(memory_space=pltpu.VMEM)


def params(number):
    return pltpu.CompilerParams(collective_id=number, has_side_effects=True, vmem_limit_bytes=LIMIT)


def head_weights(w_qkv):
    width, heads, three = w_qkv.shape
    turned_w = jnp.transpose(w_qkv, (2, 1, 0)).reshape(3, three // 3, heads, width)
    return jnp.transpose(turned_w, (0, 2, 1, 3))


def shards(counts, panels, membership, w_proj, w_qkv_within, w_out_within, w_qkv_cross, w_out_cross, w_mean, w_disp):
    cells, genes = counts.shape
    width = w_qkv_within.shape[0]
    head = w_out_within.shape[1]
    genes_all = genes * NG
    cells_all = cells * NR
    panel_count = w_disp.shape[1]
    counts_t = counts.T
    swap_sems = [pltpu.SemaphoreType.DMA((2, NG))] * 2
    hidden, library = pl.pallas_call(
        functools.partial(encoder_kernel, head),
        name="encoder",
        out_shape=(jax.ShapeDtypeStruct((cells, width), BF16), jax.ShapeDtypeStruct((8, cells), F32)),
        in_specs=[whole()] * 2 + [pl.BlockSpec(memory_space=pl.ANY)] * 5,
        out_specs=(whole(), whole()),
        scratch_shapes=encoder_scratch(width, genes, cells, head),
        compiler_params=params(0),
    )(counts_t, membership, w_proj, head_weights(w_qkv_within), head_weights(w_qkv_cross), w_out_within, w_out_cross)
    cell_loss, gradient, disp_block = pl.pallas_call(
        functools.partial(decode_kernel, genes_all, cells_all, panel_count),
        name="decode",
        out_shape=(
            jax.ShapeDtypeStruct((1, cells), F32),
            jax.ShapeDtypeStruct((genes, 256), F32),
            jax.ShapeDtypeStruct((NR, panel_count, 256), F32),
        ),
        in_specs=[whole()] * 7,
        out_specs=(whole(), whole(), whole()),
        scratch_shapes=[
            pltpu.VMEM((NG, 8, cells), F32),
            pltpu.VMEM((NG, 8, cells), F32),
            pltpu.VMEM((NG, 8, cells), F32),
            pltpu.VMEM((NR, ROWS, 256), BF16),
            pltpu.VMEM((NR, cells, 256), BF16),
            pltpu.VMEM((NR, genes + panel_count, cells), BF16),
            pltpu.VMEM((128, cells), F32),
            pltpu.VMEM((1, cells), F32),
        ] + swap_sems + [
            pltpu.SemaphoreType.DMA((NR,)),
            pltpu.SemaphoreType.DMA((NR,)),
            pltpu.SemaphoreType.DMA((1, 16)),
            pltpu.SemaphoreType.DMA((1, 16)),
            pltpu.SemaphoreType.DMA((4, GroupGather.SLOTS)),
            pltpu.SemaphoreType.DMA((4, GroupGather.SLOTS)),
            pltpu.SemaphoreType.DMA((NR,)),
            pltpu.SemaphoreType.DMA((NR,)),
            pltpu.SemaphoreType.DMA((NR,)),
            pltpu.SemaphoreType.DMA((NR,)),
        ],
        compiler_params=params(3),
    )(counts_t, panels[None, :], panels[:, None], library, hidden, w_mean.T, w_disp.T)
    cell_loss, grad_mean, grad_disp = pl.pallas_call(
        finish_kernel,
        name="finish",
        out_shape=(
            jax.ShapeDtypeStruct((1, cells), F32),
            jax.ShapeDtypeStruct((width // NR, genes), F32),
            jax.ShapeDtypeStruct((panel_count, width), F32),
        ),
        in_specs=[whole()] * 3,
        out_specs=(whole(), whole(), whole()),
    )(gradient, disp_block, cell_loss)
    return cell_loss[0], grad_mean, grad_disp.T


def solution(mesh):
    return jax.shard_map(
        shards,
        mesh=mesh,
        in_specs=(
            P("grp", "gene"),
            P("gene"),
            P("grp", None),
            P("gene", None),
            P(None, "gene", None),
            P("gene", None, None),
            P(None, "gene", None),
            P("gene", None, None),
            P(None, "gene"),
            P(),
        ),
        out_specs=(P("grp"), P("grp", "gene"), P()),
        check_vma=False,
    )
```

```python
import functools
import math

import jax
import jax.numpy as jnp
from jax import lax
from jax.experimental import pallas as pl
from jax.experimental.pallas import tpu as pltpu
from jax.sharding import PartitionSpec as P

EPS = 1e-06
FLOOR = 0.3
TARGET = 10000.0
DISP_BASE = 0.5
MESH = pl.DeviceIdType.MESH
F32 = jnp.float32
BF16 = jnp.bfloat16

NX = 4
NY = 2
NG = 16
NCHIP = 8
NR = 8
NZ = 4
NM = 4
ROWS = 16
LIMIT = 64 * 1024 * 1024 - 256 * 1024
DN_T = (((1,), (1,)), ((), ()))
DN_0 = (((0,), (0,)), ((), ()))


def remote(src, dst, send, recv, axis, to):
    return pltpu.make_async_remote_copy(
        src_ref=src, dst_ref=dst, send_sem=send, recv_sem=recv, device_id={axis: to}, device_id_type=MESH
    )


class Place:
    def __init__(self):
        self.g = lax.axis_index("gene")
        self.core = lax.rem(self.g, 2)
        self.x = lax.rem(self.g // 2, NX)
        self.y = self.g // (2 * NX)
        self.right = self.at(self.y, self.shift(1), self.core)
        self.left = self.at(self.y, self.shift(3), self.core)
        self.other_y = self.at(1 - self.y, self.x, self.core)
        self.other_core = self.at(self.y, self.x, 1 - self.core)

    def shift(self, by):
        return lax.rem(self.x + by, NX)

    def at(self, y, x, core):
        return (y * NX + x) * 2 + core

    def chip(self, y, x):
        return y * NX + x


def greet(axis_peers):
    barrier = pltpu.get_barrier_semaphore()
    for axis, to in axis_peers:
        pl.semaphore_signal(barrier, inc=1, device_id={axis: to}, device_id_type=MESH)
    pl.semaphore_wait(barrier, len(axis_peers))


def everyone(place):
    return [("gene", lax.rem(place.g + k, NG)) for k in range(1, NG)]


def rms(values):
    return values * lax.rsqrt(jnp.mean(values * values, axis=-1, keepdims=True) + EPS)


class Scatter:
    @staticmethod
    def scratch(width):
        return [
            pltpu.VMEM((NM, NCHIP, ROWS, width), BF16),
            pltpu.VMEM((NM, 3, ROWS, width), BF16),
            pltpu.VMEM((NM, 3, ROWS, width), BF16),
            pltpu.VMEM((NM, 2, ROWS, width), BF16),
            pltpu.VMEM((NM, ROWS, width), BF16),
            pltpu.VMEM((NM, ROWS, width), BF16),
            pltpu.VMEM((NM, ROWS, width), F32),
            pltpu.VMEM((2, NX, ROWS, width), BF16),
            pltpu.SemaphoreType.DMA((NM, 7)),
            pltpu.SemaphoreType.DMA((NM, 7)),
        ]

    def __init__(self, place, refs):
        (self.chip, self.from_left, self.from_right, self.relay, self.y_out, self.y_in, self.mine, four, send, recv) = refs
        self.send, self.recv = send, recv
        p = self.place = place
        ahead, behind, across = p.shift(1), p.shift(3), p.shift(2)
        self.copies, self.turned = [], {}
        for m in range(NM):
            if m % 2:
                self.turned[m] = ScatterY(self, m, four.at[m // 2], 1 if m == 1 else -1)
                self.copies.append(self.turned[m].c)
                continue

            def go(slot, src, dst, to):
                return remote(src, dst, send.at[m, slot], recv.at[m, slot], "gene", to)
            self.copies.append([
                go(0, self.chip.at[m, p.chip(0, across)], self.from_left.at[m, 0], p.right),
                go(1, self.chip.at[m, p.chip(1, across)], self.from_right.at[m, 0], p.left),
                go(2, self.chip.at[m, p.chip(1, ahead)], self.from_left.at[m, 2], p.right),
                go(3, self.chip.at[m, p.chip(0, behind)], self.from_right.at[m, 2], p.left),
                go(4, self.relay.at[m, 0], self.from_left.at[m, 1], p.right),
                go(5, self.relay.at[m, 1], self.from_right.at[m, 1], p.left),
                go(6, self.y_out.at[m], self.y_in.at[m], p.other_y),
            ])

    def spread(self, m):
        if m in self.turned:
            return self.turned[m].spread()
        for k in (0, 1, 2, 3):
            self.copies[m][k].start()

    def forward(self, m):
        if m in self.turned:
            return self.turned[m].forward()
        p = self.place
        self.copies[m][0].wait_recv()
        self.relay[m, 0] = (
            self.chip[m, p.chip(0, p.shift(1))].astype(F32) + self.from_left[m, 0].astype(F32)
        ).astype(BF16)
        self.copies[m][4].start()
        self.copies[m][1].wait_recv()
        self.relay[m, 1] = (
            self.chip[m, p.chip(1, p.shift(3))].astype(F32) + self.from_right[m, 0].astype(F32)
        ).astype(BF16)
        self.copies[m][5].start()

    def cross(self, m):
        if m in self.turned:
            return self.turned[m].cross()
        p = self.place
        for k in (2, 3, 4, 5):
            self.copies[m][k].wait_recv()
        self.y_out[m] = (
            self.chip[m, p.chip(1 - p.y, p.x)].astype(F32)
            + self.from_left[m, 2 - p.y].astype(F32)
            + self.from_right[m, 1 + p.y].astype(F32)
        ).astype(BF16)
        self.copies[m][6].start()
        self.mine[m] = (
            self.chip[m, p.chip(p.y, p.x)].astype(F32)
            + self.from_left[m, 1 + p.y].astype(F32)
            + self.from_right[m, 2 - p.y].astype(F32)
        )

    def take(self, m):
        if m in self.turned:
            return self.turned[m].take()
        self.copies[m][6].wait_recv()
        return self.mine[m] + self.y_in[m].astype(F32)

    def drain(self):
        for row in self.copies:
            for copy in row:
                copy.wait_send()


class ScatterY:
    def __init__(self, base, m, y_four, way):
        p = base.place
        self.base, self.m, self.four = base, m, y_four
        to, back = (p.right, p.left) if way > 0 else (p.left, p.right)
        ahead, behind = (p.shift(1), p.shift(3)) if way > 0 else (p.shift(3), p.shift(1))
        self.order = (p.shift(2), behind, ahead)
        self.outgoing = (base.relay.at[m, 0], base.relay.at[m, 1], base.y_out.at[m])
        self.incoming = (base.from_left.at[m, 0], base.from_right.at[m, 0], base.from_left.at[m, 1])

        def go(slot, src, dst, device):
            return remote(src, dst, base.send.at[m, slot], base.recv.at[m, slot], "gene", device)

        self.c = [go(0, base.chip.at[m, pl.ds((1 - p.y) * NX, NX)], y_four, p.other_y)] + [
            go(1 + k, self.outgoing[k], self.incoming[k], (to, back, to)[k]) for k in range(3)
        ]

    def spread(self):
        self.c[0].start()

    def total(self, x):
        p = self.base.place
        return self.base.chip[self.m, p.chip(p.y, x)].astype(F32) + self.four[x].astype(F32)

    def forward(self):
        self.c[0].wait_recv()
        for k in (0, 1):
            self.outgoing[k][...] = self.total(self.order[k]).astype(BF16)
            self.c[1 + k].start()
        self.base.mine[self.m] = self.total(self.base.place.x)

    def cross(self):
        self.c[1].wait_recv()
        self.outgoing[2][...] = (self.total(self.order[2]) + self.incoming[0][...].astype(F32)).astype(BF16)
        self.c[3].start()

    def take(self):
        self.c[2].wait_recv()
        self.c[3].wait_recv()
        return self.base.mine[self.m] + self.incoming[1][...].astype(F32) + self.incoming[2][...].astype(F32)


def run_pipeline(steps, count=NM):
    for t in range(count + len(steps) - 1):
        for lag, step in enumerate(steps):
            if 0 <= t - lag < count:
                step(t - lag)


class Gather:
    SLOTS = 7

    def __init__(self, place, block, send, recv, index):
        p = place
        ahead, behind, across = p.shift(1), p.shift(3), p.shift(2)
        y, z, x = p.y, 1 - p.y, p.x

        def go(slot, owner, to):
            ref = block(owner)
            return remote(ref, ref, send.at[index, slot], recv.at[index, slot], "gene", to)

        own, paired = p.chip(y, x), p.chip(z, x)
        self.c = [
            go(0, own, p.other_y),
            go(1, own, p.right),
            go(2, own, p.left),
            go(3, paired, p.right),
            go(4, paired, p.left),
            go(5, p.chip(y, behind), p.right),
            go(6, p.chip(z, ahead), p.left),
        ]

    def start(self):
        for k in (1, 2, 0):
            self.c[k].start()

    def second(self):
        c = self.c
        c[1].wait_recv()
        c[5].start()
        c[0].wait_recv()
        c[3].start()
        c[4].start()

    def third(self):
        self.c[4].wait_recv()
        self.c[6].start()

    def finish(self):
        for k in (2, 3, 5, 6):
            self.c[k].wait_recv()

    def drain(self):
        for copy in self.c:
            copy.wait_send()


class GatherX:
    def __init__(self, place, block, send, recv, index, rightward):
        p = place
        ahead, behind, across = p.shift(1), p.shift(3), p.shift(2)
        y, x = p.y, p.x
        self.rightward = rightward

        def go(slot, owner, to):
            ref = block(owner)
            return remote(ref, ref, send.at[index, slot], recv.at[index, slot], "gene", to)

        self.c = [
            go(0, p.chip(y, x), p.right),
            go(1, p.chip(y, x), p.left),
            go(2, p.chip(y, behind), p.right) if rightward else go(2, p.chip(y, ahead), p.left),
            go(3, p.chip(y, x), p.other_y),
            go(4, p.chip(y, behind), p.other_y),
            go(5, p.chip(y, ahead), p.other_y),
            go(6, p.chip(y, across), p.other_y),
        ]

    def start(self):
        for k in (0, 1, 3):
            self.c[k].start()

    def second(self):
        c = self.c
        for k in (0, 1):
            c[k].wait_recv()
            if self.rightward == (k == 0):
                c[2].start()
            c[4 + k].start()

    def third(self):
        self.c[2].wait_recv()
        self.c[6].start()

    def finish(self):
        for k in (3, 4, 5, 6):
            self.c[k].wait_recv()

    def drain(self):
        for copy in self.c:
            copy.wait_send()


class WideGather:
    SLOTS = 15

    def __init__(self, place, block, send, recv, index):
        p = place
        core, x, y, z = p.core, p.x, p.y, 1 - p.y
        ahead, behind, across = p.shift(1), p.shift(3), p.shift(2)
        self.far = Gather(place, lambda q: block(2 * q + core), send, recv, index)
        held = [p.chip(y, x), p.chip(z, x), p.chip(y, behind), p.chip(y, ahead), p.chip(z, behind), p.chip(z, ahead),
                p.chip(y, across), p.chip(z, across)]
        self.near = []
        for k, q in enumerate(held):
            ref = block(2 * q + core)
            self.near.append(remote(ref, ref, send.at[index, 7 + k], recv.at[index, 7 + k], "gene", p.other_core))

    def start(self):
        self.far.start()
        self.near[0].start()

    def second(self):
        self.far.second()
        self.near[1].start()
        self.near[2].start()

    def third(self):
        self.far.third()
        self.near[5].start()

    def finish(self):
        self.far.finish()
        for k in (3, 4, 6, 7):
            self.near[k].start()
        for copy in self.near:
            copy.wait_recv()

    def drain(self):
        self.far.drain()
        for copy in self.near:
            copy.wait_send()


class DirectSum:
    def __init__(self, place, shares, slots, send, recv):
        p = place
        self.shares, self.slots = shares, slots
        self.chip = p.chip(p.y, p.x)
        self.c = []
        for k in range(1, NCHIP):
            to = lax.rem(self.chip + k, NCHIP)
            self.c.append(remote(shares.at[to], slots.at[k], send.at[k], recv.at[k], "gene", to * 2 + p.core))

    def start(self):
        for copy in self.c:
            copy.start()

    def take(self):
        total = self.shares[self.chip].astype(F32)
        for k in range(1, NCHIP):
            self.c[k - 1].wait_recv()
            total = total + self.slots[k].astype(F32)
        return total

    def drain(self):
        for copy in self.c:
            copy.wait_send()


class Direct:
    def __init__(self, place, block, send, recv, index):
        p = place
        chip = p.chip(p.y, p.x)
        own = block(p.g)
        self.out, self.pair = [], []
        for k in range(NCHIP):
            to, frm = lax.rem(chip + k, NCHIP) * 2 + p.core, lax.rem(chip + NCHIP - k, NCHIP) * 2 + p.core
            ref = block(frm)
            if k:
                self.out.append(remote(own, own, send.at[index, k], recv.at[index, k], "gene", to))
            self.pair.append(remote(ref, ref, send.at[index, 7 + k if k else 0], recv.at[index, 7 + k if k else 0], "gene", p.other_core))

    def start(self):
        for copy in self.out + self.pair[:1]:
            copy.start()

    def finish(self):
        for k in range(1, NCHIP):
            self.out[k - 1].wait_recv()
            self.pair[k].start()
        for copy in self.pair:
            copy.wait_recv()

    def drain(self):
        for copy in self.out + self.pair:
            copy.wait_send()


class Swap:
    def __init__(self, place, source, slots, send, recv, index):
        self.out, self.into = [], []
        for k in range(1, NG):
            to, frm = lax.rem(place.g + k, NG), lax.rem(place.g + NG - k, NG)
            self.out.append(remote(source(to), slots.at[place.g], send.at[index, k], recv.at[index, place.g], "gene", to))
            self.into.append(remote(source(frm), slots.at[frm], send.at[index, k], recv.at[index, frm], "gene", frm))

    def start(self):
        for copy in self.out:
            copy.start()

    def finish(self):
        for copy in self.into:
            copy.wait_recv()

    def drain(self):
        for copy in self.out:
            copy.wait_send()


def total_of(slots):
    total = slots[0]
    for k in range(1, NG):
        total = total + slots[k]
    return total


def group_sum(values):
    high = values.astype(BF16)
    low = (values - high.astype(F32)).astype(BF16)
    shape = (values.shape[1], values.shape[1])
    row = lax.broadcasted_iota(jnp.int32, shape, 0) // 64
    col = lax.broadcasted_iota(jnp.int32, shape, 1) // 64
    ones = (row == col).astype(F32).astype(BF16)
    return jnp.dot(high, ones, preferred_element_type=F32) + jnp.dot(low, ones, preferred_element_type=F32)


def heads_of(rows, weights, head):
    parts = [jnp.dot(rows, weights[k], preferred_element_type=F32) for k in range(3)]
    for k in range(2):
        mean = group_sum(parts[k] * parts[k]) / head
        parts[k] = (parts[k] * lax.rsqrt(jnp.maximum(mean, FLOOR))).astype(BF16)
    parts[2] = parts[2].astype(BF16)
    return parts


def turned(values, by):
    if by == 0:
        return values
    row = lax.rem(lax.broadcasted_iota(jnp.int32, values.shape, 0), ROWS)
    count = values.shape[0]
    return jnp.where(row < by, pltpu.roll(values, count - ROWS + by, 0), pltpu.roll(values, by, 0))


def within_mix(query, keys, values, head):
    q, k, v = (part.astype(F32) for part in (query, keys, values))
    count = q.shape[0]
    scores = group_sum(jnp.concatenate([q * turned(k, 4 * d) for d in range(NM)], axis=0))
    weights = [jnp.exp(scores[d * count:(d + 1) * count] * head ** (-0.5)) for d in range(NM)]
    total = weights[0] + weights[1] + weights[2] + weights[3]
    mixed = None
    for d in range(NM):
        term = (weights[d] / total).astype(BF16).astype(F32) * turned(v, 4 * d)
        mixed = term if mixed is None else mixed + term
    return mixed.astype(BF16)


def cross_mix(query, keys, values, same, head):
    lane = lax.broadcasted_iota(jnp.int32, query.shape, 1) // 64
    q = query.astype(F32)
    mixed = jnp.zeros(query.shape, F32)
    for h in range(query.shape[1] // 64):
        one = jnp.where(lane == h, q, 0.0).astype(BF16)
        scores = lax.dot_general(one, keys, DN_T, preferred_element_type=F32) * head ** (-0.5)
        weights = jnp.where(same, jnp.exp(scores), 0.0)
        probs = (weights / jnp.sum(weights, axis=-1, keepdims=True)).astype(BF16)
        mixed = jnp.where(lane == h, jnp.dot(probs, values, preferred_element_type=F32), mixed)
    return mixed.astype(BF16)


def encoder_scratch(width, genes, cells, head):
    half = cells // 2
    raw = [pltpu.VMEM((3, 2, head, width), BF16), pltpu.VMEM((2, head, width), BF16)]
    layer = [
        pltpu.VMEM((3, width, 256), BF16),
        pltpu.VMEM((256, width), BF16),
        pltpu.VMEM((NM, NCHIP, ROWS, width), BF16),
    ]
    return (
        [
            pltpu.VMEM((cells, genes), BF16),
            pltpu.VMEM((NM, genes, 1664), BF16),
            pltpu.VMEM((8, cells), F32),
            pltpu.VMEM((NG, 8, cells), F32),
            pltpu.VMEM((NM, NCHIP, 2, ROWS, width), BF16),
            pltpu.VMEM((NM, NCHIP, ROWS, width), BF16),
            pltpu.VMEM((128, width), F32),
            pltpu.VMEM((NM, ROWS, width), F32),
            pltpu.VMEM((NM, ROWS, width), F32),
            pltpu.VMEM((NM, 2, 2, half, 256), BF16),
            pltpu.VMEM((NM, half, 256), BF16),
            pltpu.VMEM((cells, 128), F32),
            pltpu.SemaphoreType.DMA((NM + 4,)),
        ]
        + raw * 2
        + layer * 2
        + [pltpu.SemaphoreType.DMA((1, NG))] * 2
        + [pltpu.SemaphoreType.DMA((NM,))] * 2
        + [pltpu.SemaphoreType.DMA((NM,))] * 2
        + [pltpu.SemaphoreType.DMA((NM, NM))] * 2
        + [pltpu.SemaphoreType.DMA((2 * NM, Gather.SLOTS))] * 2
        + [pltpu.SemaphoreType.DMA((1, 16))] * 2
        + Scatter.scratch(width) * 2
        + [
            pltpu.VMEM((half, width), F32),
            pltpu.VMEM((NCHIP, ROWS, width), BF16),
            pltpu.VMEM((NCHIP, ROWS, width), BF16),
            pltpu.SemaphoreType.DMA((NCHIP,)),
            pltpu.SemaphoreType.DMA((NCHIP,)),
        ]
    )


def encoder_kernel(head, counts, groups, w_hbm, q1_hbm, q2_hbm, o1_hbm, o2_hbm, hidden, library, *refs):
    (scaled, w_proj, tile, slots, halves, pair, padded, tokens, resid, kv, queries, spot, load_sem) = refs[:13]
    raws, layers = refs[13:17], refs[17:23]
    (s_send, s_recv, w_send, w_recv, p_send, p_recv, k_send, k_recv, a_send, a_recv, d_send, d_recv) = refs[23:35]
    sums, (gathered, shares, share_in, z_send, z_recv) = refs[35:-5], refs[-5:]
    place = Place()
    width = resid.shape[-1]
    wide = w_proj.shape[-1]
    core, here = place.core, place.chip(place.y, place.x)
    scatter = [Scatter(place, sums[10 * k:10 * k + 10]) for k in range(2)]
    weights, outs, blocks = layers[0::3], layers[1::3], layers[2::3]

    greet(everyone(place))
    tile[...] = jnp.broadcast_to(jnp.sum(counts[...].astype(F32), axis=0, keepdims=True), tile.shape)
    swap = Swap(place, lambda t: tile, slots, s_send, s_recv, 0)
    swap.start()
    small = [
        pltpu.make_async_copy(src, dst, load_sem.at[NM + k])
        for k, (src, dst) in enumerate(zip((q1_hbm, o1_hbm, q2_hbm, o2_hbm), raws))
    ]
    loads = [
        pltpu.make_async_copy(w_hbm.at[:, pl.ds((m * width) // 128 * 128, wide)], w_proj.at[m], load_sem.at[m])
        for m in range(NM)
    ]
    for load in small[:2] + loads + small[2:]:
        load.start()
    slots[place.g] = tile[...]

    lanes = pl.ds(pl.multiple_of(core * 128, 128), 128)
    share = []
    for k in range(2):
        share.append([
            remote(weights[k].at[:, :, lanes], weights[k].at[:, :, lanes], w_send.at[2 * k], w_recv.at[2 * k], "gene", place.other_core),
            remote(outs[k].at[lanes, :], outs[k].at[lanes, :], w_send.at[2 * k + 1], w_recv.at[2 * k + 1], "gene", place.other_core),
        ])

    def prepare(k):
        padded[...] = jnp.zeros_like(padded)
        small[2 * k].wait()
        for a in range(3):
            for h in range(2):
                padded[64 * h:64 * h + head, :] = raws[2 * k][a, h].astype(F32)
            weights[k][a, :, lanes] = padded[...].T.astype(BF16)
        share[k][0].start()
        small[2 * k + 1].wait()
        for h in range(2):
            padded[64 * h:64 * h + head, :] = raws[2 * k + 1][h].astype(F32)
        outs[k][lanes, :] = padded[...].astype(BF16)
        share[k][1].start()

    prepare(0)
    swap.finish()
    total = 1.0 + total_of(slots)
    library[...] = total
    scaled[...] = jnp.log1p(counts[...].astype(F32) * (TARGET / total[0:1])).T.astype(BF16)

    pairs = [
        remote(halves.at[m, :, 1 - core], pair.at[m], p_send.at[m], p_recv.at[m], "gene", place.other_core)
        for m in range(NM)
    ]

    def project(m):
        loads[m].wait()
        skip = (m * width) % 128
        out = jnp.dot(scaled[...], w_proj[m], preferred_element_type=F32)[:, skip:skip + width]
        halves[m] = out.astype(BF16).reshape(NCHIP, 2, ROWS, width)
        pairs[m].start()

    def join(m):
        pairs[m].wait_recv()
        for q in range(NCHIP):
            scatter[0].chip[m, q] = (halves[m, q, core].astype(F32) + pair[m, q].astype(F32)).astype(BF16)
        scatter[0].spread(m)

    def keep(m):
        scatter[0].mine[m] = scatter[0].take(m)

    run_pipeline([project, join, scatter[0].forward, scatter[0].cross, keep])

    gathers = [
        [
            GatherX(place, lambda q, k=k, m=m: blocks[k].at[m, q], a_send, a_recv, k * NM + m, m == 1)
            if m % 2
            else Gather(place, lambda q, k=k, m=m: blocks[k].at[m, q], a_send, a_recv, k * NM + m)
            for m in range(NM)
        ]
        for k in range(2)
    ]
    for s in range(NM):
        for m in range(NM):
            tokens[s, 4 * m:4 * m + 4, :] = scatter[0].mine[m, 4 * s:4 * s + 4, :]
        blocks[0][s, here] = rms(tokens[s]).astype(BF16)
        gathers[0][s].start()

    prepare(1)
    cells = 2 * kv.shape[3]
    at = lax.broadcasted_iota(jnp.int32, (cells, cells), 1)
    source = 32 * (lax.rem(at, 128) // ROWS) + ROWS * (at // 128) + lax.rem(at, ROWS)
    order = (lax.broadcasted_iota(jnp.int32, (cells, cells), 0) == source).astype(F32).astype(BF16)
    row = jnp.dot(
        jnp.broadcast_to(groups[...].astype(F32), (128, cells)).astype(BF16), order, preferred_element_type=F32
    )
    spot[...] = row.T
    same = jnp.broadcast_to(spot[lanes, 0:1], (128, cells)) == row
    for copy in share[0]:
        copy.wait_recv()

    def within(s):
        gathers[0][s].finish()
        rows = blocks[0][s].reshape(NCHIP * ROWS, width)
        mixed = within_mix(*heads_of(rows, weights[0], head), head)
        out = jnp.dot(mixed, outs[0][...], preferred_element_type=F32)
        scatter[1].chip[s] = out.astype(BF16).reshape(NCHIP, ROWS, width)
        scatter[1].spread(s)

    def add_within(s):
        tokens[s] = tokens[s] + scatter[1].take(s)

    run_pipeline([
        lambda s: gathers[0][s].second(), lambda s: gathers[0][s].third(), within,
        scatter[1].forward, scatter[1].cross, add_within,
    ])

    for m in range(NM):
        for s in range(NM):
            resid[m, 4 * s:4 * s + 4, :] = tokens[s, 4 * m:4 * m + 4, :]
        blocks[1][m, here] = rms(resid[m]).astype(BF16)
        gathers[1][m].start()
    for copy in share[1]:
        copy.wait_recv()
    trade = [
        remote(kv.at[m, core], kv.at[m, core], k_send.at[m, 0], k_recv.at[m, 0], "gene", place.other_core)
        for m in range(NM)
    ]

    def look(m):
        gathers[1][m].finish()
        rows = blocks[1][m].reshape(NCHIP * ROWS, width)
        queries[m], kv[m, core, 0], kv[m, core, 1] = heads_of(rows, weights[1], head)
        trade[m].start()

    def attend(m):
        trade[m].wait_recv()
        keys = jnp.concatenate([kv[m, 0, 0], kv[m, 1, 0]], axis=0)
        values = jnp.concatenate([kv[m, 0, 1], kv[m, 1, 1]], axis=0)
        mixed = cross_mix(queries[m], keys, values, same, head)
        out = jnp.dot(mixed, outs[1][...], preferred_element_type=F32)
        gathered[...] = gathered[...] + out if m else out

    run_pipeline([lambda m: gathers[1][m].second(), lambda m: gathers[1][m].third(), look, attend])

    shares[...] = gathered[...].astype(BF16).reshape(NCHIP, ROWS, width)
    final = DirectSum(place, shares, share_in, z_send, z_recv)
    final.start()
    pooled = (resid[0] + resid[1] + resid[2] + resid[3] + final.take()) * (1.0 / NM)
    hidden[pl.ds(pl.multiple_of(place.g * ROWS, ROWS), ROWS), :] = rms(pooled).astype(BF16)
    last = Direct(
        place, lambda o: hidden.at[pl.ds(pl.multiple_of(o * ROWS, ROWS), ROWS), :], d_send, d_recv, 0
    )
    last.start()
    last.finish()
    for one in scatter + gathers[0] + gathers[1] + [swap, final, last]:
        one.drain()
    for copy in share[0] + share[1] + pairs + trade:
        copy.wait_send()


class GroupGather:
    SLOTS = 7

    def __init__(self, r, block, send, recv, index):
        z, h = lax.rem(r, NZ), r // NZ
        up, down = lax.rem(z + 1, NZ), lax.rem(z + 3, NZ)
        k = 1 - h

        def at(a, b):
            return a * NZ + b

        def go(slot, owner, to):
            ref = block(owner)
            return remote(ref, ref, send.at[index, slot], recv.at[index, slot], "grp", to)

        self.c = [
            go(0, at(h, z), at(k, z)),
            go(1, at(h, z), at(h, up)),
            go(2, at(h, z), at(h, down)),
            go(3, at(k, z), at(h, up)),
            go(4, at(k, z), at(h, down)),
            go(5, at(h, down), at(h, up)),
            go(6, at(k, up), at(h, down)),
        ]

    def start(self):
        for k in (1, 2, 0):
            self.c[k].start()

    def second(self):
        c = self.c
        c[1].wait_recv()
        c[5].start()
        c[0].wait_recv()
        c[3].start()
        c[4].start()

    def third(self):
        self.c[4].wait_recv()
        self.c[6].start()

    def finish(self):
        for k in (2, 3, 5, 6):
            self.c[k].wait_recv()

    def drain(self):
        for copy in self.c:
            copy.wait_send()


class GroupGatherZ:
    def __init__(self, r, block, send, recv, index, upward):
        z, h = lax.rem(r, NZ), r // NZ
        up, down, across = lax.rem(z + 1, NZ), lax.rem(z + 3, NZ), lax.rem(z + 2, NZ)
        k = 1 - h
        self.upward = upward

        def at(a, b):
            return a * NZ + b

        def go(slot, owner, to):
            ref = block(owner)
            return remote(ref, ref, send.at[index, slot], recv.at[index, slot], "grp", to)

        self.c = [
            go(0, at(h, z), at(h, up)),
            go(1, at(h, z), at(h, down)),
            go(2, at(h, down), at(h, up)) if upward else go(2, at(h, up), at(h, down)),
            go(3, at(h, z), at(k, z)),
            go(4, at(h, down), at(k, z)),
            go(5, at(h, up), at(k, z)),
            go(6, at(h, across), at(k, z)),
        ]

    def start(self):
        for k in (0, 1, 3):
            self.c[k].start()

    def second(self):
        c = self.c
        for k in (0, 1):
            c[k].wait_recv()
            if self.upward == (k == 0):
                c[2].start()
            c[4 + k].start()

    def third(self):
        self.c[2].wait_recv()
        self.c[6].start()

    def finish(self):
        for k in (3, 4, 5, 6):
            self.c[k].wait_recv()

    def drain(self):
        for copy in self.c:
            copy.wait_send()


class GroupDirect:
    def __init__(self, r, block, send, recv):
        self.out, self.into = [], []
        for k in range(1, NR):
            to, frm = lax.rem(r + k, NR), lax.rem(r + NR - k, NR)
            self.out.append(remote(block(r), block(r), send.at[k], recv.at[k], "grp", to))
            self.into.append(remote(block(r), block(frm), send.at[k], recv.at[k], "grp", frm))

    def start(self):
        for copy in self.out:
            copy.start()

    def finish(self):
        for copy in self.into:
            copy.wait_recv()

    def drain(self):
        for copy in self.out:
            copy.wait_send()


def log_factorials(count):
    return [math.log(math.factorial(k)) for k in range(count)]


def terms(x, theta, logit, rate_scale, norm_scale, most):
    tail = jnp.exp(-jnp.abs(logit))
    soft = jnp.maximum(logit, 0.0) + jnp.log1p(tail)
    sigmoid = jnp.where(logit >= 0, 1.0, tail) / (1.0 + tail)
    rate = rate_scale * soft
    product = jnp.ones_like(theta)
    slope = jnp.zeros_like(theta)
    log_factorial = jnp.zeros_like(theta)
    table = log_factorials(most + 1)
    for k in range(most):
        on = x > k
        term = theta + float(k)
        slope = jnp.where(on, slope * term + product, slope)
        product = jnp.where(on, product * term, product)
        if k:
            log_factorial = jnp.where(on, table[k + 1], log_factorial)
    total = theta + rate
    log_total = jnp.log(total)
    log_theta = jnp.log(theta)
    ratio = (theta + x) / total
    nll = -(
        jnp.log(product) - log_factorial
        + theta * (log_theta - log_total)
        + x * (jnp.log(rate) - log_total)
    )
    d_logit = (ratio - x / rate) * rate_scale * sigmoid * norm_scale
    d_theta = -(slope / product + log_theta + 1.0 - log_total - ratio)
    return nll, d_logit, d_theta


def decode_kernel(
    genes_all, cells_all, panel_count,
    counts, panel_row, library, hidden, w_mean, w_disp,
    cell_loss, gradient, disp_block,
    tile, slots, back, piece, columns, field, panel_part, loss, panel_col,
    s_send, s_recv, h_send, h_recv, v_send, v_recv, f_send, f_recv, d_send, d_recv, o_send, o_recv,
):
    place = Place()
    r = lax.axis_index("grp")
    genes, cells = counts.shape
    width = hidden.shape[1]
    share = width // NR
    parts = 4
    step = genes // parts
    norm_scale = cells_all ** (-0.5)
    greet(everyone(place) + [("grp", lax.rem(r + k, NR)) for k in range(1, NR)])

    panel_col[...] = jnp.broadcast_to(panel_row[...].astype(F32), (128, genes)).T
    disp = lax.dot_general(w_disp[...], hidden[...], DN_T, preferred_element_type=F32)
    table = DISP_BASE + (jnp.maximum(disp, 0.0) + jnp.log1p(jnp.exp(-jnp.abs(disp))))
    high = table.astype(BF16)
    rest = table - high.astype(F32)
    middle = rest.astype(BF16)
    low = (rest - middle.astype(F32)).astype(BF16)
    tables = jnp.concatenate([high, middle, low], axis=0)
    rate_scale = library[0:1] / genes_all
    panel_part[...] = jnp.zeros_like(panel_part)
    loss[...] = jnp.zeros_like(loss)

    v_gather = WideGather(
        place, lambda o: columns.at[:, pl.ds(pl.multiple_of(o * ROWS, ROWS), ROWS), :], v_send, v_recv, 0
    )
    field_gather = []
    for p in range(parts):
        block = lambda o, p=p: field.at[o, pl.ds(p * step, step), :]
        field_gather.append(
            GroupGatherZ(r, block, f_send, f_recv, p, True) if p == 1 else GroupGather(r, block, f_send, f_recv, p)
        )
    disp_gather = GroupDirect(r, lambda o: field.at[o, pl.ds(genes, panel_count), :], d_send, d_recv)
    spread = GroupDirect(r, lambda o: disp_block.at[o], o_send, o_recv)

    def decode(p):
        at = pl.ds(p * step, step)
        x = counts[at, :].astype(F32)
        logit = lax.dot_general(w_mean[at, :], hidden[...], DN_T, preferred_element_type=F32)
        lane = lax.broadcasted_iota(jnp.int32, (step, 3 * panel_count), 1)
        pick = (panel_col[at, 0:1] == lax.rem(lane, panel_count).astype(F32)).astype(F32).astype(BF16)
        theta = jnp.dot(pick, tables, preferred_element_type=F32)
        nll, d_logit, d_theta = terms(x, theta, logit, rate_scale, norm_scale, 12)
        field[r, at, :] = d_logit.astype(BF16)
        field_gather[p].start()
        loss[...] += jnp.sum(nll, axis=0, keepdims=True)
        row = lax.broadcasted_iota(jnp.int32, (step, 128), 1)
        wanted = jnp.where(lax.rem(row, 8) < 4, (row // 8) * 4 + lax.rem(row, 8), -1)
        pick_t = (panel_col[at, :] == wanted.astype(F32)).astype(F32).astype(BF16)
        upper = d_theta.astype(BF16)
        lower = (d_theta - upper.astype(F32)).astype(BF16)
        panel_part[...] += lax.dot_general(pick_t, upper, DN_0, preferred_element_type=F32) + lax.dot_general(
            pick_t, lower, DN_0, preferred_element_type=F32
        )

    decode(0)
    own = hidden[pl.ds(pl.multiple_of(place.g * ROWS, ROWS), ROWS), :].astype(F32)
    piece[...] = jnp.zeros_like(piece)
    for k in range(NR):
        piece[k, :, 0:share] = own[:, k * share:(k + 1) * share].astype(BF16)
    rows = pl.ds(pl.multiple_of(place.g * ROWS, ROWS), ROWS)
    out, into = [], []
    for k in range(1, NR):
        to, frm = lax.rem(r + k, NR), lax.rem(r + NR - k, NR)
        out.append(remote(piece.at[to], columns.at[r, rows], h_send.at[k], h_recv.at[r], "grp", to))
        into.append(remote(piece.at[frm], columns.at[frm, rows], h_send.at[k], h_recv.at[frm], "grp", frm))
    for copy in out:
        copy.start()
    columns[r, rows] = piece[r]

    decode(1)
    for copy in into:
        copy.wait_recv()
    v_gather.start()
    field_gather[0].second()
    decode(2)
    v_gather.second()
    field_gather[1].second()
    field_gather[0].third()
    decode(3)

    row = lax.broadcasted_iota(jnp.int32, (128, cells), 0)
    both = jnp.where(lax.rem(row, 8) == 4, loss[...], panel_part[...])
    tile[...] = both.reshape(NG, 8, cells)
    first = Swap(place, lambda t: tile.at[t], slots, s_send, s_recv, 0)
    first.start()
    slots[place.g] = tile[place.g]
    v_gather.third()
    field_gather[2].second()
    field_gather[1].third()
    first.finish()
    summed = total_of(slots)
    cell_loss[...] = summed[4:5] / genes_all
    back[place.g] = summed
    second = Swap(place, lambda t: back.at[place.g], back, s_send, s_recv, 1)
    second.start()
    field_gather[2].third()
    field_gather[3].second()
    second.finish()
    d_panel = jnp.concatenate([back[k, 0:4] for k in range(NG)], axis=0)
    tail = jnp.exp(-jnp.abs(disp))
    d_disp = d_panel * (jnp.where(disp >= 0, 1.0, tail) / (1.0 + tail)) * norm_scale
    field[r, pl.ds(genes, panel_count), :] = d_disp.astype(BF16)
    disp_gather.start()
    field_gather[3].third()

    def contract(at, size):
        total = jnp.zeros((size, columns.shape[2]), F32)
        for k in range(NR):
            total = total + jnp.dot(field[k, pl.ds(at, size), :], columns[k], preferred_element_type=F32)
        return total

    def gradient_of(p):
        field_gather[p].finish()
        gradient[pl.ds(p * step, step), :] = contract(p * step, step)

    v_gather.finish()
    gradient_of(0)
    gradient_of(1)
    disp_gather.finish()
    disp_block[r] = contract(genes, panel_count)
    spread.start()
    gradient_of(2)
    gradient_of(3)
    spread.finish()
    for copy in out:
        copy.wait_send()
    for one in [v_gather, first, second, disp_gather, spread] + field_gather:
        one.drain()


def finish_kernel(gradient, disp_block, loss, cell_loss, grad_mean, grad_disp):
    share = grad_mean.shape[0]
    cell_loss[...] = loss[...]
    grad_mean[...] = gradient[...].T[0:share]
    for k in range(NR):
        grad_disp[:, k * share:(k + 1) * share] = disp_block[k, :, 0:share]


def whole():
    return pl.BlockSpec(memory_space=pltpu.VMEM)


def params(number):
    return pltpu.CompilerParams(collective_id=number, has_side_effects=True, vmem_limit_bytes=LIMIT)


def head_weights(w_qkv):
    width, heads, three = w_qkv.shape
    turned_w = jnp.transpose(w_qkv, (2, 1, 0)).reshape(3, three // 3, heads, width)
    return jnp.transpose(turned_w, (0, 2, 1, 3))


def shards(counts, panels, membership, w_proj, w_qkv_within, w_out_within, w_qkv_cross, w_out_cross, w_mean, w_disp):
    cells, genes = counts.shape
    width = w_qkv_within.shape[0]
    head = w_out_within.shape[1]
    genes_all = genes * NG
    cells_all = cells * NR
    panel_count = w_disp.shape[1]
    counts_t = counts.T
    swap_sems = [pltpu.SemaphoreType.DMA((2, NG))] * 2
    hidden, library = pl.pallas_call(
        functools.partial(encoder_kernel, head),
        name="encoder",
        out_shape=(jax.ShapeDtypeStruct((cells, width), BF16), jax.ShapeDtypeStruct((8, cells), F32)),
        in_specs=[whole()] * 2 + [pl.BlockSpec(memory_space=pl.ANY)] * 5,
        out_specs=(whole(), whole()),
        scratch_shapes=encoder_scratch(width, genes, cells, head),
        compiler_params=params(0),
    )(counts_t, membership, w_proj, head_weights(w_qkv_within), head_weights(w_qkv_cross), w_out_within, w_out_cross)
    cell_loss, gradient, disp_block = pl.pallas_call(
        functools.partial(decode_kernel, genes_all, cells_all, panel_count),
        name="decode",
        out_shape=(
            jax.ShapeDtypeStruct((1, cells), F32),
            jax.ShapeDtypeStruct((genes, 256), F32),
            jax.ShapeDtypeStruct((NR, panel_count, 256), F32),
        ),
        in_specs=[whole()] * 6,
        out_specs=(whole(), whole(), whole()),
        scratch_shapes=[
            pltpu.VMEM((NG, 8, cells), F32),
            pltpu.VMEM((NG, 8, cells), F32),
            pltpu.VMEM((NG, 8, cells), F32),
            pltpu.VMEM((NR, ROWS, 256), BF16),
            pltpu.VMEM((NR, cells, 256), BF16),
            pltpu.VMEM((NR, genes + panel_count, cells), BF16),
            pltpu.VMEM((128, cells), F32),
            pltpu.VMEM((1, cells), F32),
            pltpu.VMEM((genes, 128), F32),
        ] + swap_sems + [
            pltpu.SemaphoreType.DMA((NR,)),
            pltpu.SemaphoreType.DMA((NR,)),
            pltpu.SemaphoreType.DMA((1, WideGather.SLOTS)),
            pltpu.SemaphoreType.DMA((1, WideGather.SLOTS)),
            pltpu.SemaphoreType.DMA((4, GroupGather.SLOTS)),
            pltpu.SemaphoreType.DMA((4, GroupGather.SLOTS)),
            pltpu.SemaphoreType.DMA((NR,)),
            pltpu.SemaphoreType.DMA((NR,)),
            pltpu.SemaphoreType.DMA((NR,)),
            pltpu.SemaphoreType.DMA((NR,)),
        ],
        compiler_params=params(3),
    )(counts_t, panels[None, :], library, hidden, w_mean.T, w_disp.T)
    cell_loss, grad_mean, grad_disp = pl.pallas_call(
        finish_kernel,
        name="finish",
        out_shape=(
            jax.ShapeDtypeStruct((1, cells), F32),
            jax.ShapeDtypeStruct((width // NR, genes), F32),
            jax.ShapeDtypeStruct((panel_count, width), F32),
        ),
        in_specs=[whole()] * 3,
        out_specs=(whole(), whole(), whole()),
    )(gradient, disp_block, cell_loss)
    return cell_loss[0], grad_mean, grad_disp.T


def solution(mesh):
    return jax.shard_map(
        shards,
        mesh=mesh,
        in_specs=(
            P("grp", "gene"),
            P("gene"),
            P("grp", None),
            P("gene", None),
            P(None, "gene", None),
            P("gene", None, None),
            P(None, "gene", None),
            P("gene", None, None),
            P(None, "gene"),
            P(),
        ),
        out_specs=(P("grp"), P("grp", "gene"), P()),
        check_vma=False,
    )
```

```python
import functools
import math

import jax
import jax.numpy as jnp
from jax import lax
from jax.experimental import pallas as pl
from jax.experimental.pallas import tpu as pltpu
from jax.sharding import PartitionSpec as P

EPS = 1e-06
FLOOR = 0.3
TARGET = 10000.0
DISP_BASE = 0.5
MESH = pl.DeviceIdType.MESH
F32 = jnp.float32
BF16 = jnp.bfloat16

NX = 4
NY = 2
NG = 16
NCHIP = 8
NR = 8
NZ = 4
NM = 4
ROWS = 16
LIMIT = 64 * 1024 * 1024 - 256 * 1024
DN_T = (((1,), (1,)), ((), ()))
DN_0 = (((0,), (0,)), ((), ()))


def remote(src, dst, send, recv, axis, to):
    return pltpu.make_async_remote_copy(
        src_ref=src, dst_ref=dst, send_sem=send, recv_sem=recv, device_id={axis: to}, device_id_type=MESH
    )


class Place:
    def __init__(self):
        self.g = lax.axis_index("gene")
        self.core = lax.rem(self.g, 2)
        self.x = lax.rem(self.g // 2, NX)
        self.y = self.g // (2 * NX)
        self.right = self.at(self.y, self.shift(1), self.core)
        self.left = self.at(self.y, self.shift(3), self.core)
        self.other_y = self.at(1 - self.y, self.x, self.core)
        self.other_core = self.at(self.y, self.x, 1 - self.core)

    def shift(self, by):
        return lax.rem(self.x + by, NX)

    def at(self, y, x, core):
        return (y * NX + x) * 2 + core

    def chip(self, y, x):
        return y * NX + x


def greet(axis_peers):
    barrier = pltpu.get_barrier_semaphore()
    for axis, to in axis_peers:
        pl.semaphore_signal(barrier, inc=1, device_id={axis: to}, device_id_type=MESH)
    pl.semaphore_wait(barrier, len(axis_peers))


def everyone(place):
    return [("gene", lax.rem(place.g + k, NG)) for k in range(1, NG)]


def rms(values):
    return values * lax.rsqrt(jnp.mean(values * values, axis=-1, keepdims=True) + EPS)


class Scatter:
    @staticmethod
    def scratch(width):
        return [
            pltpu.VMEM((NM, NCHIP, ROWS, width), BF16),
            pltpu.VMEM((NM, 3, ROWS, width), BF16),
            pltpu.VMEM((NM, 3, ROWS, width), BF16),
            pltpu.VMEM((NM, 2, ROWS, width), BF16),
            pltpu.VMEM((NM, ROWS, width), BF16),
            pltpu.VMEM((NM, ROWS, width), BF16),
            pltpu.VMEM((NM, ROWS, width), F32),
            pltpu.VMEM((2, NX, ROWS, width), BF16),
            pltpu.SemaphoreType.DMA((NM, 7)),
            pltpu.SemaphoreType.DMA((NM, 7)),
        ]

    def __init__(self, place, refs):
        (self.chip, self.from_left, self.from_right, self.relay, self.y_out, self.y_in, self.mine, four, send, recv) = refs
        self.send, self.recv = send, recv
        p = self.place = place
        ahead, behind, across = p.shift(1), p.shift(3), p.shift(2)
        self.copies, self.turned = [], {}
        for m in range(NM):
            if m % 2 == 0:
                self.turned[m] = ScatterY(self, m, four.at[m // 2], 1 if m == 0 else -1)
                self.copies.append(self.turned[m].c)
                continue

            def go(slot, src, dst, to):
                return remote(src, dst, send.at[m, slot], recv.at[m, slot], "gene", to)
            self.copies.append([
                go(0, self.chip.at[m, p.chip(0, across)], self.from_left.at[m, 0], p.right),
                go(1, self.chip.at[m, p.chip(1, across)], self.from_right.at[m, 0], p.left),
                go(2, self.chip.at[m, p.chip(1, ahead)], self.from_left.at[m, 2], p.right),
                go(3, self.chip.at[m, p.chip(0, behind)], self.from_right.at[m, 2], p.left),
                go(4, self.relay.at[m, 0], self.from_left.at[m, 1], p.right),
                go(5, self.relay.at[m, 1], self.from_right.at[m, 1], p.left),
                go(6, self.y_out.at[m], self.y_in.at[m], p.other_y),
            ])

    def spread(self, m):
        if m in self.turned:
            return self.turned[m].spread()
        for k in (0, 1, 2, 3):
            self.copies[m][k].start()

    def forward(self, m):
        if m in self.turned:
            return self.turned[m].forward()
        p = self.place
        self.copies[m][0].wait_recv()
        self.relay[m, 0] = (
            self.chip[m, p.chip(0, p.shift(1))].astype(F32) + self.from_left[m, 0].astype(F32)
        ).astype(BF16)
        self.copies[m][4].start()
        self.copies[m][1].wait_recv()
        self.relay[m, 1] = (
            self.chip[m, p.chip(1, p.shift(3))].astype(F32) + self.from_right[m, 0].astype(F32)
        ).astype(BF16)
        self.copies[m][5].start()

    def cross(self, m):
        if m in self.turned:
            return self.turned[m].cross()
        p = self.place
        for k in (2, 3, 4, 5):
            self.copies[m][k].wait_recv()
        self.y_out[m] = (
            self.chip[m, p.chip(1 - p.y, p.x)].astype(F32)
            + self.from_left[m, 2 - p.y].astype(F32)
            + self.from_right[m, 1 + p.y].astype(F32)
        ).astype(BF16)
        self.copies[m][6].start()
        self.mine[m] = (
            self.chip[m, p.chip(p.y, p.x)].astype(F32)
            + self.from_left[m, 1 + p.y].astype(F32)
            + self.from_right[m, 2 - p.y].astype(F32)
        )

    def take(self, m):
        if m in self.turned:
            return self.turned[m].take()
        self.copies[m][6].wait_recv()
        return self.mine[m] + self.y_in[m].astype(F32)

    def drain(self):
        for row in self.copies:
            for copy in row:
                copy.wait_send()


class ScatterY:
    def __init__(self, base, m, y_four, way):
        p = base.place
        self.base, self.m, self.four = base, m, y_four
        to, back = (p.right, p.left) if way > 0 else (p.left, p.right)
        ahead, behind = (p.shift(1), p.shift(3)) if way > 0 else (p.shift(3), p.shift(1))
        self.order = (p.shift(2), behind, ahead)
        self.outgoing = (base.relay.at[m, 0], base.relay.at[m, 1], base.y_out.at[m])
        self.incoming = (base.from_left.at[m, 0], base.from_right.at[m, 0], base.from_left.at[m, 1])

        def go(slot, src, dst, device):
            return remote(src, dst, base.send.at[m, slot], base.recv.at[m, slot], "gene", device)

        self.c = [
            go(k, base.chip.at[m, p.chip(1 - p.y, x)], y_four.at[x], p.other_y)
            for k, x in enumerate(self.order + (p.x,))
        ] + [go(4 + k, self.outgoing[k], self.incoming[k], (to, back, to)[k]) for k in range(3)]

    def spread(self):
        for k in range(4):
            self.c[k].start()

    def total(self, k):
        p = self.base.place
        x = p.x if k == 3 else self.order[k]
        self.c[k].wait_recv()
        return self.base.chip[self.m, p.chip(p.y, x)].astype(F32) + self.four[x].astype(F32)

    def forward(self):
        for k in (0, 1):
            self.outgoing[k][...] = self.total(k).astype(BF16)
            self.c[4 + k].start()

    def cross(self):
        value = self.total(2)
        self.c[4].wait_recv()
        self.outgoing[2][...] = (value + self.incoming[0][...].astype(F32)).astype(BF16)
        self.c[6].start()
        self.base.mine[self.m] = self.total(3)

    def take(self):
        self.c[5].wait_recv()
        self.c[6].wait_recv()
        return self.base.mine[self.m] + self.incoming[1][...].astype(F32) + self.incoming[2][...].astype(F32)


def run_pipeline(steps, count=NM):
    for t in range(count + len(steps) - 1):
        for lag, step in enumerate(steps):
            if 0 <= t - lag < count:
                step(t - lag)


class Gather:
    SLOTS = 7

    def __init__(self, place, block, send, recv, index):
        p = place
        ahead, behind, across = p.shift(1), p.shift(3), p.shift(2)
        y, z, x = p.y, 1 - p.y, p.x

        def go(slot, owner, to):
            ref = block(owner)
            return remote(ref, ref, send.at[index, slot], recv.at[index, slot], "gene", to)

        own, paired = p.chip(y, x), p.chip(z, x)
        self.c = [
            go(0, own, p.other_y),
            go(1, own, p.right),
            go(2, own, p.left),
            go(3, paired, p.right),
            go(4, paired, p.left),
            go(5, p.chip(y, behind), p.right),
            go(6, p.chip(z, ahead), p.left),
        ]

    def start(self):
        for k in (1, 2, 0):
            self.c[k].start()

    def second(self):
        c = self.c
        c[1].wait_recv()
        c[5].start()
        c[0].wait_recv()
        c[3].start()
        c[4].start()

    def third(self):
        self.c[4].wait_recv()
        self.c[6].start()

    def finish(self):
        for k in (2, 3, 5, 6):
            self.c[k].wait_recv()

    def drain(self):
        for copy in self.c:
            copy.wait_send()


class GatherX:
    def __init__(self, place, block, send, recv, index, rightward):
        p = place
        ahead, behind, across = p.shift(1), p.shift(3), p.shift(2)
        y, x = p.y, p.x
        self.rightward = rightward

        def go(slot, owner, to):
            ref = block(owner)
            return remote(ref, ref, send.at[index, slot], recv.at[index, slot], "gene", to)

        self.c = [
            go(0, p.chip(y, x), p.right),
            go(1, p.chip(y, x), p.left),
            go(2, p.chip(y, behind), p.right) if rightward else go(2, p.chip(y, ahead), p.left),
            go(3, p.chip(y, x), p.other_y),
            go(4, p.chip(y, behind), p.other_y),
            go(5, p.chip(y, ahead), p.other_y),
            go(6, p.chip(y, across), p.other_y),
        ]

    def start(self):
        for k in (0, 1, 3):
            self.c[k].start()

    def second(self):
        c = self.c
        for k in (0, 1):
            c[k].wait_recv()
            if self.rightward == (k == 0):
                c[2].start()
            c[4 + k].start()

    def third(self):
        self.c[2].wait_recv()
        self.c[6].start()

    def finish(self):
        for k in (3, 4, 5, 6):
            self.c[k].wait_recv()

    def drain(self):
        for copy in self.c:
            copy.wait_send()


class WideGather:
    SLOTS = 15

    def __init__(self, place, block, send, recv, index):
        p = place
        core, x, y, z = p.core, p.x, p.y, 1 - p.y
        ahead, behind, across = p.shift(1), p.shift(3), p.shift(2)
        self.far = Gather(place, lambda q: block(2 * q + core), send, recv, index)
        held = [p.chip(y, x), p.chip(z, x), p.chip(y, behind), p.chip(y, ahead), p.chip(z, behind), p.chip(z, ahead),
                p.chip(y, across), p.chip(z, across)]
        self.near = []
        for k, q in enumerate(held):
            ref = block(2 * q + core)
            self.near.append(remote(ref, ref, send.at[index, 7 + k], recv.at[index, 7 + k], "gene", p.other_core))

    def start(self):
        self.far.start()
        self.near[0].start()

    def second(self):
        self.far.second()
        self.near[1].start()
        self.near[2].start()

    def third(self):
        self.far.third()
        self.near[5].start()

    def finish(self):
        self.far.finish()
        for k in (3, 4, 6, 7):
            self.near[k].start()
        for copy in self.near:
            copy.wait_recv()

    def drain(self):
        self.far.drain()
        for copy in self.near:
            copy.wait_send()


class DirectSum:
    def __init__(self, place, shares, slots, send, recv):
        p = place
        self.shares, self.slots = shares, slots
        self.chip = p.chip(p.y, p.x)
        self.c = []
        for k in range(1, NCHIP):
            to = lax.rem(self.chip + k, NCHIP)
            self.c.append(remote(shares.at[to], slots.at[k], send.at[k], recv.at[k], "gene", to * 2 + p.core))

    def start(self):
        for copy in self.c:
            copy.start()

    def take(self):
        total = self.shares[self.chip].astype(F32)
        for k in range(1, NCHIP):
            self.c[k - 1].wait_recv()
            total = total + self.slots[k].astype(F32)
        return total

    def drain(self):
        for copy in self.c:
            copy.wait_send()


class Direct:
    def __init__(self, place, block, send, recv, index):
        p = place
        chip = p.chip(p.y, p.x)
        own = block(p.g)
        self.out, self.pair = [], []
        for k in range(NCHIP):
            to, frm = lax.rem(chip + k, NCHIP) * 2 + p.core, lax.rem(chip + NCHIP - k, NCHIP) * 2 + p.core
            ref = block(frm)
            if k:
                self.out.append(remote(own, own, send.at[index, k], recv.at[index, k], "gene", to))
            self.pair.append(remote(ref, ref, send.at[index, 7 + k if k else 0], recv.at[index, 7 + k if k else 0], "gene", p.other_core))

    def start(self):
        for copy in self.out + self.pair[:1]:
            copy.start()

    def finish(self):
        for k in range(1, NCHIP):
            self.out[k - 1].wait_recv()
            self.pair[k].start()
        for copy in self.pair:
            copy.wait_recv()

    def drain(self):
        for copy in self.out + self.pair:
            copy.wait_send()


class Swap:
    def __init__(self, place, source, slots, send, recv, index):
        self.out, self.into = [], []
        for k in range(1, NG):
            to, frm = lax.rem(place.g + k, NG), lax.rem(place.g + NG - k, NG)
            self.out.append(remote(source(to), slots.at[place.g], send.at[index, k], recv.at[index, place.g], "gene", to))
            self.into.append(remote(source(frm), slots.at[frm], send.at[index, k], recv.at[index, frm], "gene", frm))

    def start(self):
        for copy in self.out:
            copy.start()

    def finish(self):
        for copy in self.into:
            copy.wait_recv()

    def drain(self):
        for copy in self.out:
            copy.wait_send()


def total_of(slots):
    total = slots[0]
    for k in range(1, NG):
        total = total + slots[k]
    return total


def group_sum(values):
    high = values.astype(BF16)
    low = (values - high.astype(F32)).astype(BF16)
    shape = (values.shape[1], values.shape[1])
    row = lax.broadcasted_iota(jnp.int32, shape, 0) // 64
    col = lax.broadcasted_iota(jnp.int32, shape, 1) // 64
    ones = (row == col).astype(F32).astype(BF16)
    return jnp.dot(high, ones, preferred_element_type=F32) + jnp.dot(low, ones, preferred_element_type=F32)


def heads_of(rows, weights, head):
    parts = [jnp.dot(rows, weights[k], preferred_element_type=F32) for k in range(3)]
    for k in range(2):
        mean = group_sum(parts[k] * parts[k]) / head
        parts[k] = (parts[k] * lax.rsqrt(jnp.maximum(mean, FLOOR))).astype(BF16)
    parts[2] = parts[2].astype(BF16)
    return parts


def turned(values, by):
    if by == 0:
        return values
    row = lax.rem(lax.broadcasted_iota(jnp.int32, values.shape, 0), ROWS)
    count = values.shape[0]
    return jnp.where(row < by, pltpu.roll(values, count - ROWS + by, 0), pltpu.roll(values, by, 0))


def within_mix(query, keys, values, head):
    q, k, v = (part.astype(F32) for part in (query, keys, values))
    count = q.shape[0]
    scores = group_sum(jnp.concatenate([q * turned(k, 4 * d) for d in range(NM)], axis=0))
    weights = [jnp.exp(scores[d * count:(d + 1) * count] * head ** (-0.5)) for d in range(NM)]
    total = weights[0] + weights[1] + weights[2] + weights[3]
    mixed = None
    for d in range(NM):
        term = (weights[d] / total).astype(BF16).astype(F32) * turned(v, 4 * d)
        mixed = term if mixed is None else mixed + term
    return mixed.astype(BF16)


def cross_mix(query, keys, values, same, head):
    lane = lax.broadcasted_iota(jnp.int32, query.shape, 1) // 64
    q = query.astype(F32)
    mixed = jnp.zeros(query.shape, F32)
    for h in range(query.shape[1] // 64):
        one = jnp.where(lane == h, q, 0.0).astype(BF16)
        scores = lax.dot_general(one, keys, DN_T, preferred_element_type=F32) * head ** (-0.5)
        weights = jnp.where(same, jnp.exp(scores), 0.0)
        probs = (weights / jnp.sum(weights, axis=-1, keepdims=True)).astype(BF16)
        mixed = jnp.where(lane == h, jnp.dot(probs, values, preferred_element_type=F32), mixed)
    return mixed.astype(BF16)


def encoder_scratch(width, genes, cells, head):
    half = cells // 2
    raw = [pltpu.VMEM((3 * head, 2, width), BF16), pltpu.VMEM((head, 2, width), BF16)]
    layer = [
        pltpu.VMEM((3, width, 256), BF16),
        pltpu.VMEM((256, width), BF16),
        pltpu.VMEM((NM, NCHIP, ROWS, width), BF16),
    ]
    return (
        [
            pltpu.VMEM((cells, genes), BF16),
            pltpu.VMEM((NM, genes, 1664), BF16),
            pltpu.VMEM((8, cells), F32),
            pltpu.VMEM((NG, 8, cells), F32),
            pltpu.VMEM((NM, NCHIP, 2, ROWS, width), BF16),
            pltpu.VMEM((NM, NCHIP, ROWS, width), BF16),
            pltpu.VMEM((128, width), F32),
            pltpu.VMEM((2, 3 * head, width), F32),
            pltpu.VMEM((NM, ROWS, width), F32),
            pltpu.VMEM((NM, ROWS, width), F32),
            pltpu.VMEM((NM, 2, 2, half, 256), BF16),
            pltpu.VMEM((NM, half, 256), BF16),
            pltpu.VMEM((cells, 128), F32),
            pltpu.SemaphoreType.DMA((NM + 4,)),
        ]
        + raw * 2
        + layer * 2
        + [pltpu.SemaphoreType.DMA((1, NG))] * 2
        + [pltpu.SemaphoreType.DMA((NM,))] * 2
        + [pltpu.SemaphoreType.DMA((NM,))] * 2
        + [pltpu.SemaphoreType.DMA((NM, NM))] * 2
        + [pltpu.SemaphoreType.DMA((2 * NM, Gather.SLOTS))] * 2
        + [pltpu.SemaphoreType.DMA((1, 16))] * 2
        + Scatter.scratch(width) * 2
        + [
            pltpu.VMEM((half, width), F32),
            pltpu.VMEM((NCHIP, ROWS, width), BF16),
            pltpu.VMEM((NCHIP, ROWS, width), BF16),
            pltpu.SemaphoreType.DMA((NCHIP,)),
            pltpu.SemaphoreType.DMA((NCHIP,)),
        ]
    )


def encode(head, early, after, counts, groups, w_hbm, q1_hbm, q2_hbm, o1_hbm, o2_hbm, hidden, library, *refs):
    (scaled, w_proj, tile, slots, halves, pair, padded, split, tokens, resid, kv, queries, spot, load_sem) = refs[:14]
    raws, layers = refs[14:18], refs[18:24]
    (s_send, s_recv, w_send, w_recv, p_send, p_recv, k_send, k_recv, a_send, a_recv, d_send, d_recv) = refs[24:36]
    sums, (gathered, shares, share_in, z_send, z_recv) = refs[36:-5], refs[-5:]
    place = Place()
    width = resid.shape[-1]
    wide = w_proj.shape[-1]
    core, here = place.core, place.chip(place.y, place.x)
    scatter = [Scatter(place, sums[10 * k:10 * k + 10]) for k in range(2)]
    weights, outs, blocks = layers[0::3], layers[1::3], layers[2::3]

    tile[...] = jnp.broadcast_to(jnp.sum(counts[...].astype(F32), axis=0, keepdims=True), tile.shape)
    swap = Swap(place, lambda t: tile, slots, s_send, s_recv, 0)
    swap.start()
    small = [
        pltpu.make_async_copy(src, dst, load_sem.at[NM + k])
        for k, (src, dst) in enumerate(zip((q1_hbm, o1_hbm, q2_hbm, o2_hbm), raws))
    ]
    loads = [
        pltpu.make_async_copy(w_hbm.at[:, pl.ds((m * width) // 128 * 128, wide)], w_proj.at[m], load_sem.at[m])
        for m in range(NM)
    ]
    for load in small[:2] + loads + small[2:]:
        load.start()
    early()
    slots[place.g] = tile[...]

    lanes = pl.ds(pl.multiple_of(core * 128, 128), 128)
    share = []
    for k in range(2):
        share.append([
            remote(weights[k].at[:, :, lanes], weights[k].at[:, :, lanes], w_send.at[2 * k], w_recv.at[2 * k], "gene", place.other_core),
            remote(outs[k].at[lanes, :], outs[k].at[lanes, :], w_send.at[2 * k + 1], w_recv.at[2 * k + 1], "gene", place.other_core),
        ])

    def prepare(k):
        padded[...] = jnp.zeros_like(padded)
        small[2 * k].wait()
        for h in range(2):
            split[h] = raws[2 * k][:, h, :].astype(F32)
        for a in range(3):
            for h in range(2):
                padded[64 * h:64 * h + head, :] = split[h, a * head:(a + 1) * head, :]
            weights[k][a, :, lanes] = padded[...].T.astype(BF16)
        share[k][0].start()
        small[2 * k + 1].wait()
        for h in range(2):
            padded[64 * h:64 * h + head, :] = raws[2 * k + 1][:, h, :].astype(F32)
        outs[k][lanes, :] = padded[...].astype(BF16)
        share[k][1].start()

    prepare(0)
    swap.finish()
    total = 1.0 + total_of(slots)
    library[...] = total
    scaled[...] = jnp.log1p(counts[...].astype(F32) * (TARGET / total[0:1])).T.astype(BF16)

    pairs = [
        remote(halves.at[m, :, 1 - core], pair.at[m], p_send.at[m], p_recv.at[m], "gene", place.other_core)
        for m in range(NM)
    ]

    def project(m):
        loads[m].wait()
        skip = (m * width) % 128
        out = jnp.dot(scaled[...], w_proj[m], preferred_element_type=F32)[:, skip:skip + width]
        halves[m] = out.astype(BF16).reshape(NCHIP, 2, ROWS, width)
        pairs[m].start()

    def join(m):
        pairs[m].wait_recv()
        for q in range(NCHIP):
            scatter[0].chip[m, q] = (halves[m, q, core].astype(F32) + pair[m, q].astype(F32)).astype(BF16)
        scatter[0].spread(m)

    def keep(m):
        scatter[0].mine[m] = scatter[0].take(m)

    run_pipeline([project, join, scatter[0].forward, scatter[0].cross, keep])

    gathers = [
        [
            GatherX(place, lambda q, k=k, m=m: blocks[k].at[m, q], a_send, a_recv, k * NM + m, m == 0)
            if m % 2 == 0
            else Gather(place, lambda q, k=k, m=m: blocks[k].at[m, q], a_send, a_recv, k * NM + m)
            for m in range(NM)
        ]
        for k in range(2)
    ]
    for s in range(NM):
        for m in range(NM):
            tokens[s, 4 * m:4 * m + 4, :] = scatter[0].mine[m, 4 * s:4 * s + 4, :]
        blocks[0][s, here] = rms(tokens[s]).astype(BF16)
        gathers[0][s].start()

    prepare(1)
    cells = 2 * kv.shape[3]
    at = lax.broadcasted_iota(jnp.int32, (cells, cells), 1)
    source = 32 * (lax.rem(at, 128) // ROWS) + ROWS * (at // 128) + lax.rem(at, ROWS)
    order = (lax.broadcasted_iota(jnp.int32, (cells, cells), 0) == source).astype(F32).astype(BF16)
    row = jnp.dot(
        jnp.broadcast_to(groups[...].astype(F32), (128, cells)).astype(BF16), order, preferred_element_type=F32
    )
    spot[...] = row.T
    same = jnp.broadcast_to(spot[lanes, 0:1], (128, cells)) == row
    for copy in share[0]:
        copy.wait_recv()

    def within(s):
        gathers[0][s].finish()
        rows = blocks[0][s].reshape(NCHIP * ROWS, width)
        mixed = within_mix(*heads_of(rows, weights[0], head), head)
        out = jnp.dot(mixed, outs[0][...], preferred_element_type=F32)
        scatter[1].chip[s] = out.astype(BF16).reshape(NCHIP, ROWS, width)
        scatter[1].spread(s)

    def add_within(s):
        tokens[s] = tokens[s] + scatter[1].take(s)

    run_pipeline([
        lambda s: gathers[0][s].second(), lambda s: gathers[0][s].third(), within,
        scatter[1].forward, scatter[1].cross, add_within,
    ])

    for m in range(NM):
        for s in range(NM):
            resid[m, 4 * s:4 * s + 4, :] = tokens[s, 4 * m:4 * m + 4, :]
        blocks[1][m, here] = rms(resid[m]).astype(BF16)
        gathers[1][m].start()
    for copy in share[1]:
        copy.wait_recv()
    trade = [
        remote(kv.at[m, core], kv.at[m, core], k_send.at[m, 0], k_recv.at[m, 0], "gene", place.other_core)
        for m in range(NM)
    ]

    def look(m):
        gathers[1][m].finish()
        rows = blocks[1][m].reshape(NCHIP * ROWS, width)
        queries[m], kv[m, core, 0], kv[m, core, 1] = heads_of(rows, weights[1], head)
        trade[m].start()

    def attend(m):
        trade[m].wait_recv()
        keys = jnp.concatenate([kv[m, 0, 0], kv[m, 1, 0]], axis=0)
        values = jnp.concatenate([kv[m, 0, 1], kv[m, 1, 1]], axis=0)
        mixed = cross_mix(queries[m], keys, values, same, head)
        out = jnp.dot(mixed, outs[1][...], preferred_element_type=F32)
        gathered[...] = gathered[...] + out if m else out

    run_pipeline([lambda m: gathers[1][m].second(), lambda m: gathers[1][m].third(), look, attend])

    shares[...] = gathered[...].astype(BF16).reshape(NCHIP, ROWS, width)
    final = DirectSum(place, shares, share_in, z_send, z_recv)
    final.start()
    pooled = (resid[0] + resid[1] + resid[2] + resid[3] + final.take()) * (1.0 / NM)
    hidden[pl.ds(pl.multiple_of(place.g * ROWS, ROWS), ROWS), :] = rms(pooled).astype(BF16)
    last = Direct(
        place, lambda o: hidden.at[pl.ds(pl.multiple_of(o * ROWS, ROWS), ROWS), :], d_send, d_recv, 0
    )
    last.start()
    after()
    last.finish()
    for one in scatter + gathers[0] + gathers[1] + [swap, final, last]:
        one.drain()
    for copy in share[0] + share[1] + pairs + trade:
        copy.wait_send()


class GroupGather:
    SLOTS = 7

    def __init__(self, r, block, send, recv, index):
        z, h = lax.rem(r, NZ), r // NZ
        up, down = lax.rem(z + 1, NZ), lax.rem(z + 3, NZ)
        k = 1 - h

        def at(a, b):
            return a * NZ + b

        def go(slot, owner, to):
            ref = block(owner)
            return remote(ref, ref, send.at[index, slot], recv.at[index, slot], "grp", to)

        self.c = [
            go(0, at(h, z), at(k, z)),
            go(1, at(h, z), at(h, up)),
            go(2, at(h, z), at(h, down)),
            go(3, at(k, z), at(h, up)),
            go(4, at(k, z), at(h, down)),
            go(5, at(h, down), at(h, up)),
            go(6, at(k, up), at(h, down)),
        ]

    def start(self):
        for k in (1, 2, 0):
            self.c[k].start()

    def second(self):
        c = self.c
        c[1].wait_recv()
        c[5].start()
        c[0].wait_recv()
        c[3].start()
        c[4].start()

    def third(self):
        self.c[4].wait_recv()
        self.c[6].start()

    def finish(self):
        for k in (2, 3, 5, 6):
            self.c[k].wait_recv()

    def drain(self):
        for copy in self.c:
            copy.wait_send()


class GroupGatherZ:
    def __init__(self, r, block, send, recv, index, upward):
        z, h = lax.rem(r, NZ), r // NZ
        up, down, across = lax.rem(z + 1, NZ), lax.rem(z + 3, NZ), lax.rem(z + 2, NZ)
        k = 1 - h
        self.upward = upward

        def at(a, b):
            return a * NZ + b

        def go(slot, owner, to):
            ref = block(owner)
            return remote(ref, ref, send.at[index, slot], recv.at[index, slot], "grp", to)

        self.c = [
            go(0, at(h, z), at(h, up)),
            go(1, at(h, z), at(h, down)),
            go(2, at(h, down), at(h, up)) if upward else go(2, at(h, up), at(h, down)),
            go(3, at(h, z), at(k, z)),
            go(4, at(h, down), at(k, z)),
            go(5, at(h, up), at(k, z)),
            go(6, at(h, across), at(k, z)),
        ]

    def start(self):
        for k in (0, 1, 3):
            self.c[k].start()

    def second(self):
        c = self.c
        for k in (0, 1):
            c[k].wait_recv()
            if self.upward == (k == 0):
                c[2].start()
            c[4 + k].start()

    def third(self):
        self.c[2].wait_recv()
        self.c[6].start()

    def finish(self):
        for k in (3, 4, 5, 6):
            self.c[k].wait_recv()

    def drain(self):
        for copy in self.c:
            copy.wait_send()


class GroupDirect:
    def __init__(self, r, block, send, recv):
        self.out, self.into = [], []
        for k in range(1, NR):
            to, frm = lax.rem(r + k, NR), lax.rem(r + NR - k, NR)
            self.out.append(remote(block(r), block(r), send.at[k], recv.at[k], "grp", to))
            self.into.append(remote(block(r), block(frm), send.at[k], recv.at[k], "grp", frm))

    def start(self):
        for copy in self.out:
            copy.start()

    def finish(self):
        for copy in self.into:
            copy.wait_recv()

    def drain(self):
        for copy in self.out:
            copy.wait_send()


def log_factorials(count):
    return [math.log(math.factorial(k)) for k in range(count)]


def terms(x, theta, logit, rate_scale, norm_scale, most):
    tail = jnp.exp(-jnp.abs(logit))
    soft = jnp.maximum(logit, 0.0) + jnp.log1p(tail)
    sigmoid = jnp.where(logit >= 0, 1.0, tail) / (1.0 + tail)
    rate = rate_scale * soft
    product = jnp.ones_like(theta)
    slope = jnp.zeros_like(theta)
    log_factorial = jnp.zeros_like(theta)
    table = log_factorials(most + 1)
    for k in range(most):
        on = x > k
        term = theta + float(k)
        slope = jnp.where(on, slope * term + product, slope)
        product = jnp.where(on, product * term, product)
        if k:
            log_factorial = jnp.where(on, table[k + 1], log_factorial)
    total = theta + rate
    log_total = jnp.log(total)
    log_theta = jnp.log(theta)
    ratio = (theta + x) / total
    nll = -(
        jnp.log(product) - log_factorial
        + theta * (log_theta - log_total)
        + x * (jnp.log(rate) - log_total)
    )
    d_logit = (ratio - x / rate) * rate_scale * sigmoid * norm_scale
    d_theta = -(slope / product + log_theta + 1.0 - log_total - ratio)
    return nll, d_logit, d_theta


def network_kernel(
    head, genes_all, cells_all, panel_count, encoder_count,
    counts, groups, w_hbm, q1_hbm, q2_hbm, o1_hbm, o2_hbm, panel_row, w_mean_hbm, w_disp,
    cell_loss, gradient, disp_block, *refs,
):
    (
        hidden, library, w_mean, tile, slots, back, piece, columns, field, panel_part, loss, panel_col, mean_sem,
        s_send, s_recv, h_send, h_recv, v_send, v_recv, f_send, f_recv, d_send, d_recv, o_send, o_recv,
    ) = refs[encoder_count:]
    place = Place()
    r = lax.axis_index("grp")
    genes, cells = counts.shape
    width = hidden.shape[1]
    share = width // NR
    parts = 4
    step = genes // parts
    norm_scale = cells_all ** (-0.5)
    rows = pl.ds(pl.multiple_of(place.g * ROWS, ROWS), ROWS)
    out, into = [], []
    for k in range(1, NR):
        to, frm = lax.rem(r + k, NR), lax.rem(r + NR - k, NR)
        out.append(remote(piece.at[to], columns.at[r, rows], h_send.at[k], h_recv.at[r], "grp", to))
        into.append(remote(piece.at[frm], columns.at[frm, rows], h_send.at[k], h_recv.at[frm], "grp", frm))
    load_mean = pltpu.make_async_copy(w_mean_hbm, w_mean, mean_sem)

    def early():
        load_mean.start()
        panel_col[...] = jnp.broadcast_to(panel_row[...].astype(F32), (128, genes)).T
        piece[...] = jnp.zeros_like(piece)
        panel_part[...] = jnp.zeros_like(panel_part)
        loss[...] = jnp.zeros_like(loss)

    def after():
        own = hidden[rows, :].astype(F32)
        for k in range(NR):
            piece[k, :, 0:share] = own[:, k * share:(k + 1) * share].astype(BF16)
        for copy in out:
            copy.start()
        columns[r, rows] = piece[r]

    greet(everyone(place) + [("grp", lax.rem(r + k, NR)) for k in range(1, NR)])
    encode(
        head, early, after, counts, groups, w_hbm, q1_hbm, q2_hbm, o1_hbm, o2_hbm, hidden, library, *refs[:encoder_count]
    )
    load_mean.wait()
    disp = lax.dot_general(w_disp[...], hidden[...], DN_T, preferred_element_type=F32)
    table = DISP_BASE + (jnp.maximum(disp, 0.0) + jnp.log1p(jnp.exp(-jnp.abs(disp))))
    high = table.astype(BF16)
    rest = table - high.astype(F32)
    middle = rest.astype(BF16)
    low = (rest - middle.astype(F32)).astype(BF16)
    tables = jnp.concatenate([high, middle, low], axis=0)
    rate_scale = library[0:1] / genes_all

    v_gather = WideGather(
        place, lambda o: columns.at[:, pl.ds(pl.multiple_of(o * ROWS, ROWS), ROWS), :], v_send, v_recv, 0
    )
    field_gather = []
    for p in range(parts):
        block = lambda o, p=p: field.at[o, pl.ds(p * step, step), :]
        field_gather.append(
            GroupGatherZ(r, block, f_send, f_recv, p, True) if p == 0 else GroupGather(r, block, f_send, f_recv, p)
        )
    disp_gather = GroupDirect(r, lambda o: field.at[o, pl.ds(genes, panel_count), :], d_send, d_recv)
    spread = GroupDirect(r, lambda o: disp_block.at[o], o_send, o_recv)

    def decode(p):
        at = pl.ds(p * step, step)
        x = counts[at, :].astype(F32)
        logit = lax.dot_general(w_mean[at, :], hidden[...], DN_T, preferred_element_type=F32)
        lane = lax.broadcasted_iota(jnp.int32, (step, 3 * panel_count), 1)
        pick = (panel_col[at, 0:1] == lax.rem(lane, panel_count).astype(F32)).astype(F32).astype(BF16)
        theta = jnp.dot(pick, tables, preferred_element_type=F32)
        nll, d_logit, d_theta = terms(x, theta, logit, rate_scale, norm_scale, 12)
        field[r, at, :] = d_logit.astype(BF16)
        field_gather[p].start()
        loss[...] += jnp.sum(nll, axis=0, keepdims=True)
        row = lax.broadcasted_iota(jnp.int32, (step, 128), 1)
        wanted = jnp.where(lax.rem(row, 8) < 4, (row // 8) * 4 + lax.rem(row, 8), -1)
        pick_t = (panel_col[at, :] == wanted.astype(F32)).astype(F32).astype(BF16)
        upper = d_theta.astype(BF16)
        lower = (d_theta - upper.astype(F32)).astype(BF16)
        panel_part[...] += lax.dot_general(pick_t, upper, DN_0, preferred_element_type=F32) + lax.dot_general(
            pick_t, lower, DN_0, preferred_element_type=F32
        )

    for copy in into:
        copy.wait_recv()
    v_gather.start()
    decode(0)
    v_gather.second()
    decode(1)
    field_gather[0].second()
    v_gather.third()
    decode(2)
    field_gather[1].second()
    field_gather[0].third()
    decode(3)

    row = lax.broadcasted_iota(jnp.int32, (128, cells), 0)
    both = jnp.where(lax.rem(row, 8) == 4, loss[...], panel_part[...])
    tile[...] = both.reshape(NG, 8, cells)
    first = Swap(place, lambda t: tile.at[t], slots, s_send, s_recv, 0)
    first.start()
    slots[place.g] = tile[place.g]
    field_gather[2].second()
    field_gather[1].third()
    first.finish()
    summed = total_of(slots)
    cell_loss[...] = summed[4:5] / genes_all
    back[place.g] = summed
    second = Swap(place, lambda t: back.at[place.g], back, s_send, s_recv, 1)
    second.start()
    field_gather[2].third()
    field_gather[3].second()
    second.finish()
    d_panel = jnp.concatenate([back[k, 0:4] for k in range(NG)], axis=0)
    tail = jnp.exp(-jnp.abs(disp))
    d_disp = d_panel * (jnp.where(disp >= 0, 1.0, tail) / (1.0 + tail)) * norm_scale
    field[r, pl.ds(genes, panel_count), :] = d_disp.astype(BF16)
    disp_gather.start()
    field_gather[3].third()

    def contract(at, size):
        total = jnp.zeros((size, columns.shape[2]), F32)
        for k in range(NR):
            total = total + jnp.dot(field[k, pl.ds(at, size), :], columns[k], preferred_element_type=F32)
        return total

    def gradient_of(p):
        field_gather[p].finish()
        gradient[pl.ds(p * step, step), :] = contract(p * step, step)

    v_gather.finish()
    gradient_of(0)
    gradient_of(1)
    disp_gather.finish()
    disp_block[r] = contract(genes, panel_count)
    spread.start()
    gradient_of(2)
    gradient_of(3)
    spread.finish()
    for copy in out:
        copy.wait_send()
    for one in [v_gather, first, second, disp_gather, spread] + field_gather:
        one.drain()


def finish_kernel(gradient, disp_block, loss, cell_loss, grad_mean, grad_disp):
    share = grad_mean.shape[0]
    cell_loss[...] = loss[...]
    grad_mean[...] = gradient[...].T[0:share]
    for k in range(NR):
        grad_disp[:, k * share:(k + 1) * share] = disp_block[k, :, 0:share]


def whole():
    return pl.BlockSpec(memory_space=pltpu.VMEM)


def params(number):
    return pltpu.CompilerParams(collective_id=number, has_side_effects=True, vmem_limit_bytes=LIMIT)


def shards(counts, panels, membership, w_proj, w_qkv_within, w_out_within, w_qkv_cross, w_out_cross, w_mean, w_disp):
    cells, genes = counts.shape
    width = w_qkv_within.shape[0]
    head = w_out_within.shape[1]
    genes_all = genes * NG
    cells_all = cells * NR
    panel_count = w_disp.shape[1]
    counts_t = counts.T
    swap_sems = [pltpu.SemaphoreType.DMA((2, NG))] * 2
    first_part = encoder_scratch(width, genes, cells, head)
    cell_loss, gradient, disp_block = pl.pallas_call(
        functools.partial(network_kernel, head, genes_all, cells_all, panel_count, len(first_part)),
        name="network",
        out_shape=(
            jax.ShapeDtypeStruct((1, cells), F32),
            jax.ShapeDtypeStruct((genes, 256), F32),
            jax.ShapeDtypeStruct((NR, panel_count, 256), F32),
        ),
        in_specs=[whole()] * 2 + [pl.BlockSpec(memory_space=pl.ANY)] * 5 + [whole(), pl.BlockSpec(memory_space=pl.ANY), whole()],
        out_specs=(whole(), whole(), whole()),
        scratch_shapes=first_part + [
            pltpu.VMEM((cells, width), BF16),
            pltpu.VMEM((8, cells), F32),
            pltpu.VMEM((genes, width), BF16),
            pltpu.VMEM((NG, 8, cells), F32),
            pltpu.VMEM((NG, 8, cells), F32),
            pltpu.VMEM((NG, 8, cells), F32),
            pltpu.VMEM((NR, ROWS, 256), BF16),
            pltpu.VMEM((NR, cells, 256), BF16),
            pltpu.VMEM((NR, genes + panel_count, cells), BF16),
            pltpu.VMEM((128, cells), F32),
            pltpu.VMEM((1, cells), F32),
            pltpu.VMEM((genes, 128), F32),
            pltpu.SemaphoreType.DMA,
        ] + swap_sems + [
            pltpu.SemaphoreType.DMA((NR,)),
            pltpu.SemaphoreType.DMA((NR,)),
            pltpu.SemaphoreType.DMA((1, WideGather.SLOTS)),
            pltpu.SemaphoreType.DMA((1, WideGather.SLOTS)),
            pltpu.SemaphoreType.DMA((4, GroupGather.SLOTS)),
            pltpu.SemaphoreType.DMA((4, GroupGather.SLOTS)),
            pltpu.SemaphoreType.DMA((NR,)),
            pltpu.SemaphoreType.DMA((NR,)),
            pltpu.SemaphoreType.DMA((NR,)),
            pltpu.SemaphoreType.DMA((NR,)),
        ],
        compiler_params=params(0),
    )(
        counts_t, membership, w_proj, jnp.transpose(w_qkv_within, (2, 1, 0)), jnp.transpose(w_qkv_cross, (2, 1, 0)),
        jnp.transpose(w_out_within, (1, 0, 2)), jnp.transpose(w_out_cross, (1, 0, 2)),
        panels[None, :], w_mean.T, w_disp.T,
    )
    cell_loss, grad_mean, grad_disp = pl.pallas_call(
        finish_kernel,
        name="finish",
        out_shape=(
            jax.ShapeDtypeStruct((1, cells), F32),
            jax.ShapeDtypeStruct((width // NR, genes), F32),
            jax.ShapeDtypeStruct((panel_count, width), F32),
        ),
        in_specs=[whole()] * 3,
        out_specs=(whole(), whole(), whole()),
    )(gradient, disp_block, cell_loss)
    return cell_loss[0], grad_mean, grad_disp.T


def solution(mesh):
    return jax.shard_map(
        shards,
        mesh=mesh,
        in_specs=(
            P("grp", "gene"),
            P("gene"),
            P("grp", None),
            P("gene", None),
            P(None, "gene", None),
            P("gene", None, None),
            P(None, "gene", None),
            P("gene", None, None),
            P(None, "gene"),
            P(),
        ),
        out_specs=(P("grp"), P("grp", "gene"), P()),
        check_vma=False,
    )
```

```python
import functools
import math

import jax
import jax.numpy as jnp
from jax import lax
from jax.experimental import pallas as pl
from jax.experimental.pallas import tpu as pltpu
from jax.sharding import PartitionSpec as P

EPS = 1e-06
FLOOR = 0.3
TARGET = 10000.0
DISP_BASE = 0.5
MESH = pl.DeviceIdType.MESH
F32 = jnp.float32
BF16 = jnp.bfloat16

NX = 4
NY = 2
NG = 16
NCHIP = 8
NR = 8
NZ = 4
NM = 4
ROWS = 16
LIMIT = 64 * 1024 * 1024 - 256 * 1024
DN_T = (((1,), (1,)), ((), ()))
DN_0 = (((0,), (0,)), ((), ()))


def remote(src, dst, send, recv, axis, to):
    return pltpu.make_async_remote_copy(
        src_ref=src, dst_ref=dst, send_sem=send, recv_sem=recv, device_id={axis: to}, device_id_type=MESH
    )


class Place:
    def __init__(self):
        self.g = lax.axis_index("gene")
        self.core = lax.rem(self.g, 2)
        self.x = lax.rem(self.g // 2, NX)
        self.y = self.g // (2 * NX)
        self.right = self.at(self.y, self.shift(1), self.core)
        self.left = self.at(self.y, self.shift(3), self.core)
        self.other_y = self.at(1 - self.y, self.x, self.core)
        self.other_core = self.at(self.y, self.x, 1 - self.core)

    def shift(self, by):
        return lax.rem(self.x + by, NX)

    def at(self, y, x, core):
        return (y * NX + x) * 2 + core

    def chip(self, y, x):
        return y * NX + x


def greet(axis_peers, meanwhile):
    barrier = pltpu.get_barrier_semaphore()
    for axis, to in axis_peers:
        pl.semaphore_signal(barrier, inc=1, device_id={axis: to}, device_id_type=MESH)
    meanwhile()
    pl.semaphore_wait(barrier, len(axis_peers))


def everyone(place):
    return [("gene", lax.rem(place.g + k, NG)) for k in range(1, NG)]


def rms(values):
    return values * lax.rsqrt(jnp.mean(values * values, axis=-1, keepdims=True) + EPS)


class Scatter:
    @staticmethod
    def scratch(width):
        return [
            pltpu.VMEM((NM, NCHIP, ROWS, width), BF16),
            pltpu.VMEM((NM, 3, ROWS, width), BF16),
            pltpu.VMEM((NM, 3, ROWS, width), BF16),
            pltpu.VMEM((NM, 2, ROWS, width), BF16),
            pltpu.VMEM((NM, ROWS, width), BF16),
            pltpu.VMEM((NM, ROWS, width), BF16),
            pltpu.VMEM((NM, ROWS, width), F32),
            pltpu.VMEM((2, NX, ROWS, width), BF16),
            pltpu.SemaphoreType.DMA((NM, 7)),
            pltpu.SemaphoreType.DMA((NM, 7)),
        ]

    def __init__(self, place, refs):
        (self.chip, self.from_left, self.from_right, self.relay, self.y_out, self.y_in, self.mine, four, send, recv) = refs
        self.send, self.recv = send, recv
        p = self.place = place
        ahead, behind, across = p.shift(1), p.shift(3), p.shift(2)
        self.copies, self.turned = [], {}
        for m in range(NM):
            if m % 2 == 0:
                self.turned[m] = ScatterY(self, m, four.at[m // 2], 1 if m == 0 else -1)
                self.copies.append(self.turned[m].c)
                continue

            def go(slot, src, dst, to):
                return remote(src, dst, send.at[m, slot], recv.at[m, slot], "gene", to)
            self.copies.append([
                go(0, self.chip.at[m, p.chip(0, across)], self.from_left.at[m, 0], p.right),
                go(1, self.chip.at[m, p.chip(1, across)], self.from_right.at[m, 0], p.left),
                go(2, self.chip.at[m, p.chip(1, ahead)], self.from_left.at[m, 2], p.right),
                go(3, self.chip.at[m, p.chip(0, behind)], self.from_right.at[m, 2], p.left),
                go(4, self.relay.at[m, 0], self.from_left.at[m, 1], p.right),
                go(5, self.relay.at[m, 1], self.from_right.at[m, 1], p.left),
                go(6, self.y_out.at[m], self.y_in.at[m], p.other_y),
            ])

    def spread(self, m):
        if m in self.turned:
            return self.turned[m].spread()
        for k in (0, 1, 2, 3):
            self.copies[m][k].start()

    def forward(self, m):
        if m in self.turned:
            return self.turned[m].forward()
        p = self.place
        self.copies[m][0].wait_recv()
        self.relay[m, 0] = (
            self.chip[m, p.chip(0, p.shift(1))].astype(F32) + self.from_left[m, 0].astype(F32)
        ).astype(BF16)
        self.copies[m][4].start()
        self.copies[m][1].wait_recv()
        self.relay[m, 1] = (
            self.chip[m, p.chip(1, p.shift(3))].astype(F32) + self.from_right[m, 0].astype(F32)
        ).astype(BF16)
        self.copies[m][5].start()

    def cross(self, m):
        if m in self.turned:
            return self.turned[m].cross()
        p = self.place
        for k in (2, 3, 4, 5):
            self.copies[m][k].wait_recv()
        self.y_out[m] = (
            self.chip[m, p.chip(1 - p.y, p.x)].astype(F32)
            + self.from_left[m, 2 - p.y].astype(F32)
            + self.from_right[m, 1 + p.y].astype(F32)
        ).astype(BF16)
        self.copies[m][6].start()
        self.mine[m] = (
            self.chip[m, p.chip(p.y, p.x)].astype(F32)
            + self.from_left[m, 1 + p.y].astype(F32)
            + self.from_right[m, 2 - p.y].astype(F32)
        )

    def take(self, m):
        if m in self.turned:
            return self.turned[m].take()
        self.copies[m][6].wait_recv()
        return self.mine[m] + self.y_in[m].astype(F32)

    def drain(self):
        for row in self.copies:
            for copy in row:
                copy.wait_send()


class ScatterY:
    def __init__(self, base, m, y_four, way):
        p = base.place
        self.base, self.m, self.four = base, m, y_four
        to, back = (p.right, p.left) if way > 0 else (p.left, p.right)
        ahead, behind = (p.shift(1), p.shift(3)) if way > 0 else (p.shift(3), p.shift(1))
        self.order = (p.shift(2), behind, ahead)
        self.outgoing = (base.relay.at[m, 0], base.relay.at[m, 1], base.y_out.at[m])
        self.incoming = (base.from_left.at[m, 0], base.from_right.at[m, 0], base.from_left.at[m, 1])

        def go(slot, src, dst, device):
            return remote(src, dst, base.send.at[m, slot], base.recv.at[m, slot], "gene", device)

        self.c = [
            go(k, base.chip.at[m, p.chip(1 - p.y, x)], y_four.at[x], p.other_y)
            for k, x in enumerate(self.order + (p.x,))
        ] + [go(4 + k, self.outgoing[k], self.incoming[k], (to, back, to)[k]) for k in range(3)]

    def spread(self):
        for k in range(4):
            self.c[k].start()

    def total(self, k):
        p = self.base.place
        x = p.x if k == 3 else self.order[k]
        self.c[k].wait_recv()
        return self.base.chip[self.m, p.chip(p.y, x)].astype(F32) + self.four[x].astype(F32)

    def forward(self):
        for k in (0, 1):
            self.outgoing[k][...] = self.total(k).astype(BF16)
            self.c[4 + k].start()

    def cross(self):
        value = self.total(2)
        self.c[4].wait_recv()
        self.outgoing[2][...] = (value + self.incoming[0][...].astype(F32)).astype(BF16)
        self.c[6].start()
        self.base.mine[self.m] = self.total(3)

    def take(self):
        self.c[5].wait_recv()
        self.c[6].wait_recv()
        return self.base.mine[self.m] + self.incoming[1][...].astype(F32) + self.incoming[2][...].astype(F32)


def run_pipeline(steps, count=NM):
    for t in range(count + len(steps) - 1):
        for lag, step in enumerate(steps):
            if 0 <= t - lag < count:
                step(t - lag)


class Gather:
    SLOTS = 7

    def __init__(self, place, block, send, recv, index):
        p = place
        ahead, behind, across = p.shift(1), p.shift(3), p.shift(2)
        y, z, x = p.y, 1 - p.y, p.x

        def go(slot, owner, to):
            ref = block(owner)
            return remote(ref, ref, send.at[index, slot], recv.at[index, slot], "gene", to)

        own, paired = p.chip(y, x), p.chip(z, x)
        self.c = [
            go(0, own, p.other_y),
            go(1, own, p.right),
            go(2, own, p.left),
            go(3, paired, p.right),
            go(4, paired, p.left),
            go(5, p.chip(y, behind), p.right),
            go(6, p.chip(z, ahead), p.left),
        ]

    def start(self):
        for k in (1, 2, 0):
            self.c[k].start()

    def second(self):
        c = self.c
        c[1].wait_recv()
        c[5].start()
        c[0].wait_recv()
        c[3].start()
        c[4].start()

    def third(self):
        self.c[4].wait_recv()
        self.c[6].start()

    def finish(self):
        for k in (2, 3, 5, 6):
            self.c[k].wait_recv()

    def drain(self):
        for copy in self.c:
            copy.wait_send()


class GatherX:
    def __init__(self, place, block, send, recv, index, rightward):
        p = place
        ahead, behind, across = p.shift(1), p.shift(3), p.shift(2)
        y, x = p.y, p.x
        self.rightward = rightward

        def go(slot, owner, to):
            ref = block(owner)
            return remote(ref, ref, send.at[index, slot], recv.at[index, slot], "gene", to)

        self.c = [
            go(0, p.chip(y, x), p.right),
            go(1, p.chip(y, x), p.left),
            go(2, p.chip(y, behind), p.right) if rightward else go(2, p.chip(y, ahead), p.left),
            go(3, p.chip(y, x), p.other_y),
            go(4, p.chip(y, behind), p.other_y),
            go(5, p.chip(y, ahead), p.other_y),
            go(6, p.chip(y, across), p.other_y),
        ]

    def start(self):
        for k in (0, 1, 3):
            self.c[k].start()

    def second(self):
        c = self.c
        for k in (0, 1):
            c[k].wait_recv()
            if self.rightward == (k == 0):
                c[2].start()
            c[4 + k].start()

    def third(self):
        self.c[2].wait_recv()
        self.c[6].start()

    def finish(self):
        for k in (3, 4, 5, 6):
            self.c[k].wait_recv()

    def drain(self):
        for copy in self.c:
            copy.wait_send()


class WideGather:
    SLOTS = 15

    def __init__(self, place, block, send, recv, index):
        p = place
        core, x, y, z = p.core, p.x, p.y, 1 - p.y
        ahead, behind, across = p.shift(1), p.shift(3), p.shift(2)
        self.far = Gather(place, lambda q: block(2 * q + core), send, recv, index)
        held = [p.chip(y, x), p.chip(z, x), p.chip(y, behind), p.chip(y, ahead), p.chip(z, behind), p.chip(z, ahead),
                p.chip(y, across), p.chip(z, across)]
        self.near = []
        for k, q in enumerate(held):
            ref = block(2 * q + core)
            self.near.append(remote(ref, ref, send.at[index, 7 + k], recv.at[index, 7 + k], "gene", p.other_core))

    def start(self):
        self.far.start()
        self.near[0].start()

    def second(self):
        self.far.second()
        self.near[1].start()
        self.near[2].start()

    def third(self):
        self.far.third()
        self.near[5].start()

    def finish(self):
        self.far.finish()
        for k in (3, 4, 6, 7):
            self.near[k].start()
        for copy in self.near:
            copy.wait_recv()

    def drain(self):
        self.far.drain()
        for copy in self.near:
            copy.wait_send()


class DirectSum:
    def __init__(self, place, shares, slots, send, recv):
        p = place
        self.shares, self.slots = shares, slots
        self.chip = p.chip(p.y, p.x)
        self.c = []
        for k in range(1, NCHIP):
            to = lax.rem(self.chip + k, NCHIP)
            self.c.append(remote(shares.at[to], slots.at[k], send.at[k], recv.at[k], "gene", to * 2 + p.core))

    def start(self):
        for copy in self.c:
            copy.start()

    def take(self):
        total = self.shares[self.chip].astype(F32)
        for k in range(1, NCHIP):
            self.c[k - 1].wait_recv()
            total = total + self.slots[k].astype(F32)
        return total

    def drain(self):
        for copy in self.c:
            copy.wait_send()


class Direct:
    def __init__(self, place, block, send, recv, index):
        p = place
        chip = p.chip(p.y, p.x)
        own = block(p.g)
        self.out, self.pair = [], []
        for k in range(NCHIP):
            to, frm = lax.rem(chip + k, NCHIP) * 2 + p.core, lax.rem(chip + NCHIP - k, NCHIP) * 2 + p.core
            ref = block(frm)
            if k:
                self.out.append(remote(own, own, send.at[index, k], recv.at[index, k], "gene", to))
            self.pair.append(remote(ref, ref, send.at[index, 7 + k if k else 0], recv.at[index, 7 + k if k else 0], "gene", p.other_core))

    def start(self):
        for copy in self.out + self.pair[:1]:
            copy.start()

    def finish(self):
        for k in range(1, NCHIP):
            self.out[k - 1].wait_recv()
            self.pair[k].start()
        for copy in self.pair:
            copy.wait_recv()

    def drain(self):
        for copy in self.out + self.pair:
            copy.wait_send()


class Swap:
    def __init__(self, place, source, slots, send, recv, index):
        self.out, self.into = [], []
        for k in range(1, NG):
            to, frm = lax.rem(place.g + k, NG), lax.rem(place.g + NG - k, NG)
            self.out.append(remote(source(to), slots.at[place.g], send.at[index, k], recv.at[index, place.g], "gene", to))
            self.into.append(remote(source(frm), slots.at[frm], send.at[index, k], recv.at[index, frm], "gene", frm))

    def start(self):
        for copy in self.out:
            copy.start()

    def finish(self):
        for copy in self.into:
            copy.wait_recv()

    def drain(self):
        for copy in self.out:
            copy.wait_send()


def total_of(slots):
    total = slots[0]
    for k in range(1, NG):
        total = total + slots[k]
    return total


def group_sum(values):
    high = values.astype(BF16)
    low = (values - high.astype(F32)).astype(BF16)
    shape = (values.shape[1], values.shape[1])
    row = lax.broadcasted_iota(jnp.int32, shape, 0) // 64
    col = lax.broadcasted_iota(jnp.int32, shape, 1) // 64
    ones = (row == col).astype(F32).astype(BF16)
    return jnp.dot(high, ones, preferred_element_type=F32) + jnp.dot(low, ones, preferred_element_type=F32)


def heads_of(rows, weights, head):
    parts = [jnp.dot(rows, weights[k], preferred_element_type=F32) for k in range(3)]
    for k in range(2):
        mean = group_sum(parts[k] * parts[k]) / head
        parts[k] = (parts[k] * lax.rsqrt(jnp.maximum(mean, FLOOR))).astype(BF16)
    parts[2] = parts[2].astype(BF16)
    return parts


def turned(values, by):
    if by == 0:
        return values
    row = lax.rem(lax.broadcasted_iota(jnp.int32, values.shape, 0), ROWS)
    count = values.shape[0]
    return jnp.where(row < by, pltpu.roll(values, count - ROWS + by, 0), pltpu.roll(values, by, 0))


def within_mix(query, keys, values, head):
    q, k, v = (part.astype(F32) for part in (query, keys, values))
    count = q.shape[0]
    scores = group_sum(jnp.concatenate([q * turned(k, 4 * d) for d in range(NM)], axis=0))
    weights = [jnp.exp(scores[d * count:(d + 1) * count] * head ** (-0.5)) for d in range(NM)]
    total = weights[0] + weights[1] + weights[2] + weights[3]
    mixed = None
    for d in range(NM):
        term = (weights[d] / total).astype(BF16).astype(F32) * turned(v, 4 * d)
        mixed = term if mixed is None else mixed + term
    return mixed.astype(BF16)


def cross_mix(query, keys, values, same, head):
    lane = lax.broadcasted_iota(jnp.int32, query.shape, 1) // 64
    q = query.astype(F32)
    mixed = jnp.zeros(query.shape, F32)
    for h in range(query.shape[1] // 64):
        one = jnp.where(lane == h, q, 0.0).astype(BF16)
        scores = lax.dot_general(one, keys, DN_T, preferred_element_type=F32) * head ** (-0.5)
        weights = jnp.where(same, jnp.exp(scores), 0.0)
        probs = (weights / jnp.sum(weights, axis=-1, keepdims=True)).astype(BF16)
        mixed = jnp.where(lane == h, jnp.dot(probs, values, preferred_element_type=F32), mixed)
    return mixed.astype(BF16)


def encoder_scratch(width, genes, cells, head):
    half = cells // 2
    raw = [pltpu.VMEM((3 * head, 2, width), BF16), pltpu.VMEM((head, 2, width), BF16)]
    layer = [
        pltpu.VMEM((3, width, 256), BF16),
        pltpu.VMEM((256, width), BF16),
        pltpu.VMEM((NM, NCHIP, ROWS, width), BF16),
    ]
    return (
        [
            pltpu.VMEM((cells, genes), BF16),
            pltpu.VMEM((NM, genes, 1664), BF16),
            pltpu.VMEM((8, cells), F32),
            pltpu.VMEM((NG, 8, cells), F32),
            pltpu.VMEM((NM, NCHIP, 2, ROWS, width), BF16),
            pltpu.VMEM((NM, NCHIP, ROWS, width), BF16),
            pltpu.VMEM((128, width), F32),
            pltpu.VMEM((2, 3 * head, width), F32),
            pltpu.VMEM((NM, ROWS, width), F32),
            pltpu.VMEM((NM, ROWS, width), F32),
            pltpu.VMEM((NM, 2, 2, half, 256), BF16),
            pltpu.VMEM((NM, half, 256), BF16),
            pltpu.VMEM((cells, 128), F32),
            pltpu.SemaphoreType.DMA((NM + 4,)),
        ]
        + raw * 2
        + layer * 2
        + [pltpu.SemaphoreType.DMA((1, NG))] * 2
        + [pltpu.SemaphoreType.DMA((NM,))] * 2
        + [pltpu.SemaphoreType.DMA((NM,))] * 2
        + [pltpu.SemaphoreType.DMA((NM, NM))] * 2
        + [pltpu.SemaphoreType.DMA((2 * NM, Gather.SLOTS))] * 2
        + [pltpu.SemaphoreType.DMA((1, 16))] * 2
        + Scatter.scratch(width) * 2
        + [
            pltpu.VMEM((half, width), F32),
            pltpu.VMEM((NCHIP, ROWS, width), BF16),
            pltpu.VMEM((NCHIP, ROWS, width), BF16),
            pltpu.SemaphoreType.DMA((NCHIP,)),
            pltpu.SemaphoreType.DMA((NCHIP,)),
        ]
    )


def encode(head, meet, after, counts, groups, w_hbm, q1_hbm, q2_hbm, o1_hbm, o2_hbm, hidden, library, *refs):
    (scaled, w_proj, tile, slots, halves, pair, padded, split, tokens, resid, kv, queries, spot, load_sem) = refs[:14]
    raws, layers = refs[14:18], refs[18:24]
    (s_send, s_recv, w_send, w_recv, p_send, p_recv, k_send, k_recv, a_send, a_recv, d_send, d_recv) = refs[24:36]
    sums, (gathered, shares, share_in, z_send, z_recv) = refs[36:-5], refs[-5:]
    place = Place()
    width = resid.shape[-1]
    wide = w_proj.shape[-1]
    core, here = place.core, place.chip(place.y, place.x)
    scatter = [Scatter(place, sums[10 * k:10 * k + 10]) for k in range(2)]
    weights, outs, blocks = layers[0::3], layers[1::3], layers[2::3]

    small = [
        pltpu.make_async_copy(src, dst, load_sem.at[NM + k])
        for k, (src, dst) in enumerate(zip((q1_hbm, o1_hbm, q2_hbm, o2_hbm), raws))
    ]
    loads = [
        pltpu.make_async_copy(w_hbm.at[:, pl.ds((m * width) // 128 * 128, wide)], w_proj.at[m], load_sem.at[m])
        for m in range(NM)
    ]

    def first():
        for load in small[:2] + loads + small[2:]:
            load.start()

    def second():
        tile[...] = jnp.broadcast_to(jnp.sum(counts[...].astype(F32), axis=0, keepdims=True), tile.shape)

    meet(first, second)
    swap = Swap(place, lambda t: tile, slots, s_send, s_recv, 0)
    swap.start()
    slots[place.g] = tile[...]

    lanes = pl.ds(pl.multiple_of(core * 128, 128), 128)
    share = []
    for k in range(2):
        share.append([
            remote(weights[k].at[:, :, lanes], weights[k].at[:, :, lanes], w_send.at[2 * k], w_recv.at[2 * k], "gene", place.other_core),
            remote(outs[k].at[lanes, :], outs[k].at[lanes, :], w_send.at[2 * k + 1], w_recv.at[2 * k + 1], "gene", place.other_core),
        ])

    def prepare(k):
        padded[...] = jnp.zeros_like(padded)
        small[2 * k].wait()
        for h in range(2):
            split[h] = raws[2 * k][:, h, :].astype(F32)
        for a in range(3):
            for h in range(2):
                padded[64 * h:64 * h + head, :] = split[h, a * head:(a + 1) * head, :]
            weights[k][a, :, lanes] = padded[...].T.astype(BF16)
        share[k][0].start()
        small[2 * k + 1].wait()
        for h in range(2):
            padded[64 * h:64 * h + head, :] = raws[2 * k + 1][:, h, :].astype(F32)
        outs[k][lanes, :] = padded[...].astype(BF16)
        share[k][1].start()

    prepare(0)
    swap.finish()
    total = 1.0 + total_of(slots)
    library[...] = total
    scaled[...] = jnp.log1p(counts[...].astype(F32) * (TARGET / total[0:1])).T.astype(BF16)

    pairs = [
        remote(halves.at[m, :, 1 - core], pair.at[m], p_send.at[m], p_recv.at[m], "gene", place.other_core)
        for m in range(NM)
    ]

    def project(m):
        loads[m].wait()
        skip = (m * width) % 128
        out = jnp.dot(scaled[...], w_proj[m], preferred_element_type=F32)[:, skip:skip + width]
        halves[m] = out.astype(BF16).reshape(NCHIP, 2, ROWS, width)
        pairs[m].start()

    def join(m):
        pairs[m].wait_recv()
        for q in range(NCHIP):
            scatter[0].chip[m, q] = (halves[m, q, core].astype(F32) + pair[m, q].astype(F32)).astype(BF16)
        scatter[0].spread(m)

    def keep(m):
        scatter[0].mine[m] = scatter[0].take(m)

    run_pipeline([project, join, scatter[0].forward, scatter[0].cross, keep])

    gathers = [
        [
            GatherX(place, lambda q, k=k, m=m: blocks[k].at[m, q], a_send, a_recv, k * NM + m, m == 0)
            if m % 2 == 0
            else Gather(place, lambda q, k=k, m=m: blocks[k].at[m, q], a_send, a_recv, k * NM + m)
            for m in range(NM)
        ]
        for k in range(2)
    ]
    for s in range(NM):
        for m in range(NM):
            tokens[s, 4 * m:4 * m + 4, :] = scatter[0].mine[m, 4 * s:4 * s + 4, :]
        blocks[0][s, here] = rms(tokens[s]).astype(BF16)
        gathers[0][s].start()

    prepare(1)
    cells = 2 * kv.shape[3]
    at = lax.broadcasted_iota(jnp.int32, (cells, cells), 1)
    source = 32 * (lax.rem(at, 128) // ROWS) + ROWS * (at // 128) + lax.rem(at, ROWS)
    order = (lax.broadcasted_iota(jnp.int32, (cells, cells), 0) == source).astype(F32).astype(BF16)
    row = jnp.dot(
        jnp.broadcast_to(groups[...].astype(F32), (128, cells)).astype(BF16), order, preferred_element_type=F32
    )
    spot[...] = row.T
    same = jnp.broadcast_to(spot[lanes, 0:1], (128, cells)) == row
    for copy in share[0]:
        copy.wait_recv()

    def within(s):
        gathers[0][s].finish()
        rows = blocks[0][s].reshape(NCHIP * ROWS, width)
        mixed = within_mix(*heads_of(rows, weights[0], head), head)
        out = jnp.dot(mixed, outs[0][...], preferred_element_type=F32)
        scatter[1].chip[s] = out.astype(BF16).reshape(NCHIP, ROWS, width)
        scatter[1].spread(s)

    def add_within(s):
        tokens[s] = tokens[s] + scatter[1].take(s)

    run_pipeline([
        lambda s: gathers[0][s].second(), lambda s: gathers[0][s].third(), within,
        scatter[1].forward, scatter[1].cross, add_within,
    ])

    for m in range(NM):
        for s in range(NM):
            resid[m, 4 * s:4 * s + 4, :] = tokens[s, 4 * m:4 * m + 4, :]
        blocks[1][m, here] = rms(resid[m]).astype(BF16)
        gathers[1][m].start()
    for copy in share[1]:
        copy.wait_recv()
    trade = [
        remote(kv.at[m, core], kv.at[m, core], k_send.at[m, 0], k_recv.at[m, 0], "gene", place.other_core)
        for m in range(NM)
    ]

    def look(m):
        gathers[1][m].finish()
        rows = blocks[1][m].reshape(NCHIP * ROWS, width)
        queries[m], kv[m, core, 0], kv[m, core, 1] = heads_of(rows, weights[1], head)
        trade[m].start()

    def attend(m):
        trade[m].wait_recv()
        keys = jnp.concatenate([kv[m, 0, 0], kv[m, 1, 0]], axis=0)
        values = jnp.concatenate([kv[m, 0, 1], kv[m, 1, 1]], axis=0)
        mixed = cross_mix(queries[m], keys, values, same, head)
        out = jnp.dot(mixed, outs[1][...], preferred_element_type=F32)
        gathered[...] = gathered[...] + out if m else out

    run_pipeline([lambda m: gathers[1][m].second(), lambda m: gathers[1][m].third(), look, attend])

    shares[...] = gathered[...].astype(BF16).reshape(NCHIP, ROWS, width)
    final = DirectSum(place, shares, share_in, z_send, z_recv)
    final.start()
    pooled = (resid[0] + resid[1] + resid[2] + resid[3] + final.take()) * (1.0 / NM)
    hidden[pl.ds(pl.multiple_of(place.g * ROWS, ROWS), ROWS), :] = rms(pooled).astype(BF16)
    last = Direct(
        place, lambda o: hidden.at[pl.ds(pl.multiple_of(o * ROWS, ROWS), ROWS), :], d_send, d_recv, 0
    )
    last.start()
    after()
    last.finish()
    for one in scatter + gathers[0] + gathers[1] + [swap, final, last]:
        one.drain()
    for copy in share[0] + share[1] + pairs + trade:
        copy.wait_send()


class GroupGather:
    SLOTS = 7

    def __init__(self, r, block, send, recv, index):
        z, h = lax.rem(r, NZ), r // NZ
        up, down = lax.rem(z + 1, NZ), lax.rem(z + 3, NZ)
        k = 1 - h

        def at(a, b):
            return a * NZ + b

        def go(slot, owner, to):
            ref = block(owner)
            return remote(ref, ref, send.at[index, slot], recv.at[index, slot], "grp", to)

        self.c = [
            go(0, at(h, z), at(k, z)),
            go(1, at(h, z), at(h, up)),
            go(2, at(h, z), at(h, down)),
            go(3, at(k, z), at(h, up)),
            go(4, at(k, z), at(h, down)),
            go(5, at(h, down), at(h, up)),
            go(6, at(k, up), at(h, down)),
        ]

    def start(self):
        for k in (1, 2, 0):
            self.c[k].start()

    def second(self):
        c = self.c
        c[1].wait_recv()
        c[5].start()
        c[0].wait_recv()
        c[3].start()
        c[4].start()

    def third(self):
        self.c[4].wait_recv()
        self.c[6].start()

    def finish(self):
        for k in (2, 3, 5, 6):
            self.c[k].wait_recv()

    def drain(self):
        for copy in self.c:
            copy.wait_send()


class GroupDirect:
    def __init__(self, r, block, send, recv):
        self.out, self.into = [], []
        for k in range(1, NR):
            to, frm = lax.rem(r + k, NR), lax.rem(r + NR - k, NR)
            self.out.append(remote(block(r), block(r), send.at[k], recv.at[k], "grp", to))
            self.into.append(remote(block(r), block(frm), send.at[k], recv.at[k], "grp", frm))

    def start(self):
        for copy in self.out:
            copy.start()

    def finish(self):
        for copy in self.into:
            copy.wait_recv()

    def drain(self):
        for copy in self.out:
            copy.wait_send()


def log_factorials(count):
    return [math.log(math.factorial(k)) for k in range(count)]


def terms(x, theta, logit, rate_scale, norm_scale, most):
    tail = jnp.exp(-jnp.abs(logit))
    soft = jnp.maximum(logit, 0.0) + jnp.log1p(tail)
    sigmoid = jnp.where(logit >= 0, 1.0, tail) / (1.0 + tail)
    rate = rate_scale * soft
    product = jnp.ones_like(theta)
    slope = jnp.zeros_like(theta)
    log_factorial = jnp.zeros_like(theta)
    table = log_factorials(most + 1)
    for k in range(most):
        on = x > k
        term = theta + float(k)
        slope = jnp.where(on, slope * term + product, slope)
        product = jnp.where(on, product * term, product)
        if k:
            log_factorial = jnp.where(on, table[k + 1], log_factorial)
    total = theta + rate
    log_total = jnp.log(total)
    log_theta = jnp.log(theta)
    ratio = (theta + x) / total
    nll = -(
        jnp.log(product) - log_factorial
        + theta * (log_theta - log_total)
        + x * (jnp.log(rate) - log_total)
    )
    d_logit = (ratio - x / rate) * rate_scale * sigmoid * norm_scale
    d_theta = -(slope / product + log_theta + 1.0 - log_total - ratio)
    return nll, d_logit, d_theta


def network_kernel(
    head, genes_all, cells_all, panel_count, encoder_count,
    counts_hbm, groups, w_hbm, q1_hbm, q2_hbm, o1_hbm, o2_hbm, panel_row, w_mean_hbm, w_disp,
    cell_loss, gradient, disp_block, *refs,
):
    (
        counts, hidden, library, w_mean, tile, slots, back, piece, columns, field, panel_part, loss, panel_col, mean_sem,
        s_send, s_recv, h_send, h_recv, v_send, v_recv, f_send, f_recv, d_send, d_recv, o_send, o_recv,
    ) = refs[encoder_count:]
    place = Place()
    r = lax.axis_index("grp")
    genes, cells = counts.shape
    width = hidden.shape[1]
    share = width // NR
    parts = 4
    step = genes // parts
    norm_scale = cells_all ** (-0.5)
    rows = pl.ds(pl.multiple_of(place.g * ROWS, ROWS), ROWS)
    out, into = [], []
    for k in range(1, NR):
        to, frm = lax.rem(r + k, NR), lax.rem(r + NR - k, NR)
        out.append(remote(piece.at[to], columns.at[r, rows], h_send.at[k], h_recv.at[r], "grp", to))
        into.append(remote(piece.at[frm], columns.at[frm, rows], h_send.at[k], h_recv.at[frm], "grp", frm))
    load_mean = pltpu.make_async_copy(w_mean_hbm, w_mean, mean_sem.at[0])
    load_counts = pltpu.make_async_copy(counts_hbm, counts, mean_sem.at[1])

    def early():
        panel_col[...] = jnp.broadcast_to(panel_row[...].astype(F32), (128, genes)).T
        piece[...] = jnp.zeros_like(piece)
        panel_part[...] = jnp.zeros_like(panel_part)
        loss[...] = jnp.zeros_like(loss)

    def after():
        own = hidden[rows, :].astype(F32)
        for k in range(NR):
            piece[k, :, 0:share] = own[:, k * share:(k + 1) * share].astype(BF16)
        for copy in out:
            copy.start()
        columns[r, rows] = piece[r]

    def meet(start, finish):
        def meanwhile():
            load_counts.start()
            start()
            load_mean.start()
            early()
            load_counts.wait()
            finish()

        greet(everyone(place) + [("grp", lax.rem(r + k, NR)) for k in range(1, NR)], meanwhile)

    encode(
        head, meet, after, counts, groups, w_hbm, q1_hbm, q2_hbm, o1_hbm, o2_hbm, hidden, library, *refs[:encoder_count]
    )
    load_mean.wait()
    disp = lax.dot_general(w_disp[...], hidden[...], DN_T, preferred_element_type=F32)
    table = DISP_BASE + (jnp.maximum(disp, 0.0) + jnp.log1p(jnp.exp(-jnp.abs(disp))))
    high = table.astype(BF16)
    rest = table - high.astype(F32)
    middle = rest.astype(BF16)
    low = (rest - middle.astype(F32)).astype(BF16)
    tables = jnp.concatenate([high, middle, low], axis=0)
    rate_scale = library[0:1] / genes_all

    v_gather = WideGather(
        place, lambda o: columns.at[:, pl.ds(pl.multiple_of(o * ROWS, ROWS), ROWS), :], v_send, v_recv, 0
    )
    field_gather = []
    for p in range(parts):
        block = lambda o, p=p: field.at[o, pl.ds(p * step, step), :]
        field_gather.append(
            GroupGather(r, block, f_send, f_recv, p)
        )
    disp_gather = GroupDirect(r, lambda o: field.at[o, pl.ds(genes, panel_count), :], d_send, d_recv)
    spread = GroupDirect(r, lambda o: disp_block.at[o], o_send, o_recv)

    def decode(p):
        at = pl.ds(p * step, step)
        x = counts[at, :].astype(F32)
        logit = lax.dot_general(w_mean[at, :], hidden[...], DN_T, preferred_element_type=F32)
        lane = lax.broadcasted_iota(jnp.int32, (step, 3 * panel_count), 1)
        pick = (panel_col[at, 0:1] == lax.rem(lane, panel_count).astype(F32)).astype(F32).astype(BF16)
        theta = jnp.dot(pick, tables, preferred_element_type=F32)
        nll, d_logit, d_theta = terms(x, theta, logit, rate_scale, norm_scale, 12)
        field[r, at, :] = d_logit.astype(BF16)
        if p < parts - 1:
            field_gather[p].start()
        loss[...] += jnp.sum(nll, axis=0, keepdims=True)
        row = lax.broadcasted_iota(jnp.int32, (step, 128), 1)
        wanted = jnp.where(lax.rem(row, 8) < 4, (row // 8) * 4 + lax.rem(row, 8), -1)
        pick_t = (panel_col[at, :] == wanted.astype(F32)).astype(F32).astype(BF16)
        upper = d_theta.astype(BF16)
        lower = (d_theta - upper.astype(F32)).astype(BF16)
        panel_part[...] += lax.dot_general(pick_t, upper, DN_0, preferred_element_type=F32) + lax.dot_general(
            pick_t, lower, DN_0, preferred_element_type=F32
        )

    for copy in into:
        copy.wait_recv()
    v_gather.start()
    decode(0)
    v_gather.second()
    decode(1)
    field_gather[0].second()
    v_gather.third()
    decode(2)
    field_gather[1].second()
    field_gather[0].third()
    decode(3)

    row = lax.broadcasted_iota(jnp.int32, (128, cells), 0)
    both = jnp.where(lax.rem(row, 8) == 4, loss[...], panel_part[...])
    tile[...] = both.reshape(NG, 8, cells)
    first = Swap(place, lambda t: tile.at[t], slots, s_send, s_recv, 0)
    first.start()
    field_gather[3].start()
    slots[place.g] = tile[place.g]
    field_gather[2].second()
    field_gather[1].third()
    first.finish()
    summed = total_of(slots)
    back[place.g] = summed
    second = Swap(place, lambda t: back.at[place.g], back, s_send, s_recv, 1)
    second.start()
    cell_loss[...] = summed[4:5] / genes_all
    v_gather.finish()
    second.finish()
    d_panel = jnp.concatenate([back[k, 0:4] for k in range(NG)], axis=0)
    tail = jnp.exp(-jnp.abs(disp))
    d_disp = d_panel * (jnp.where(disp >= 0, 1.0, tail) / (1.0 + tail)) * norm_scale
    field[r, pl.ds(genes, panel_count), :] = d_disp.astype(BF16)
    disp_gather.start()
    field_gather[2].third()
    field_gather[3].second()

    def contract(at, size):
        total = jnp.zeros((size, columns.shape[2]), F32)
        for k in range(NR):
            total = total + jnp.dot(field[k, pl.ds(at, size), :], columns[k], preferred_element_type=F32)
        return total

    def gradient_of(p):
        field_gather[p].finish()
        gradient[pl.ds(p * step, step), :] = contract(p * step, step)

    gradient_of(0)
    gradient_of(1)
    disp_gather.finish()
    disp_block[r] = contract(genes, panel_count)
    spread.start()
    field_gather[3].third()
    gradient_of(2)
    gradient_of(3)
    spread.finish()
    for copy in out:
        copy.wait_send()
    for one in [v_gather, first, second, disp_gather, spread] + field_gather:
        one.drain()


def finish_kernel(gradient, disp_block, loss, cell_loss, grad_mean, grad_disp):
    share = grad_mean.shape[0]
    cell_loss[...] = loss[...]
    grad_mean[...] = gradient[...].T[0:share]
    for k in range(NR):
        grad_disp[:, k * share:(k + 1) * share] = disp_block[k, :, 0:share]


def hbm():
    return pl.BlockSpec(memory_space=pl.ANY)


def whole():
    return pl.BlockSpec(memory_space=pltpu.VMEM)


def params(number):
    return pltpu.CompilerParams(collective_id=number, has_side_effects=True, vmem_limit_bytes=LIMIT)


def shards(counts, panels, membership, w_proj, w_qkv_within, w_out_within, w_qkv_cross, w_out_cross, w_mean, w_disp):
    cells, genes = counts.shape
    width = w_qkv_within.shape[0]
    head = w_out_within.shape[1]
    genes_all = genes * NG
    cells_all = cells * NR
    panel_count = w_disp.shape[1]
    counts_t = counts.T
    swap_sems = [pltpu.SemaphoreType.DMA((2, NG))] * 2
    first_part = encoder_scratch(width, genes, cells, head)
    cell_loss, gradient, disp_block = pl.pallas_call(
        functools.partial(network_kernel, head, genes_all, cells_all, panel_count, len(first_part)),
        name="network",
        out_shape=(
            jax.ShapeDtypeStruct((1, cells), F32),
            jax.ShapeDtypeStruct((genes, 256), F32),
            jax.ShapeDtypeStruct((NR, panel_count, 256), F32),
        ),
        in_specs=[hbm(), whole()] + [hbm()] * 5 + [whole(), hbm(), whole()],
        out_specs=(whole(), whole(), whole()),
        scratch_shapes=first_part + [
            pltpu.VMEM((genes, cells), jnp.int32),
            pltpu.VMEM((cells, width), BF16),
            pltpu.VMEM((8, cells), F32),
            pltpu.VMEM((genes, width), BF16),
            pltpu.VMEM((NG, 8, cells), F32),
            pltpu.VMEM((NG, 8, cells), F32),
            pltpu.VMEM((NG, 8, cells), F32),
            pltpu.VMEM((NR, ROWS, 256), BF16),
            pltpu.VMEM((NR, cells, 256), BF16),
            pltpu.VMEM((NR, genes + panel_count, cells), BF16),
            pltpu.VMEM((128, cells), F32),
            pltpu.VMEM((1, cells), F32),
            pltpu.VMEM((genes, 128), F32),
            pltpu.SemaphoreType.DMA((2,)),
        ] + swap_sems + [
            pltpu.SemaphoreType.DMA((NR,)),
            pltpu.SemaphoreType.DMA((NR,)),
            pltpu.SemaphoreType.DMA((1, WideGather.SLOTS)),
            pltpu.SemaphoreType.DMA((1, WideGather.SLOTS)),
            pltpu.SemaphoreType.DMA((4, GroupGather.SLOTS)),
            pltpu.SemaphoreType.DMA((4, GroupGather.SLOTS)),
            pltpu.SemaphoreType.DMA((NR,)),
            pltpu.SemaphoreType.DMA((NR,)),
            pltpu.SemaphoreType.DMA((NR,)),
            pltpu.SemaphoreType.DMA((NR,)),
        ],
        compiler_params=params(0),
    )(
        counts_t, membership, w_proj, jnp.transpose(w_qkv_within, (2, 1, 0)), jnp.transpose(w_qkv_cross, (2, 1, 0)),
        jnp.transpose(w_out_within, (1, 0, 2)), jnp.transpose(w_out_cross, (1, 0, 2)),
        panels[None, :], w_mean.T, w_disp.T,
    )
    cell_loss, grad_mean, grad_disp = pl.pallas_call(
        finish_kernel,
        name="finish",
        out_shape=(
            jax.ShapeDtypeStruct((1, cells), F32),
            jax.ShapeDtypeStruct((width // NR, genes), F32),
            jax.ShapeDtypeStruct((panel_count, width), F32),
        ),
        in_specs=[whole()] * 3,
        out_specs=(whole(), whole(), whole()),
    )(gradient, disp_block, cell_loss)
    return cell_loss[0], grad_mean, grad_disp.T


def solution(mesh):
    return jax.shard_map(
        shards,
        mesh=mesh,
        in_specs=(
            P("grp", "gene"),
            P("gene"),
            P("grp", None),
            P("gene", None),
            P(None, "gene", None),
            P("gene", None, None),
            P(None, "gene", None),
            P("gene", None, None),
            P(None, "gene"),
            P(),
        ),
        out_specs=(P("grp"), P("grp", "gene"), P()),
        check_vma=False,
    )
```

```python
import functools
import math

import jax
import jax.numpy as jnp
from jax import lax
from jax.experimental import pallas as pl
from jax.experimental.pallas import tpu as pltpu
from jax.sharding import PartitionSpec as P

EPS = 1e-06
FLOOR = 0.3
TARGET = 10000.0
DISP_BASE = 0.5
MESH = pl.DeviceIdType.MESH
F32 = jnp.float32
BF16 = jnp.bfloat16

NX = 4
NY = 2
NG = 16
NCHIP = 8
NR = 8
NZ = 4
NM = 4
ROWS = 16
LIMIT = 64 * 1024 * 1024 - 256 * 1024
DN_T = (((1,), (1,)), ((), ()))
DN_0 = (((0,), (0,)), ((), ()))


def remote(src, dst, send, recv, axis, to):
    return pltpu.make_async_remote_copy(
        src_ref=src, dst_ref=dst, send_sem=send, recv_sem=recv, device_id={axis: to}, device_id_type=MESH
    )


class Place:
    def __init__(self):
        self.g = lax.axis_index("gene")
        self.core = lax.rem(self.g, 2)
        self.x = lax.rem(self.g // 2, NX)
        self.y = self.g // (2 * NX)
        self.right = self.at(self.y, self.shift(1), self.core)
        self.left = self.at(self.y, self.shift(3), self.core)
        self.other_y = self.at(1 - self.y, self.x, self.core)
        self.other_core = self.at(self.y, self.x, 1 - self.core)

    def shift(self, by):
        return lax.rem(self.x + by, NX)

    def at(self, y, x, core):
        return (y * NX + x) * 2 + core

    def chip(self, y, x):
        return y * NX + x


def greet(axis_peers, meanwhile):
    barrier = pltpu.get_barrier_semaphore()
    for axis, to in axis_peers:
        pl.semaphore_signal(barrier, inc=1, device_id={axis: to}, device_id_type=MESH)
    meanwhile()
    pl.semaphore_wait(barrier, len(axis_peers))


def everyone(place):
    return [("gene", lax.rem(place.g + k, NG)) for k in range(1, NG)]


def rms(values):
    return values * lax.rsqrt(jnp.mean(values * values, axis=-1, keepdims=True) + EPS)


class Scatter:
    @staticmethod
    def scratch(width):
        return [
            pltpu.VMEM((NM, NCHIP, ROWS, width), BF16),
            pltpu.VMEM((NM, 3, ROWS, width), BF16),
            pltpu.VMEM((NM, 3, ROWS, width), BF16),
            pltpu.VMEM((NM, 2, ROWS, width), BF16),
            pltpu.VMEM((NM, ROWS, width), BF16),
            pltpu.VMEM((NM, ROWS, width), BF16),
            pltpu.VMEM((NM, ROWS, width), F32),
            pltpu.VMEM((2, NX, ROWS, width), BF16),
            pltpu.SemaphoreType.DMA((NM, 7)),
            pltpu.SemaphoreType.DMA((NM, 7)),
        ]

    def __init__(self, place, refs):
        (self.chip, self.from_left, self.from_right, self.relay, self.y_out, self.y_in, self.mine, four, send, recv) = refs
        self.send, self.recv = send, recv
        p = self.place = place
        ahead, behind, across = p.shift(1), p.shift(3), p.shift(2)
        self.copies, self.turned = [], {}
        for m in range(NM):
            if m % 2 == 0:
                self.turned[m] = ScatterY(self, m, four.at[m // 2], 1 if m == 0 else -1)
                self.copies.append(self.turned[m].c)
                continue

            def go(slot, src, dst, to):
                return remote(src, dst, send.at[m, slot], recv.at[m, slot], "gene", to)
            self.copies.append([
                go(0, self.chip.at[m, p.chip(0, across)], self.from_left.at[m, 0], p.right),
                go(1, self.chip.at[m, p.chip(1, across)], self.from_right.at[m, 0], p.left),
                go(2, self.chip.at[m, p.chip(1, ahead)], self.from_left.at[m, 2], p.right),
                go(3, self.chip.at[m, p.chip(0, behind)], self.from_right.at[m, 2], p.left),
                go(4, self.relay.at[m, 0], self.from_left.at[m, 1], p.right),
                go(5, self.relay.at[m, 1], self.from_right.at[m, 1], p.left),
                go(6, self.y_out.at[m], self.y_in.at[m], p.other_y),
            ])

    def spread(self, m):
        if m in self.turned:
            return self.turned[m].spread()
        for k in (0, 1, 2, 3):
            self.copies[m][k].start()

    def forward(self, m):
        if m in self.turned:
            return self.turned[m].forward()
        p = self.place
        self.copies[m][0].wait_recv()
        self.relay[m, 0] = (
            self.chip[m, p.chip(0, p.shift(1))].astype(F32) + self.from_left[m, 0].astype(F32)
        ).astype(BF16)
        self.copies[m][4].start()
        self.copies[m][1].wait_recv()
        self.relay[m, 1] = (
            self.chip[m, p.chip(1, p.shift(3))].astype(F32) + self.from_right[m, 0].astype(F32)
        ).astype(BF16)
        self.copies[m][5].start()

    def cross(self, m):
        if m in self.turned:
            return self.turned[m].cross()
        p = self.place
        for k in (2, 3, 4, 5):
            self.copies[m][k].wait_recv()
        self.y_out[m] = (
            self.chip[m, p.chip(1 - p.y, p.x)].astype(F32)
            + self.from_left[m, 2 - p.y].astype(F32)
            + self.from_right[m, 1 + p.y].astype(F32)
        ).astype(BF16)
        self.copies[m][6].start()
        self.mine[m] = (
            self.chip[m, p.chip(p.y, p.x)].astype(F32)
            + self.from_left[m, 1 + p.y].astype(F32)
            + self.from_right[m, 2 - p.y].astype(F32)
        )

    def take(self, m):
        if m in self.turned:
            return self.turned[m].take()
        self.copies[m][6].wait_recv()
        return self.mine[m] + self.y_in[m].astype(F32)

    def drain(self):
        for row in self.copies:
            for copy in row:
                copy.wait_send()


class ScatterY:
    def __init__(self, base, m, y_four, way):
        p = base.place
        self.base, self.m, self.four = base, m, y_four
        to, back = (p.right, p.left) if way > 0 else (p.left, p.right)
        ahead, behind = (p.shift(1), p.shift(3)) if way > 0 else (p.shift(3), p.shift(1))
        self.order = (p.shift(2), behind, ahead)
        self.outgoing = (base.relay.at[m, 0], base.relay.at[m, 1], base.y_out.at[m])
        self.incoming = (base.from_left.at[m, 0], base.from_right.at[m, 0], base.from_left.at[m, 1])

        def go(slot, src, dst, device):
            return remote(src, dst, base.send.at[m, slot], base.recv.at[m, slot], "gene", device)

        self.c = [
            go(k, base.chip.at[m, p.chip(1 - p.y, x)], y_four.at[x], p.other_y)
            for k, x in enumerate(self.order + (p.x,))
        ] + [go(4 + k, self.outgoing[k], self.incoming[k], (to, back, to)[k]) for k in range(3)]

    def spread(self):
        for k in range(4):
            self.c[k].start()

    def total(self, k):
        p = self.base.place
        x = p.x if k == 3 else self.order[k]
        self.c[k].wait_recv()
        return self.base.chip[self.m, p.chip(p.y, x)].astype(F32) + self.four[x].astype(F32)

    def forward(self):
        for k in (0, 1):
            self.outgoing[k][...] = self.total(k).astype(BF16)
            self.c[4 + k].start()

    def cross(self):
        value = self.total(2)
        self.c[4].wait_recv()
        self.outgoing[2][...] = (value + self.incoming[0][...].astype(F32)).astype(BF16)
        self.c[6].start()
        self.base.mine[self.m] = self.total(3)

    def take(self):
        self.c[5].wait_recv()
        self.c[6].wait_recv()
        return self.base.mine[self.m] + self.incoming[1][...].astype(F32) + self.incoming[2][...].astype(F32)


def run_pipeline(steps, count=NM):
    for t in range(count + len(steps) - 1):
        for lag, step in enumerate(steps):
            if 0 <= t - lag < count:
                step(t - lag)


class Gather:
    SLOTS = 7

    def __init__(self, place, block, send, recv, index):
        p = place
        ahead, behind, across = p.shift(1), p.shift(3), p.shift(2)
        y, z, x = p.y, 1 - p.y, p.x

        def go(slot, owner, to):
            ref = block(owner)
            return remote(ref, ref, send.at[index, slot], recv.at[index, slot], "gene", to)

        own, paired = p.chip(y, x), p.chip(z, x)
        self.c = [
            go(0, own, p.other_y),
            go(1, own, p.right),
            go(2, own, p.left),
            go(3, paired, p.right),
            go(4, paired, p.left),
            go(5, p.chip(y, behind), p.right),
            go(6, p.chip(z, ahead), p.left),
        ]

    def start(self):
        for k in (1, 2, 0):
            self.c[k].start()

    def second(self):
        c = self.c
        c[1].wait_recv()
        c[5].start()
        c[0].wait_recv()
        c[3].start()
        c[4].start()

    def third(self):
        self.c[4].wait_recv()
        self.c[6].start()

    def finish(self):
        for k in (2, 3, 5, 6):
            self.c[k].wait_recv()

    def drain(self):
        for copy in self.c:
            copy.wait_send()


class GatherX:
    def __init__(self, place, block, send, recv, index, rightward):
        p = place
        ahead, behind, across = p.shift(1), p.shift(3), p.shift(2)
        y, x = p.y, p.x
        self.rightward = rightward

        def go(slot, owner, to):
            ref = block(owner)
            return remote(ref, ref, send.at[index, slot], recv.at[index, slot], "gene", to)

        self.c = [
            go(0, p.chip(y, x), p.right),
            go(1, p.chip(y, x), p.left),
            go(2, p.chip(y, behind), p.right) if rightward else go(2, p.chip(y, ahead), p.left),
            go(3, p.chip(y, x), p.other_y),
            go(4, p.chip(y, behind), p.other_y),
            go(5, p.chip(y, ahead), p.other_y),
            go(6, p.chip(y, across), p.other_y),
        ]

    def start(self):
        for k in (0, 1, 3):
            self.c[k].start()

    def second(self):
        c = self.c
        for k in (0, 1):
            c[k].wait_recv()
            if self.rightward == (k == 0):
                c[2].start()
            c[4 + k].start()

    def third(self):
        self.c[2].wait_recv()
        self.c[6].start()

    def finish(self):
        for k in (3, 4, 5, 6):
            self.c[k].wait_recv()

    def drain(self):
        for copy in self.c:
            copy.wait_send()


def lead(gathers):
    for one in gathers:
        one.second()
    for one in gathers[:2]:
        one.third()


class WideGather:
    SLOTS = 15

    def __init__(self, place, block, send, recv, index):
        p = place
        core, x, y, z = p.core, p.x, p.y, 1 - p.y
        ahead, behind, across = p.shift(1), p.shift(3), p.shift(2)
        self.far = Gather(place, lambda q: block(2 * q + core), send, recv, index)
        held = [p.chip(y, x), p.chip(z, x), p.chip(y, behind), p.chip(y, ahead), p.chip(z, behind), p.chip(z, ahead),
                p.chip(y, across), p.chip(z, across)]
        self.near = []
        for k, q in enumerate(held):
            ref = block(2 * q + core)
            self.near.append(remote(ref, ref, send.at[index, 7 + k], recv.at[index, 7 + k], "gene", p.other_core))

    def start(self):
        self.far.start()
        self.near[0].start()

    def second(self):
        self.far.second()
        self.near[1].start()
        self.near[2].start()

    def third(self):
        self.far.third()
        self.near[5].start()

    def finish(self):
        self.far.finish()
        for k in (3, 4, 6, 7):
            self.near[k].start()
        for copy in self.near:
            copy.wait_recv()

    def drain(self):
        self.far.drain()
        for copy in self.near:
            copy.wait_send()


class DirectSum:
    def __init__(self, place, shares, slots, send, recv):
        p = place
        self.shares, self.slots = shares, slots
        self.chip = p.chip(p.y, p.x)
        self.c = []
        for k in range(1, NCHIP):
            to = lax.rem(self.chip + k, NCHIP)
            self.c.append(remote(shares.at[to], slots.at[k], send.at[k], recv.at[k], "gene", to * 2 + p.core))

    def start(self):
        for copy in self.c:
            copy.start()

    def take(self):
        total = self.shares[self.chip].astype(F32)
        for k in range(1, NCHIP):
            self.c[k - 1].wait_recv()
            total = total + self.slots[k].astype(F32)
        return total

    def drain(self):
        for copy in self.c:
            copy.wait_send()


class Direct:
    def __init__(self, place, block, send, recv, index):
        p = place
        chip = p.chip(p.y, p.x)
        own = block(p.g)
        self.out, self.pair = [], []
        for k in range(NCHIP):
            to, frm = lax.rem(chip + k, NCHIP) * 2 + p.core, lax.rem(chip + NCHIP - k, NCHIP) * 2 + p.core
            ref = block(frm)
            if k:
                self.out.append(remote(own, own, send.at[index, k], recv.at[index, k], "gene", to))
            self.pair.append(remote(ref, ref, send.at[index, 7 + k if k else 0], recv.at[index, 7 + k if k else 0], "gene", p.other_core))

    def start(self):
        for copy in self.out + self.pair[:1]:
            copy.start()

    def finish(self):
        for k in range(1, NCHIP):
            self.out[k - 1].wait_recv()
            self.pair[k].start()
        for copy in self.pair:
            copy.wait_recv()

    def drain(self):
        for copy in self.out + self.pair:
            copy.wait_send()


class Swap:
    def __init__(self, place, source, slots, send, recv, index):
        self.out, self.into = [], []
        for k in range(1, NG):
            to, frm = lax.rem(place.g + k, NG), lax.rem(place.g + NG - k, NG)
            self.out.append(remote(source(to), slots.at[place.g], send.at[index, k], recv.at[index, place.g], "gene", to))
            self.into.append(remote(source(frm), slots.at[frm], send.at[index, k], recv.at[index, frm], "gene", frm))

    def start(self):
        for copy in self.out:
            copy.start()

    def finish(self):
        for copy in self.into:
            copy.wait_recv()

    def drain(self):
        for copy in self.out:
            copy.wait_send()


def total_of(slots):
    total = slots[0]
    for k in range(1, NG):
        total = total + slots[k]
    return total


def group_sum(values):
    high = values.astype(BF16)
    low = (values - high.astype(F32)).astype(BF16)
    shape = (values.shape[1], values.shape[1])
    row = lax.broadcasted_iota(jnp.int32, shape, 0) // 64
    col = lax.broadcasted_iota(jnp.int32, shape, 1) // 64
    ones = (row == col).astype(F32).astype(BF16)
    return jnp.dot(high, ones, preferred_element_type=F32) + jnp.dot(low, ones, preferred_element_type=F32)


def heads_of(rows, weights, head):
    parts = [jnp.dot(rows, weights[k], preferred_element_type=F32) for k in range(3)]
    for k in range(2):
        mean = group_sum(parts[k] * parts[k]) / head
        parts[k] = (parts[k] * lax.rsqrt(jnp.maximum(mean, FLOOR))).astype(BF16)
    parts[2] = parts[2].astype(BF16)
    return parts


def turned(values, by):
    if by == 0:
        return values
    row = lax.rem(lax.broadcasted_iota(jnp.int32, values.shape, 0), ROWS)
    count = values.shape[0]
    return jnp.where(row < by, pltpu.roll(values, count - ROWS + by, 0), pltpu.roll(values, by, 0))


def within_mix(query, keys, values, head):
    q, k, v = (part.astype(F32) for part in (query, keys, values))
    count = q.shape[0]
    scores = group_sum(jnp.concatenate([q * turned(k, 4 * d) for d in range(NM)], axis=0))
    weights = [jnp.exp(scores[d * count:(d + 1) * count] * head ** (-0.5)) for d in range(NM)]
    total = weights[0] + weights[1] + weights[2] + weights[3]
    mixed = None
    for d in range(NM):
        term = (weights[d] / total).astype(BF16).astype(F32) * turned(v, 4 * d)
        mixed = term if mixed is None else mixed + term
    return mixed.astype(BF16)


def cross_mix(query, keys, values, same, head):
    lane = lax.broadcasted_iota(jnp.int32, query.shape, 1) // 64
    q = query.astype(F32)
    mixed = jnp.zeros(query.shape, F32)
    for h in range(query.shape[1] // 64):
        one = jnp.where(lane == h, q, 0.0).astype(BF16)
        scores = lax.dot_general(one, keys, DN_T, preferred_element_type=F32) * head ** (-0.5)
        weights = jnp.where(same, jnp.exp(scores), 0.0)
        probs = (weights / jnp.sum(weights, axis=-1, keepdims=True)).astype(BF16)
        mixed = jnp.where(lane == h, jnp.dot(probs, values, preferred_element_type=F32), mixed)
    return mixed.astype(BF16)


def encoder_scratch(width, genes, cells, head):
    half = cells // 2
    raw = [pltpu.VMEM((3 * head, 2, width), BF16), pltpu.VMEM((head, 2, width), BF16)]
    layer = [
        pltpu.VMEM((3, width, 256), BF16),
        pltpu.VMEM((256, width), BF16),
        pltpu.VMEM((NM, NCHIP, ROWS, width), BF16),
    ]
    return (
        [
            pltpu.VMEM((cells, genes), BF16),
            pltpu.VMEM((NM, genes, 1664), BF16),
            pltpu.VMEM((8, cells), F32),
            pltpu.VMEM((NG, 8, cells), F32),
            pltpu.VMEM((NM, NCHIP, 2, ROWS, width), BF16),
            pltpu.VMEM((NM, NCHIP, ROWS, width), BF16),
            pltpu.VMEM((128, width), F32),
            pltpu.VMEM((2, 3 * head, width), F32),
            pltpu.VMEM((NM, ROWS, width), F32),
            pltpu.VMEM((NM, ROWS, width), F32),
            pltpu.VMEM((NM, 2, 2, half, 256), BF16),
            pltpu.VMEM((NM, half, 256), BF16),
            pltpu.VMEM((cells, 128), F32),
            pltpu.SemaphoreType.DMA((NM + 4,)),
        ]
        + raw * 2
        + layer * 2
        + [pltpu.SemaphoreType.DMA((1, NG))] * 2
        + [pltpu.SemaphoreType.DMA((NM,))] * 2
        + [pltpu.SemaphoreType.DMA((NM,))] * 2
        + [pltpu.SemaphoreType.DMA((NM, NM))] * 2
        + [pltpu.SemaphoreType.DMA((2 * NM, Gather.SLOTS))] * 2
        + [pltpu.SemaphoreType.DMA((1, 16))] * 2
        + Scatter.scratch(width) * 2
        + [
            pltpu.VMEM((half, width), F32),
            pltpu.VMEM((NCHIP, ROWS, width), BF16),
            pltpu.VMEM((NCHIP, ROWS, width), BF16),
            pltpu.SemaphoreType.DMA((NCHIP,)),
            pltpu.SemaphoreType.DMA((NCHIP,)),
        ]
    )


def encode(head, meet, after, counts, groups, w_hbm, q1_hbm, q2_hbm, o1_hbm, o2_hbm, hidden, library, *refs):
    (scaled, w_proj, tile, slots, halves, pair, padded, split, tokens, resid, kv, queries, spot, load_sem) = refs[:14]
    raws, layers = refs[14:18], refs[18:24]
    (s_send, s_recv, w_send, w_recv, p_send, p_recv, k_send, k_recv, a_send, a_recv, d_send, d_recv) = refs[24:36]
    sums, (gathered, shares, share_in, z_send, z_recv) = refs[36:-5], refs[-5:]
    place = Place()
    width = resid.shape[-1]
    wide = w_proj.shape[-1]
    core, here = place.core, place.chip(place.y, place.x)
    scatter = [Scatter(place, sums[10 * k:10 * k + 10]) for k in range(2)]
    weights, outs, blocks = layers[0::3], layers[1::3], layers[2::3]

    small = [
        pltpu.make_async_copy(src, dst, load_sem.at[NM + k])
        for k, (src, dst) in enumerate(zip((q1_hbm, o1_hbm, q2_hbm, o2_hbm), raws))
    ]
    loads = [
        pltpu.make_async_copy(w_hbm.at[:, pl.ds((m * width) // 128 * 128, wide)], w_proj.at[m], load_sem.at[m])
        for m in range(NM)
    ]

    def first():
        for load in small[:2] + loads + small[2:]:
            load.start()

    def second():
        tile[...] = jnp.broadcast_to(jnp.sum(counts[...].astype(F32), axis=0, keepdims=True), tile.shape)

    meet(first, second)
    swap = Swap(place, lambda t: tile, slots, s_send, s_recv, 0)
    swap.start()
    slots[place.g] = tile[...]

    lanes = pl.ds(pl.multiple_of(core * 128, 128), 128)
    share = []
    for k in range(2):
        share.append([
            remote(weights[k].at[:, :, lanes], weights[k].at[:, :, lanes], w_send.at[2 * k], w_recv.at[2 * k], "gene", place.other_core),
            remote(outs[k].at[lanes, :], outs[k].at[lanes, :], w_send.at[2 * k + 1], w_recv.at[2 * k + 1], "gene", place.other_core),
        ])

    def prepare(k):
        padded[...] = jnp.zeros_like(padded)
        small[2 * k].wait()
        for h in range(2):
            split[h] = raws[2 * k][:, h, :].astype(F32)
        for a in range(3):
            for h in range(2):
                padded[64 * h:64 * h + head, :] = split[h, a * head:(a + 1) * head, :]
            weights[k][a, :, lanes] = padded[...].T.astype(BF16)
        share[k][0].start()
        small[2 * k + 1].wait()
        for h in range(2):
            padded[64 * h:64 * h + head, :] = raws[2 * k + 1][:, h, :].astype(F32)
        outs[k][lanes, :] = padded[...].astype(BF16)
        share[k][1].start()

    prepare(0)
    swap.finish()
    total = 1.0 + total_of(slots)
    library[...] = total
    scaled[...] = jnp.log1p(counts[...].astype(F32) * (TARGET / total[0:1])).T.astype(BF16)

    pairs = [
        remote(halves.at[m, :, 1 - core], pair.at[m], p_send.at[m], p_recv.at[m], "gene", place.other_core)
        for m in range(NM)
    ]

    def project(m):
        loads[m].wait()
        skip = (m * width) % 128
        out = jnp.dot(scaled[...], w_proj[m], preferred_element_type=F32)[:, skip:skip + width]
        halves[m] = out.astype(BF16).reshape(NCHIP, 2, ROWS, width)
        pairs[m].start()

    def join(m):
        pairs[m].wait_recv()
        for q in range(NCHIP):
            scatter[0].chip[m, q] = (halves[m, q, core].astype(F32) + pair[m, q].astype(F32)).astype(BF16)
        scatter[0].spread(m)

    def keep(m):
        scatter[0].mine[m] = scatter[0].take(m)

    run_pipeline([project, join, scatter[0].forward, scatter[0].cross, keep])

    gathers = [
        [
            GatherX(place, lambda q, k=k, m=m: blocks[k].at[m, q], a_send, a_recv, k * NM + m, m == 0)
            if m % 2 == 0
            else Gather(place, lambda q, k=k, m=m: blocks[k].at[m, q], a_send, a_recv, k * NM + m)
            for m in range(NM)
        ]
        for k in range(2)
    ]
    for s in range(NM):
        for m in range(NM):
            tokens[s, 4 * m:4 * m + 4, :] = scatter[0].mine[m, 4 * s:4 * s + 4, :]
        blocks[0][s, here] = rms(tokens[s]).astype(BF16)
        gathers[0][s].start()

    prepare(1)
    cells = 2 * kv.shape[3]
    at = lax.broadcasted_iota(jnp.int32, (cells, cells), 1)
    source = 32 * (lax.rem(at, 128) // ROWS) + ROWS * (at // 128) + lax.rem(at, ROWS)
    order = (lax.broadcasted_iota(jnp.int32, (cells, cells), 0) == source).astype(F32).astype(BF16)
    row = jnp.dot(
        jnp.broadcast_to(groups[...].astype(F32), (128, cells)).astype(BF16), order, preferred_element_type=F32
    )
    spot[...] = row.T
    same = jnp.broadcast_to(spot[lanes, 0:1], (128, cells)) == row
    for copy in share[0]:
        copy.wait_recv()

    lead(gathers[0])

    def within(s):
        gathers[0][s].finish()
        if s + 2 < NM:
            gathers[0][s + 2].third()
        rows = blocks[0][s].reshape(NCHIP * ROWS, width)
        mixed = within_mix(*heads_of(rows, weights[0], head), head)
        out = jnp.dot(mixed, outs[0][...], preferred_element_type=F32)
        scatter[1].chip[s] = out.astype(BF16).reshape(NCHIP, ROWS, width)
        scatter[1].spread(s)

    def add_within(s):
        tokens[s] = tokens[s] + scatter[1].take(s)

    run_pipeline([within, scatter[1].forward, scatter[1].cross, add_within])

    for m in range(NM):
        for s in range(NM):
            resid[m, 4 * s:4 * s + 4, :] = tokens[s, 4 * m:4 * m + 4, :]
        blocks[1][m, here] = rms(resid[m]).astype(BF16)
        gathers[1][m].start()
    for copy in share[1]:
        copy.wait_recv()
    trade = [
        remote(kv.at[m, core], kv.at[m, core], k_send.at[m, 0], k_recv.at[m, 0], "gene", place.other_core)
        for m in range(NM)
    ]

    lead(gathers[1])

    def look(m):
        if m + 2 < NM:
            gathers[1][m + 2].third()
        gathers[1][m].finish()
        rows = blocks[1][m].reshape(NCHIP * ROWS, width)
        queries[m], kv[m, core, 0], kv[m, core, 1] = heads_of(rows, weights[1], head)
        trade[m].start()

    def attend(m):
        trade[m].wait_recv()
        keys = jnp.concatenate([kv[m, 0, 0], kv[m, 1, 0]], axis=0)
        values = jnp.concatenate([kv[m, 0, 1], kv[m, 1, 1]], axis=0)
        mixed = cross_mix(queries[m], keys, values, same, head)
        out = jnp.dot(mixed, outs[1][...], preferred_element_type=F32)
        gathered[...] = gathered[...] + out if m else out

    run_pipeline([look, attend])

    shares[...] = gathered[...].astype(BF16).reshape(NCHIP, ROWS, width)
    final = DirectSum(place, shares, share_in, z_send, z_recv)
    final.start()
    pooled = (resid[0] + resid[1] + resid[2] + resid[3] + final.take()) * (1.0 / NM)
    hidden[pl.ds(pl.multiple_of(place.g * ROWS, ROWS), ROWS), :] = rms(pooled).astype(BF16)
    last = Direct(
        place, lambda o: hidden.at[pl.ds(pl.multiple_of(o * ROWS, ROWS), ROWS), :], d_send, d_recv, 0
    )
    last.start()
    after()
    last.finish()
    for one in scatter + gathers[0] + gathers[1] + [swap, final, last]:
        one.drain()
    for copy in share[0] + share[1] + pairs + trade:
        copy.wait_send()


class GroupGather:
    SLOTS = 7

    def __init__(self, r, block, send, recv, index):
        z, h = lax.rem(r, NZ), r // NZ
        up, down = lax.rem(z + 1, NZ), lax.rem(z + 3, NZ)
        k = 1 - h

        def at(a, b):
            return a * NZ + b

        def go(slot, owner, to):
            ref = block(owner)
            return remote(ref, ref, send.at[index, slot], recv.at[index, slot], "grp", to)

        self.c = [
            go(0, at(h, z), at(k, z)),
            go(1, at(h, z), at(h, up)),
            go(2, at(h, z), at(h, down)),
            go(3, at(k, z), at(h, up)),
            go(4, at(k, z), at(h, down)),
            go(5, at(h, down), at(h, up)),
            go(6, at(k, up), at(h, down)),
        ]

    def start(self):
        for k in (1, 2, 0):
            self.c[k].start()

    def second(self):
        c = self.c
        c[1].wait_recv()
        c[5].start()
        c[0].wait_recv()
        c[3].start()
        c[4].start()

    def third(self):
        self.c[4].wait_recv()
        self.c[6].start()

    def finish(self):
        for k in (2, 3, 5, 6):
            self.c[k].wait_recv()

    def drain(self):
        for copy in self.c:
            copy.wait_send()


class GroupGatherZ:
    def __init__(self, r, block, send, recv, index, upward):
        z, h = lax.rem(r, NZ), r // NZ
        up, down, across = lax.rem(z + 1, NZ), lax.rem(z + 3, NZ), lax.rem(z + 2, NZ)
        k = 1 - h
        self.upward = upward

        def at(a, b):
            return a * NZ + b

        def go(slot, owner, to):
            ref = block(owner)
            return remote(ref, ref, send.at[index, slot], recv.at[index, slot], "grp", to)

        self.c = [
            go(0, at(h, z), at(h, up)),
            go(1, at(h, z), at(h, down)),
            go(2, at(h, down), at(h, up)) if upward else go(2, at(h, up), at(h, down)),
            go(3, at(h, z), at(k, z)),
            go(4, at(h, down), at(k, z)),
            go(5, at(h, up), at(k, z)),
            go(6, at(h, across), at(k, z)),
        ]

    def start(self):
        for k in (0, 1, 3):
            self.c[k].start()

    def second(self):
        c = self.c
        for k in (0, 1):
            c[k].wait_recv()
            if self.upward == (k == 0):
                c[2].start()
            c[4 + k].start()

    def third(self):
        self.c[2].wait_recv()
        self.c[6].start()

    def finish(self):
        for k in (3, 4, 5, 6):
            self.c[k].wait_recv()

    def drain(self):
        for copy in self.c:
            copy.wait_send()


class GroupDirect:
    def __init__(self, r, block, send, recv):
        self.out, self.into = [], []
        for k in range(1, NR):
            to, frm = lax.rem(r + k, NR), lax.rem(r + NR - k, NR)
            self.out.append(remote(block(r), block(r), send.at[k], recv.at[k], "grp", to))
            self.into.append(remote(block(r), block(frm), send.at[k], recv.at[k], "grp", frm))

    def start(self):
        for copy in self.out:
            copy.start()

    def finish(self):
        for copy in self.into:
            copy.wait_recv()

    def drain(self):
        for copy in self.out:
            copy.wait_send()


def log_factorials(count):
    return [math.log(math.factorial(k)) for k in range(count)]


def terms(x, theta, logit, rate_scale, norm_scale, most):
    tail = jnp.exp(-jnp.abs(logit))
    soft = jnp.maximum(logit, 0.0) + jnp.log1p(tail)
    sigmoid = jnp.where(logit >= 0, 1.0, tail) / (1.0 + tail)
    rate = rate_scale * soft
    product = jnp.ones_like(theta)
    slope = jnp.zeros_like(theta)
    log_factorial = jnp.zeros_like(theta)
    table = log_factorials(most + 1)
    for k in range(most):
        on = x > k
        term = theta + float(k)
        slope = jnp.where(on, slope * term + product, slope)
        product = jnp.where(on, product * term, product)
        if k:
            log_factorial = jnp.where(on, table[k + 1], log_factorial)
    total = theta + rate
    log_total = jnp.log(total)
    log_theta = jnp.log(theta)
    ratio = (theta + x) / total
    nll = -(
        jnp.log(product) - log_factorial
        + theta * (log_theta - log_total)
        + x * (jnp.log(rate) - log_total)
    )
    d_logit = (ratio - x / rate) * rate_scale * sigmoid * norm_scale
    d_theta = -(slope / product + log_theta + 1.0 - log_total - ratio)
    return nll, d_logit, d_theta


def network_kernel(
    head, genes_all, cells_all, panel_count, encoder_count,
    counts_hbm, groups, w_hbm, q1_hbm, q2_hbm, o1_hbm, o2_hbm, panel_row, w_mean_hbm, w_disp,
    cell_loss, gradient, disp_block, *refs,
):
    (
        counts, hidden, library, w_mean, tile, slots, back, piece, columns, field, panel_part, loss, panel_col, logits, thetas, mean_sem,
        s_send, s_recv, h_send, h_recv, v_send, v_recv, f_send, f_recv, d_send, d_recv, o_send, o_recv,
    ) = refs[encoder_count:]
    place = Place()
    r = lax.axis_index("grp")
    genes, cells = counts.shape
    width = hidden.shape[1]
    share = width // NR
    parts = 4
    few = 48
    step = genes // parts
    norm_scale = cells_all ** (-0.5)
    rows = pl.ds(pl.multiple_of(place.g * ROWS, ROWS), ROWS)
    out, into = [], []
    for k in range(1, NR):
        to, frm = lax.rem(r + k, NR), lax.rem(r + NR - k, NR)
        out.append(remote(piece.at[to], columns.at[r, rows], h_send.at[k], h_recv.at[r], "grp", to))
        into.append(remote(piece.at[frm], columns.at[frm, rows], h_send.at[k], h_recv.at[frm], "grp", frm))
    load_mean = pltpu.make_async_copy(w_mean_hbm, w_mean, mean_sem.at[0])
    load_counts = pltpu.make_async_copy(counts_hbm, counts, mean_sem.at[1])

    def early():
        panel_col[...] = jnp.broadcast_to(panel_row[...].astype(F32), (128, genes)).T
        piece[...] = jnp.zeros_like(piece)
        panel_part[...] = jnp.zeros_like(panel_part)
        loss[...] = jnp.zeros_like(loss)

    def after():
        own = hidden[rows, :].astype(F32)
        for k in range(NR):
            piece[k, :, 0:share] = own[:, k * share:(k + 1) * share].astype(BF16)
        for copy in out:
            copy.start()
        columns[r, rows] = piece[r]

    def meet(start, finish):
        def meanwhile():
            load_counts.start()
            start()
            load_mean.start()
            early()
            load_counts.wait()
            finish()

        greet(everyone(place) + [("grp", lax.rem(r + k, NR)) for k in range(1, NR)], meanwhile)

    encode(
        head, meet, after, counts, groups, w_hbm, q1_hbm, q2_hbm, o1_hbm, o2_hbm, hidden, library, *refs[:encoder_count]
    )
    load_mean.wait()
    disp = lax.dot_general(w_disp[...], hidden[...], DN_T, preferred_element_type=F32)
    table = DISP_BASE + (jnp.maximum(disp, 0.0) + jnp.log1p(jnp.exp(-jnp.abs(disp))))
    high = table.astype(BF16)
    rest = table - high.astype(F32)
    middle = rest.astype(BF16)
    low = (rest - middle.astype(F32)).astype(BF16)
    tables = jnp.concatenate([high, middle, low], axis=0)
    rate_scale = library[0:1] / genes_all

    v_gather = WideGather(
        place, lambda o: columns.at[:, pl.ds(pl.multiple_of(o * ROWS, ROWS), ROWS), :], v_send, v_recv, 0
    )
    field_gather = []
    for p in range(parts):
        block = lambda o, p=p: field.at[o, pl.ds(p * step, step), :]
        field_gather.append(
            GroupGatherZ(r, block, f_send, f_recv, p, True) if p == 0 else GroupGather(r, block, f_send, f_recv, p)
        )
    half = panel_count // 2
    mine = pl.ds(pl.multiple_of(place.core * half, half), half)
    mine_field = pl.ds(pl.multiple_of(genes + place.core * half, half), half)
    disp_gather = GroupDirect(r, lambda o: field.at[o, mine_field, :], d_send, d_recv)
    spread = GroupDirect(r, lambda o: disp_block.at[o, mine, :], o_send, o_recv)
    swap_halves = remote(
        disp_block.at[:, mine, :], disp_block.at[:, mine, :], o_send.at[0], o_recv.at[0], "gene", place.other_core
    )

    def decode(p):
        at = pl.ds(p * step, step)
        logits[...] = lax.dot_general(w_mean[at, :], hidden[...], DN_T, preferred_element_type=F32)
        lane = lax.broadcasted_iota(jnp.int32, (step, 3 * panel_count), 1)
        pick = (panel_col[at, 0:1] == lax.rem(lane, panel_count).astype(F32)).astype(F32).astype(BF16)
        thetas[...] = jnp.dot(pick, tables, preferred_element_type=F32)

        def chunk(i, lost):
            rows = pl.ds(pl.multiple_of(i * few, few), few)
            there = pl.ds(pl.multiple_of(p * step + i * few, few), few)
            nll, d_logit, d_theta = terms(
                counts[there, :].astype(F32), thetas[rows, :], logits[rows, :], rate_scale, norm_scale, 12
            )
            field[r, there, :] = d_logit.astype(BF16)
            thetas[rows, :] = d_theta
            return lost + jnp.sum(nll, axis=0, keepdims=True)

        loss[...] += lax.fori_loop(0, step // few, chunk, jnp.zeros_like(loss))
        d_theta = thetas[...]
        if p < parts - 1:
            field_gather[p].start()
        row = lax.broadcasted_iota(jnp.int32, (step, 128), 1)
        wanted = jnp.where(lax.rem(row, 8) < 4, (row // 8) * 4 + lax.rem(row, 8), -1)
        pick_t = (panel_col[at, :] == wanted.astype(F32)).astype(F32).astype(BF16)
        upper = d_theta.astype(BF16)
        lower = (d_theta - upper.astype(F32)).astype(BF16)
        panel_part[...] += lax.dot_general(pick_t, upper, DN_0, preferred_element_type=F32) + lax.dot_general(
            pick_t, lower, DN_0, preferred_element_type=F32
        )

    for copy in into:
        copy.wait_recv()
    v_gather.start()
    decode(0)
    v_gather.second()
    decode(1)
    field_gather[0].second()
    v_gather.third()
    decode(2)
    field_gather[1].second()
    field_gather[0].third()
    decode(3)

    row = lax.broadcasted_iota(jnp.int32, (128, cells), 0)
    both = jnp.where(lax.rem(row, 8) == 4, loss[...], panel_part[...])
    tile[...] = both.reshape(NG, 8, cells)
    first = Swap(place, lambda t: tile.at[t], slots, s_send, s_recv, 0)
    first.start()
    field_gather[3].start()
    slots[place.g] = tile[place.g]
    field_gather[2].second()
    field_gather[1].third()
    first.finish()
    summed = total_of(slots)
    back[place.g] = summed
    second = Swap(place, lambda t: back.at[place.g], back, s_send, s_recv, 1)
    second.start()
    cell_loss[...] = summed[4:5] / genes_all
    v_gather.finish()
    second.finish()
    d_panel = jnp.concatenate([back[k, 0:4] for k in range(NG)], axis=0)
    tail = jnp.exp(-jnp.abs(disp))
    d_disp = d_panel * (jnp.where(disp >= 0, 1.0, tail) / (1.0 + tail)) * norm_scale
    field[r, pl.ds(genes, panel_count), :] = d_disp.astype(BF16)
    disp_gather.start()
    field_gather[2].third()
    field_gather[3].second()

    def contract(at, size):
        total = jnp.zeros((size, columns.shape[2]), F32)
        for k in range(NR):
            total = total + jnp.dot(field[k, at, :], columns[k], preferred_element_type=F32)
        return total

    def gradient_of(p):
        field_gather[p].finish()
        gradient[pl.ds(p * step, step), :] = contract(pl.ds(p * step, step), step)

    gradient_of(0)
    gradient_of(1)
    field_gather[3].third()
    disp_gather.finish()
    disp_block[r, mine, :] = contract(mine_field, half)
    spread.start()
    gradient_of(2)
    gradient_of(3)
    spread.finish()
    swap_halves.start()
    swap_halves.wait()
    for copy in out:
        copy.wait_send()
    for one in [v_gather, first, second, disp_gather, spread] + field_gather:
        one.drain()


def finish_kernel(gradient, disp_block, loss, cell_loss, grad_mean, grad_disp):
    share = grad_mean.shape[0]
    cell_loss[...] = loss[...]
    grad_mean[...] = gradient[...].T[0:share]
    for k in range(NR):
        grad_disp[:, k * share:(k + 1) * share] = disp_block[k, :, 0:share]


def hbm():
    return pl.BlockSpec(memory_space=pl.ANY)


def whole():
    return pl.BlockSpec(memory_space=pltpu.VMEM)


def params(number):
    return pltpu.CompilerParams(collective_id=number, has_side_effects=True, vmem_limit_bytes=LIMIT)


def shards(counts, panels, membership, w_proj, w_qkv_within, w_out_within, w_qkv_cross, w_out_cross, w_mean, w_disp):
    cells, genes = counts.shape
    width = w_qkv_within.shape[0]
    head = w_out_within.shape[1]
    genes_all = genes * NG
    cells_all = cells * NR
    panel_count = w_disp.shape[1]
    counts_t = counts.T
    swap_sems = [pltpu.SemaphoreType.DMA((2, NG))] * 2
    first_part = encoder_scratch(width, genes, cells, head)
    cell_loss, gradient, disp_block = pl.pallas_call(
        functools.partial(network_kernel, head, genes_all, cells_all, panel_count, len(first_part)),
        name="network",
        out_shape=(
            jax.ShapeDtypeStruct((1, cells), F32),
            jax.ShapeDtypeStruct((genes, 256), F32),
            jax.ShapeDtypeStruct((NR, panel_count, 256), F32),
        ),
        in_specs=[hbm(), whole()] + [hbm()] * 5 + [whole(), hbm(), whole()],
        out_specs=(whole(), whole(), whole()),
        scratch_shapes=first_part + [
            pltpu.VMEM((genes, cells), jnp.int32),
            pltpu.VMEM((cells, width), BF16),
            pltpu.VMEM((8, cells), F32),
            pltpu.VMEM((genes, width), BF16),
            pltpu.VMEM((NG, 8, cells), F32),
            pltpu.VMEM((NG, 8, cells), F32),
            pltpu.VMEM((NG, 8, cells), F32),
            pltpu.VMEM((NR, ROWS, 256), BF16),
            pltpu.VMEM((NR, cells, 256), BF16),
            pltpu.VMEM((NR, genes + panel_count, cells), BF16),
            pltpu.VMEM((128, cells), F32),
            pltpu.VMEM((1, cells), F32),
            pltpu.VMEM((genes, 128), F32),
            pltpu.VMEM((genes // 4, cells), F32),
            pltpu.VMEM((genes // 4, cells), F32),
            pltpu.SemaphoreType.DMA((2,)),
        ] + swap_sems + [
            pltpu.SemaphoreType.DMA((NR,)),
            pltpu.SemaphoreType.DMA((NR,)),
            pltpu.SemaphoreType.DMA((1, WideGather.SLOTS)),
            pltpu.SemaphoreType.DMA((1, WideGather.SLOTS)),
            pltpu.SemaphoreType.DMA((4, GroupGather.SLOTS)),
            pltpu.SemaphoreType.DMA((4, GroupGather.SLOTS)),
            pltpu.SemaphoreType.DMA((NR,)),
            pltpu.SemaphoreType.DMA((NR,)),
            pltpu.SemaphoreType.DMA((NR,)),
            pltpu.SemaphoreType.DMA((NR,)),
        ],
        compiler_params=params(0),
    )(
        counts_t, membership, w_proj, jnp.transpose(w_qkv_within, (2, 1, 0)), jnp.transpose(w_qkv_cross, (2, 1, 0)),
        jnp.transpose(w_out_within, (1, 0, 2)), jnp.transpose(w_out_cross, (1, 0, 2)),
        panels[None, :], w_mean.T, w_disp.T,
    )
    cell_loss, grad_mean, grad_disp = pl.pallas_call(
        finish_kernel,
        name="finish",
        out_shape=(
            jax.ShapeDtypeStruct((1, cells), F32),
            jax.ShapeDtypeStruct((width // NR, genes), F32),
            jax.ShapeDtypeStruct((panel_count, width), F32),
        ),
        in_specs=[whole()] * 3,
        out_specs=(whole(), whole(), whole()),
    )(gradient, disp_block, cell_loss)
    return cell_loss[0], grad_mean, grad_disp.T


def solution(mesh):
    return jax.shard_map(
        shards,
        mesh=mesh,
        in_specs=(
            P("grp", "gene"),
            P("gene"),
            P("grp", None),
            P("gene", None),
            P(None, "gene", None),
            P("gene", None, None),
            P(None, "gene", None),
            P("gene", None, None),
            P(None, "gene"),
            P(),
        ),
        out_specs=(P("grp"), P("grp", "gene"), P()),
        check_vma=False,
    )
```

```python
import functools
import math

import jax
import jax.numpy as jnp
from jax import lax
from jax.experimental import pallas as pl
from jax.experimental.pallas import tpu as pltpu
from jax.sharding import PartitionSpec as P

EPS = 1e-06
FLOOR = 0.3
TARGET = 10000.0
DISP_BASE = 0.5
MESH = pl.DeviceIdType.MESH
F32 = jnp.float32
BF16 = jnp.bfloat16

NX = 4
NY = 2
NG = 16
NCHIP = 8
NR = 8
NZ = 4
NM = 4
ROWS = 16
LIMIT = 64 * 1024 * 1024 - 256 * 1024
DN_T = (((1,), (1,)), ((), ()))
DN_0 = (((0,), (0,)), ((), ()))


def remote(src, dst, send, recv, axis, to):
    return pltpu.make_async_remote_copy(
        src_ref=src, dst_ref=dst, send_sem=send, recv_sem=recv, device_id={axis: to}, device_id_type=MESH
    )


class Place:
    def __init__(self):
        self.g = lax.axis_index("gene")
        self.core = lax.rem(self.g, 2)
        self.x = lax.rem(self.g // 2, NX)
        self.y = self.g // (2 * NX)
        self.right = self.at(self.y, self.shift(1), self.core)
        self.left = self.at(self.y, self.shift(3), self.core)
        self.other_y = self.at(1 - self.y, self.x, self.core)
        self.other_core = self.at(self.y, self.x, 1 - self.core)

    def shift(self, by):
        return lax.rem(self.x + by, NX)

    def at(self, y, x, core):
        return (y * NX + x) * 2 + core

    def chip(self, y, x):
        return y * NX + x


def greet(axis_peers, meanwhile):
    barrier = pltpu.get_barrier_semaphore()
    for axis, to in axis_peers:
        pl.semaphore_signal(barrier, inc=1, device_id={axis: to}, device_id_type=MESH)
    meanwhile()
    pl.semaphore_wait(barrier, len(axis_peers))


def everyone(place):
    return [("gene", lax.rem(place.g + k, NG)) for k in range(1, NG)]


def rms(values):
    return values * lax.rsqrt(jnp.mean(values * values, axis=-1, keepdims=True) + EPS)


class Scatter:
    @staticmethod
    def scratch(width, sends):
        return [
            pltpu.VMEM((NM, NCHIP, ROWS, width), BF16),
            pltpu.VMEM((NM, 3, ROWS, width), BF16),
            pltpu.VMEM((NM, 3, ROWS, width), BF16),
            pltpu.VMEM((NM, 2, ROWS, width), BF16),
            pltpu.VMEM((NM, ROWS, width), BF16),
            pltpu.VMEM((NM, ROWS, width), BF16),
            pltpu.VMEM((NM, ROWS, width), F32),
            pltpu.VMEM((2, NX, ROWS, width), BF16),
            pltpu.SemaphoreType.DMA((NM, 7)),
        ] + [pltpu.SemaphoreType.DMA((NM, 7))] * sends

    def __init__(self, place, refs):
        (self.chip, self.from_left, self.from_right, self.relay, self.y_out, self.y_in, self.mine, four, recv, send) = refs
        self.send, self.recv = send, recv
        p = self.place = place
        ahead, behind, across = p.shift(1), p.shift(3), p.shift(2)
        self.copies, self.turned = [], {}
        for m in range(NM):
            if m % 2 == 0:
                self.turned[m] = ScatterY(self, m, four.at[m // 2], 1 if m == 0 else -1)
                self.copies.append(self.turned[m].c)
                continue

            def go(slot, src, dst, to):
                return remote(src, dst, send.at[m, slot], recv.at[m, slot], "gene", to)
            self.copies.append([
                go(0, self.chip.at[m, p.chip(0, across)], self.from_left.at[m, 0], p.right),
                go(1, self.chip.at[m, p.chip(1, across)], self.from_right.at[m, 0], p.left),
                go(2, self.chip.at[m, p.chip(1, ahead)], self.from_left.at[m, 2], p.right),
                go(3, self.chip.at[m, p.chip(0, behind)], self.from_right.at[m, 2], p.left),
                go(4, self.relay.at[m, 0], self.from_left.at[m, 1], p.right),
                go(5, self.relay.at[m, 1], self.from_right.at[m, 1], p.left),
                go(6, self.y_out.at[m], self.y_in.at[m], p.other_y),
            ])

    def spread(self, m):
        if m in self.turned:
            return self.turned[m].spread()
        for k in (0, 1, 2, 3):
            self.copies[m][k].start()

    def forward(self, m):
        if m in self.turned:
            return self.turned[m].forward()
        p = self.place
        self.copies[m][0].wait_recv()
        self.relay[m, 0] = (
            self.chip[m, p.chip(0, p.shift(1))].astype(F32) + self.from_left[m, 0].astype(F32)
        ).astype(BF16)
        self.copies[m][4].start()
        self.copies[m][1].wait_recv()
        self.relay[m, 1] = (
            self.chip[m, p.chip(1, p.shift(3))].astype(F32) + self.from_right[m, 0].astype(F32)
        ).astype(BF16)
        self.copies[m][5].start()

    def cross(self, m):
        if m in self.turned:
            return self.turned[m].cross()
        p = self.place
        for k in (2, 3, 4, 5):
            self.copies[m][k].wait_recv()
        self.y_out[m] = (
            self.chip[m, p.chip(1 - p.y, p.x)].astype(F32)
            + self.from_left[m, 2 - p.y].astype(F32)
            + self.from_right[m, 1 + p.y].astype(F32)
        ).astype(BF16)
        self.copies[m][6].start()
        self.mine[m] = (
            self.chip[m, p.chip(p.y, p.x)].astype(F32)
            + self.from_left[m, 1 + p.y].astype(F32)
            + self.from_right[m, 2 - p.y].astype(F32)
        )

    def take(self, m):
        if m in self.turned:
            return self.turned[m].take()
        self.copies[m][6].wait_recv()
        return self.mine[m] + self.y_in[m].astype(F32)

    def drain(self):
        for row in self.copies:
            for copy in row:
                copy.wait_send()


class ScatterY:
    def __init__(self, base, m, y_four, way):
        p = base.place
        self.base, self.m, self.four = base, m, y_four
        to, back = (p.right, p.left) if way > 0 else (p.left, p.right)
        ahead, behind = (p.shift(1), p.shift(3)) if way > 0 else (p.shift(3), p.shift(1))
        self.order = (p.shift(2), behind, ahead)
        self.outgoing = (base.relay.at[m, 0], base.relay.at[m, 1], base.y_out.at[m])
        self.incoming = (base.from_left.at[m, 0], base.from_right.at[m, 0], base.from_left.at[m, 1])

        def go(slot, src, dst, device):
            return remote(src, dst, base.send.at[m, slot], base.recv.at[m, slot], "gene", device)

        self.c = [
            go(k, base.chip.at[m, p.chip(1 - p.y, x)], y_four.at[x], p.other_y)
            for k, x in enumerate(self.order + (p.x,))
        ] + [go(4 + k, self.outgoing[k], self.incoming[k], (to, back, to)[k]) for k in range(3)]

    def spread(self):
        for k in range(4):
            self.c[k].start()

    def total(self, k):
        p = self.base.place
        x = p.x if k == 3 else self.order[k]
        self.c[k].wait_recv()
        return self.base.chip[self.m, p.chip(p.y, x)].astype(F32) + self.four[x].astype(F32)

    def forward(self):
        for k in (0, 1):
            self.outgoing[k][...] = self.total(k).astype(BF16)
            self.c[4 + k].start()

    def cross(self):
        value = self.total(2)
        self.c[4].wait_recv()
        self.outgoing[2][...] = (value + self.incoming[0][...].astype(F32)).astype(BF16)
        self.c[6].start()
        self.base.mine[self.m] = self.total(3)

    def take(self):
        self.c[5].wait_recv()
        self.c[6].wait_recv()
        return self.base.mine[self.m] + self.incoming[1][...].astype(F32) + self.incoming[2][...].astype(F32)


def run_pipeline(steps, count=NM):
    for t in range(count + len(steps) - 1):
        for lag, step in enumerate(steps):
            if 0 <= t - lag < count:
                step(t - lag)


class Gather:
    SLOTS = 7

    def __init__(self, place, block, send, recv, index, send_index=None):
        p = place
        send_index = index if send_index is None else send_index
        ahead, behind, across = p.shift(1), p.shift(3), p.shift(2)
        y, z, x = p.y, 1 - p.y, p.x

        def go(slot, owner, to):
            ref = block(owner)
            return remote(ref, ref, send.at[send_index, slot], recv.at[index, slot], "gene", to)

        own, paired = p.chip(y, x), p.chip(z, x)
        self.c = [
            go(0, own, p.other_y),
            go(1, own, p.right),
            go(2, own, p.left),
            go(3, paired, p.right),
            go(4, paired, p.left),
            go(5, p.chip(y, behind), p.right),
            go(6, p.chip(z, ahead), p.left),
        ]

    def start(self):
        for k in (1, 2, 0):
            self.c[k].start()

    def second(self):
        c = self.c
        c[1].wait_recv()
        c[5].start()
        c[0].wait_recv()
        c[3].start()
        c[4].start()

    def third(self):
        self.c[4].wait_recv()
        self.c[6].start()

    def finish(self):
        for k in (2, 3, 5, 6):
            self.c[k].wait_recv()

    def drain(self):
        for copy in self.c:
            copy.wait_send()


class GatherX:
    def __init__(self, place, block, send, recv, index, send_index, rightward):
        p = place
        ahead, behind, across = p.shift(1), p.shift(3), p.shift(2)
        y, x = p.y, p.x
        self.rightward = rightward

        def go(slot, owner, to):
            ref = block(owner)
            return remote(ref, ref, send.at[send_index, slot], recv.at[index, slot], "gene", to)

        self.c = [
            go(0, p.chip(y, x), p.right),
            go(1, p.chip(y, x), p.left),
            go(2, p.chip(y, behind), p.right) if rightward else go(2, p.chip(y, ahead), p.left),
            go(3, p.chip(y, x), p.other_y),
            go(4, p.chip(y, behind), p.other_y),
            go(5, p.chip(y, ahead), p.other_y),
            go(6, p.chip(y, across), p.other_y),
        ]

    def start(self):
        for k in (0, 1, 3):
            self.c[k].start()

    def second(self):
        c = self.c
        for k in (0, 1):
            c[k].wait_recv()
            if self.rightward == (k == 0):
                c[2].start()
            c[4 + k].start()

    def third(self):
        self.c[2].wait_recv()
        self.c[6].start()

    def finish(self):
        for k in (3, 4, 5, 6):
            self.c[k].wait_recv()

    def drain(self):
        for copy in self.c:
            copy.wait_send()


def lead(gathers):
    for one in gathers:
        one.second()
    for one in gathers[:2]:
        one.third()


class WideGather:
    SLOTS = 15

    def __init__(self, place, block, send, recv, index):
        p = place
        core, x, y, z = p.core, p.x, p.y, 1 - p.y
        ahead, behind, across = p.shift(1), p.shift(3), p.shift(2)
        self.far = Gather(place, lambda q: block(2 * q + core), send, recv, index)
        held = [p.chip(y, x), p.chip(z, x), p.chip(y, behind), p.chip(y, ahead), p.chip(z, behind), p.chip(z, ahead),
                p.chip(y, across), p.chip(z, across)]
        self.near = []
        for k, q in enumerate(held):
            ref = block(2 * q + core)
            self.near.append(remote(ref, ref, send.at[index, 7 + k], recv.at[index, 7 + k], "gene", p.other_core))

    def start(self):
        self.far.start()
        self.near[0].start()

    def second(self):
        self.far.second()
        self.near[1].start()
        self.near[2].start()

    def third(self):
        self.far.third()
        self.near[5].start()

    def finish(self):
        self.far.finish()
        for k in (3, 4, 6, 7):
            self.near[k].start()
        for copy in self.near:
            copy.wait_recv()

    def drain(self):
        self.far.drain()
        for copy in self.near:
            copy.wait_send()


class DirectSum:
    def __init__(self, place, shares, slots, send, recv):
        p = place
        self.shares, self.slots = shares, slots
        self.chip = p.chip(p.y, p.x)
        self.c = []
        for k in range(1, NCHIP):
            to = lax.rem(self.chip + k, NCHIP)
            self.c.append(remote(shares.at[to], slots.at[k], send.at[k], recv.at[k], "gene", to * 2 + p.core))

    def start(self):
        for copy in self.c:
            copy.start()

    def take(self):
        total = self.shares[self.chip].astype(F32)
        for k in range(1, NCHIP):
            self.c[k - 1].wait_recv()
            total = total + self.slots[k].astype(F32)
        return total

    def drain(self):
        for copy in self.c:
            copy.wait_send()


class Direct:
    def __init__(self, place, block, send, recv, index):
        p = place
        chip = p.chip(p.y, p.x)
        own = block(p.g)
        self.out, self.pair = [], []
        for k in range(NCHIP):
            to, frm = lax.rem(chip + k, NCHIP) * 2 + p.core, lax.rem(chip + NCHIP - k, NCHIP) * 2 + p.core
            ref = block(frm)
            if k:
                self.out.append(remote(own, own, send.at[index, k], recv.at[index, k], "gene", to))
            self.pair.append(remote(ref, ref, send.at[index, 7 + k if k else 0], recv.at[index, 7 + k if k else 0], "gene", p.other_core))

    def start(self):
        for copy in self.out + self.pair[:1]:
            copy.start()

    def finish(self):
        for k in range(1, NCHIP):
            self.out[k - 1].wait_recv()
            self.pair[k].start()
        for copy in self.pair:
            copy.wait_recv()

    def drain(self):
        for copy in self.out + self.pair:
            copy.wait_send()


class Swap:
    def __init__(self, place, source, slots, send, recv, index):
        self.out, self.into = [], []
        for k in range(1, NG):
            to, frm = lax.rem(place.g + k, NG), lax.rem(place.g + NG - k, NG)
            self.out.append(remote(source(to), slots.at[place.g], send.at[index, k], recv.at[index, place.g], "gene", to))
            self.into.append(remote(source(frm), slots.at[frm], send.at[index, k], recv.at[index, frm], "gene", frm))

    def start(self):
        for copy in self.out:
            copy.start()

    def finish(self):
        for copy in self.into:
            copy.wait_recv()

    def drain(self):
        for copy in self.out:
            copy.wait_send()


def total_of(slots):
    total = slots[0]
    for k in range(1, NG):
        total = total + slots[k]
    return total


def group_sum(values):
    high = values.astype(BF16)
    low = (values - high.astype(F32)).astype(BF16)
    shape = (values.shape[1], values.shape[1])
    row = lax.broadcasted_iota(jnp.int32, shape, 0) // 64
    col = lax.broadcasted_iota(jnp.int32, shape, 1) // 64
    ones = (row == col).astype(F32).astype(BF16)
    return jnp.dot(high, ones, preferred_element_type=F32) + jnp.dot(low, ones, preferred_element_type=F32)


def heads_of(rows, weights, head):
    parts = [jnp.dot(rows, weights[k], preferred_element_type=F32) for k in range(3)]
    for k in range(2):
        mean = group_sum(parts[k] * parts[k]) / head
        parts[k] = (parts[k] * lax.rsqrt(jnp.maximum(mean, FLOOR))).astype(BF16)
    parts[2] = parts[2].astype(BF16)
    return parts


def turned(values, by):
    if by == 0:
        return values
    row = lax.rem(lax.broadcasted_iota(jnp.int32, values.shape, 0), ROWS)
    count = values.shape[0]
    return jnp.where(row < by, pltpu.roll(values, count - ROWS + by, 0), pltpu.roll(values, by, 0))


def within_mix(query, keys, values, head):
    q, k, v = (part.astype(F32) for part in (query, keys, values))
    count = q.shape[0]
    scores = group_sum(jnp.concatenate([q * turned(k, 4 * d) for d in range(NM)], axis=0))
    weights = [jnp.exp(scores[d * count:(d + 1) * count] * head ** (-0.5)) for d in range(NM)]
    total = weights[0] + weights[1] + weights[2] + weights[3]
    mixed = None
    for d in range(NM):
        term = (weights[d] / total).astype(BF16).astype(F32) * turned(v, 4 * d)
        mixed = term if mixed is None else mixed + term
    return mixed.astype(BF16)


def cross_mix(query, keys, values, same, head):
    lane = lax.broadcasted_iota(jnp.int32, query.shape, 1) // 64
    q = query.astype(F32)
    mixed = jnp.zeros(query.shape, F32)
    for h in range(query.shape[1] // 64):
        one = jnp.where(lane == h, q, 0.0).astype(BF16)
        scores = lax.dot_general(one, keys, DN_T, preferred_element_type=F32) * head ** (-0.5)
        weights = jnp.where(same, jnp.exp(scores), 0.0)
        probs = (weights / jnp.sum(weights, axis=-1, keepdims=True)).astype(BF16)
        mixed = jnp.where(lane == h, jnp.dot(probs, values, preferred_element_type=F32), mixed)
    return mixed.astype(BF16)


def encoder_scratch(width, genes, cells, head):
    half = cells // 2
    raw = [pltpu.VMEM((3 * head, 2, width), BF16), pltpu.VMEM((head, 2, width), BF16)]
    layer = [
        pltpu.VMEM((3, width, 256), BF16),
        pltpu.VMEM((256, width), BF16),
        pltpu.VMEM((NM, NCHIP, ROWS, width), BF16),
    ]
    return (
        [
            pltpu.VMEM((cells, genes), BF16),
            pltpu.VMEM((NM, genes, 1664), BF16),
            pltpu.VMEM((8, cells), F32),
            pltpu.VMEM((NG, 8, cells), F32),
            pltpu.VMEM((NM, NCHIP, 2, ROWS, width), BF16),
            pltpu.VMEM((NM, NCHIP, ROWS, width), BF16),
            pltpu.VMEM((128, width), F32),
            pltpu.VMEM((2, 3 * head, width), F32),
            pltpu.VMEM((NM, ROWS, width), F32),
            pltpu.VMEM((NM, ROWS, width), F32),
            pltpu.VMEM((NM, 2, 2, half, 256), BF16),
            pltpu.VMEM((NM, half, 256), BF16),
            pltpu.VMEM((cells, 128), F32),
            pltpu.SemaphoreType.DMA((NM + 4,)),
        ]
        + raw * 2
        + layer * 2
        + [pltpu.SemaphoreType.DMA((1, NG))] * 2
        + [pltpu.SemaphoreType.DMA((NM,))] * 2
        + [pltpu.SemaphoreType.DMA((NM,))] * 2
        + [pltpu.SemaphoreType.DMA((NM,))] * 2
        + [pltpu.SemaphoreType.DMA((NM, Gather.SLOTS)), pltpu.SemaphoreType.DMA((2 * NM, Gather.SLOTS))]
        + [pltpu.SemaphoreType.DMA((1, 16))] * 2
        + Scatter.scratch(width, 1)
        + Scatter.scratch(width, 0)
        + [
            pltpu.VMEM((half, width), F32),
            pltpu.VMEM((NCHIP, ROWS, width), BF16),
            pltpu.VMEM((NCHIP, ROWS, width), BF16),
            pltpu.SemaphoreType.DMA((NCHIP,)),
            pltpu.SemaphoreType.DMA((NCHIP,)),
        ]
    )


def encode(head, meet, after, counts, groups, w_hbm, q1_hbm, q2_hbm, o1_hbm, o2_hbm, hidden, library, *refs):
    (scaled, w_proj, tile, slots, halves, pair, padded, split, tokens, resid, kv, queries, spot, load_sem) = refs[:14]
    raws, layers = refs[14:18], refs[18:24]
    (s_send, s_recv, w_send, w_recv, p_send, p_recv, k_send, k_recv, a_send, a_recv, d_send, d_recv) = refs[24:36]
    sums, (gathered, shares, share_in, z_send, z_recv) = refs[36:-5], refs[-5:]
    place = Place()
    width = resid.shape[-1]
    wide = w_proj.shape[-1]
    core, here = place.core, place.chip(place.y, place.x)
    scatter = [Scatter(place, sums[0:10]), Scatter(place, sums[10:19] + sums[9:10])]
    weights, outs, blocks = layers[0::3], layers[1::3], layers[2::3]

    small = [
        pltpu.make_async_copy(src, dst, load_sem.at[NM + k])
        for k, (src, dst) in enumerate(zip((q1_hbm, o1_hbm, q2_hbm, o2_hbm), raws))
    ]
    loads = [
        pltpu.make_async_copy(w_hbm.at[:, pl.ds((m * width) // 128 * 128, wide)], w_proj.at[m], load_sem.at[m])
        for m in range(NM)
    ]

    def first():
        for load in small[:2] + loads + small[2:]:
            load.start()

    def second():
        tile[...] = jnp.broadcast_to(jnp.sum(counts[...].astype(F32), axis=0, keepdims=True), tile.shape)

    meet(first, second)
    swap = Swap(place, lambda t: tile, slots, s_send, s_recv, 0)
    swap.start()
    slots[place.g] = tile[...]

    lanes = pl.ds(pl.multiple_of(core * 128, 128), 128)
    share = []
    for k in range(2):
        share.append([
            remote(weights[k].at[:, :, lanes], weights[k].at[:, :, lanes], w_send.at[2 * k], w_recv.at[2 * k], "gene", place.other_core),
            remote(outs[k].at[lanes, :], outs[k].at[lanes, :], w_send.at[2 * k + 1], w_recv.at[2 * k + 1], "gene", place.other_core),
        ])

    def prepare(k):
        padded[...] = jnp.zeros_like(padded)
        small[2 * k].wait()
        for h in range(2):
            split[h] = raws[2 * k][:, h, :].astype(F32)
        for a in range(3):
            for h in range(2):
                padded[64 * h:64 * h + head, :] = split[h, a * head:(a + 1) * head, :]
            weights[k][a, :, lanes] = padded[...].T.astype(BF16)
        share[k][0].start()
        small[2 * k + 1].wait()
        for h in range(2):
            padded[64 * h:64 * h + head, :] = raws[2 * k + 1][:, h, :].astype(F32)
        outs[k][lanes, :] = padded[...].astype(BF16)
        share[k][1].start()

    prepare(0)
    swap.finish()
    total = 1.0 + total_of(slots)
    library[...] = total
    scaled[...] = jnp.log1p(counts[...].astype(F32) * (TARGET / total[0:1])).T.astype(BF16)

    pairs = [
        remote(halves.at[m, :, 1 - core], pair.at[m], p_send.at[m], p_recv.at[m], "gene", place.other_core)
        for m in range(NM)
    ]

    def project(m):
        loads[m].wait()
        skip = (m * width) % 128
        out = jnp.dot(scaled[...], w_proj[m], preferred_element_type=F32)[:, skip:skip + width]
        halves[m] = out.astype(BF16).reshape(NCHIP, 2, ROWS, width)
        pairs[m].start()

    def join(m):
        pairs[m].wait_recv()
        for q in range(NCHIP):
            scatter[0].chip[m, q] = (halves[m, q, core].astype(F32) + pair[m, q].astype(F32)).astype(BF16)
        scatter[0].spread(m)

    def keep(m):
        scatter[0].mine[m] = scatter[0].take(m)

    run_pipeline([project, join, scatter[0].forward, scatter[0].cross, keep])
    scatter[0].drain()

    gathers = [
        [
            GatherX(place, lambda q, k=k, m=m: blocks[k].at[m, q], a_send, a_recv, k * NM + m, m, m == 0)
            if m % 2 == 0
            else Gather(place, lambda q, k=k, m=m: blocks[k].at[m, q], a_send, a_recv, k * NM + m, m)
            for m in range(NM)
        ]
        for k in range(2)
    ]
    for s in range(NM):
        for m in range(NM):
            tokens[s, 4 * m:4 * m + 4, :] = scatter[0].mine[m, 4 * s:4 * s + 4, :]
        blocks[0][s, here] = rms(tokens[s]).astype(BF16)
        gathers[0][s].start()

    prepare(1)
    cells = 2 * kv.shape[3]
    at = lax.broadcasted_iota(jnp.int32, (cells, cells), 1)
    source = 32 * (lax.rem(at, 128) // ROWS) + ROWS * (at // 128) + lax.rem(at, ROWS)
    order = (lax.broadcasted_iota(jnp.int32, (cells, cells), 0) == source).astype(F32).astype(BF16)
    row = jnp.dot(
        jnp.broadcast_to(groups[...].astype(F32), (128, cells)).astype(BF16), order, preferred_element_type=F32
    )
    spot[...] = row.T
    same = jnp.broadcast_to(spot[lanes, 0:1], (128, cells)) == row
    for copy in share[0]:
        copy.wait_recv()

    lead(gathers[0])

    def within(s):
        gathers[0][s].finish()
        if s + 2 < NM:
            gathers[0][s + 2].third()
        rows = blocks[0][s].reshape(NCHIP * ROWS, width)
        mixed = within_mix(*heads_of(rows, weights[0], head), head)
        out = jnp.dot(mixed, outs[0][...], preferred_element_type=F32)
        scatter[1].chip[s] = out.astype(BF16).reshape(NCHIP, ROWS, width)
        scatter[1].spread(s)

    def add_within(s):
        tokens[s] = tokens[s] + scatter[1].take(s)

    run_pipeline([within, scatter[1].forward, scatter[1].cross, add_within])
    for one in gathers[0]:
        one.drain()

    for m in range(NM):
        for s in range(NM):
            resid[m, 4 * s:4 * s + 4, :] = tokens[s, 4 * m:4 * m + 4, :]
        blocks[1][m, here] = rms(resid[m]).astype(BF16)
        gathers[1][m].start()
    for copy in share[1]:
        copy.wait_recv()
    trade = [
        remote(kv.at[m, core], kv.at[m, core], k_send.at[m], k_recv.at[m], "gene", place.other_core)
        for m in range(NM)
    ]

    lead(gathers[1])

    def look(m):
        if m + 2 < NM:
            gathers[1][m + 2].third()
        gathers[1][m].finish()
        rows = blocks[1][m].reshape(NCHIP * ROWS, width)
        queries[m], kv[m, core, 0], kv[m, core, 1] = heads_of(rows, weights[1], head)
        trade[m].start()

    def attend(m):
        trade[m].wait_recv()
        keys = jnp.concatenate([kv[m, 0, 0], kv[m, 1, 0]], axis=0)
        values = jnp.concatenate([kv[m, 0, 1], kv[m, 1, 1]], axis=0)
        mixed = cross_mix(queries[m], keys, values, same, head)
        out = jnp.dot(mixed, outs[1][...], preferred_element_type=F32)
        gathered[...] = gathered[...] + out if m else out

    run_pipeline([look, attend])

    shares[...] = gathered[...].astype(BF16).reshape(NCHIP, ROWS, width)
    final = DirectSum(place, shares, share_in, z_send, z_recv)
    final.start()
    pooled = (resid[0] + resid[1] + resid[2] + resid[3] + final.take()) * (1.0 / NM)
    hidden[pl.ds(pl.multiple_of(place.g * ROWS, ROWS), ROWS), :] = rms(pooled).astype(BF16)
    last = Direct(
        place, lambda o: hidden.at[pl.ds(pl.multiple_of(o * ROWS, ROWS), ROWS), :], d_send, d_recv, 0
    )
    last.start()
    after()
    last.finish()
    for one in scatter[1:] + gathers[1] + [swap, final, last]:
        one.drain()
    for copy in share[0] + share[1] + pairs + trade:
        copy.wait_send()


class GroupGather:
    SLOTS = 7

    def __init__(self, r, block, send, recv, index):
        z, h = lax.rem(r, NZ), r // NZ
        up, down = lax.rem(z + 1, NZ), lax.rem(z + 3, NZ)
        k = 1 - h

        def at(a, b):
            return a * NZ + b

        def go(slot, owner, to):
            ref = block(owner)
            return remote(ref, ref, send.at[index, slot], recv.at[index, slot], "grp", to)

        self.c = [
            go(0, at(h, z), at(k, z)),
            go(1, at(h, z), at(h, up)),
            go(2, at(h, z), at(h, down)),
            go(3, at(k, z), at(h, up)),
            go(4, at(k, z), at(h, down)),
            go(5, at(h, down), at(h, up)),
            go(6, at(k, up), at(h, down)),
        ]

    def start(self):
        for k in (1, 2, 0):
            self.c[k].start()

    def second(self):
        c = self.c
        c[1].wait_recv()
        c[5].start()
        c[0].wait_recv()
        c[3].start()
        c[4].start()

    def third(self):
        self.c[4].wait_recv()
        self.c[6].start()

    def finish(self):
        for k in (2, 3, 5, 6):
            self.c[k].wait_recv()

    def drain(self):
        for copy in self.c:
            copy.wait_send()


class GroupGatherZ:
    def __init__(self, r, block, send, recv, index, upward):
        z, h = lax.rem(r, NZ), r // NZ
        up, down, across = lax.rem(z + 1, NZ), lax.rem(z + 3, NZ), lax.rem(z + 2, NZ)
        k = 1 - h
        self.upward = upward

        def at(a, b):
            return a * NZ + b

        def go(slot, owner, to):
            ref = block(owner)
            return remote(ref, ref, send.at[index, slot], recv.at[index, slot], "grp", to)

        self.c = [
            go(0, at(h, z), at(h, up)),
            go(1, at(h, z), at(h, down)),
            go(2, at(h, down), at(h, up)) if upward else go(2, at(h, up), at(h, down)),
            go(3, at(h, z), at(k, z)),
            go(4, at(h, down), at(k, z)),
            go(5, at(h, up), at(k, z)),
            go(6, at(h, across), at(k, z)),
        ]

    def start(self):
        for k in (0, 1, 3):
            self.c[k].start()

    def second(self):
        c = self.c
        for k in (0, 1):
            c[k].wait_recv()
            if self.upward == (k == 0):
                c[2].start()
            c[4 + k].start()

    def third(self):
        self.c[2].wait_recv()
        self.c[6].start()

    def finish(self):
        for k in (3, 4, 5, 6):
            self.c[k].wait_recv()

    def drain(self):
        for copy in self.c:
            copy.wait_send()


class GroupDirect:
    def __init__(self, r, block, send, recv):
        self.out, self.into = [], []
        for k in range(1, NR):
            to, frm = lax.rem(r + k, NR), lax.rem(r + NR - k, NR)
            self.out.append(remote(block(r), block(r), send.at[k], recv.at[k], "grp", to))
            self.into.append(remote(block(r), block(frm), send.at[k], recv.at[k], "grp", frm))

    def start(self):
        for copy in self.out:
            copy.start()

    def finish(self):
        for copy in self.into:
            copy.wait_recv()

    def drain(self):
        for copy in self.out:
            copy.wait_send()


def log_factorials(count):
    return [math.log(math.factorial(k)) for k in range(count)]


def terms(x, theta, logit, rate_scale, norm_scale, most):
    tail = jnp.exp(-jnp.abs(logit))
    soft = jnp.maximum(logit, 0.0) + jnp.log1p(tail)
    sigmoid = jnp.where(logit >= 0, 1.0, tail) / (1.0 + tail)
    rate = rate_scale * soft
    product = jnp.ones_like(theta)
    slope = jnp.zeros_like(theta)
    log_factorial = jnp.zeros_like(theta)
    table = log_factorials(most + 1)
    for k in range(most):
        on = x > k
        term = theta + float(k)
        slope = jnp.where(on, slope * term + product, slope)
        product = jnp.where(on, product * term, product)
        if k:
            log_factorial = jnp.where(on, table[k + 1], log_factorial)
    total = theta + rate
    log_total = jnp.log(total)
    log_theta = jnp.log(theta)
    ratio = (theta + x) / total
    nll = -(
        jnp.log(product) - log_factorial
        + theta * (log_theta - log_total)
        + x * (jnp.log(rate) - log_total)
    )
    d_logit = (ratio - x / rate) * rate_scale * sigmoid * norm_scale
    d_theta = -(slope / product + log_theta + 1.0 - log_total - ratio)
    return nll, d_logit, d_theta


def network_kernel(
    head, genes_all, cells_all, panel_count, encoder_count,
    counts_hbm, groups, w_hbm, q1_hbm, q2_hbm, o1_hbm, o2_hbm, panel_row, w_mean_hbm, w_disp,
    cell_loss, gradient, disp_block, *refs,
):
    (
        counts, hidden, library, w_mean, tile, slots, back, piece, columns, field, panel_part, loss, panel_col, logits, thetas, mean_sem,
        s_send, s_recv, h_send, h_recv, v_send, v_recv, f_send, f_recv, d_recv, o_recv,
    ) = refs[encoder_count:]
    place = Place()
    r = lax.axis_index("grp")
    genes, cells = counts.shape
    width = hidden.shape[1]
    share = width // NR
    parts = 4
    few = 48
    step = genes // parts
    norm_scale = cells_all ** (-0.5)
    rows = pl.ds(pl.multiple_of(place.g * ROWS, ROWS), ROWS)
    out, into = [], []
    for k in range(1, NR):
        to, frm = lax.rem(r + k, NR), lax.rem(r + NR - k, NR)
        out.append(remote(piece.at[to], columns.at[r, rows], h_send.at[k], h_recv.at[r], "grp", to))
        into.append(remote(piece.at[frm], columns.at[frm, rows], h_send.at[k], h_recv.at[frm], "grp", frm))
    load_mean = pltpu.make_async_copy(w_mean_hbm, w_mean, mean_sem.at[0])
    load_counts = pltpu.make_async_copy(counts_hbm, counts, mean_sem.at[1])

    def early():
        panel_col[...] = jnp.broadcast_to(panel_row[...].astype(F32), (128, genes)).T
        piece[...] = jnp.zeros_like(piece)
        panel_part[...] = jnp.zeros_like(panel_part)
        loss[...] = jnp.zeros_like(loss)

    def after():
        own = hidden[rows, :].astype(F32)
        for k in range(NR):
            piece[k, :, 0:share] = own[:, k * share:(k + 1) * share].astype(BF16)
        for copy in out:
            copy.start()
        columns[r, rows] = piece[r]

    def meet(start, finish):
        def meanwhile():
            load_counts.start()
            start()
            load_mean.start()
            early()
            load_counts.wait()
            finish()

        greet(everyone(place) + [("grp", lax.rem(r + k, NR)) for k in range(1, NR)], meanwhile)

    encode(
        head, meet, after, counts, groups, w_hbm, q1_hbm, q2_hbm, o1_hbm, o2_hbm, hidden, library, *refs[:encoder_count]
    )
    load_mean.wait()
    disp = lax.dot_general(w_disp[...], hidden[...], DN_T, preferred_element_type=F32)
    table = DISP_BASE + (jnp.maximum(disp, 0.0) + jnp.log1p(jnp.exp(-jnp.abs(disp))))
    high = table.astype(BF16)
    rest = table - high.astype(F32)
    middle = rest.astype(BF16)
    low = (rest - middle.astype(F32)).astype(BF16)
    tables = jnp.concatenate([high, middle, low], axis=0)
    rate_scale = library[0:1] / genes_all

    v_gather = WideGather(
        place, lambda o: columns.at[:, pl.ds(pl.multiple_of(o * ROWS, ROWS), ROWS), :], v_send, v_recv, 0
    )
    field_gather = []
    for p in range(parts):
        block = lambda o, p=p: field.at[o, pl.ds(p * step, step), :]
        field_gather.append(
            GroupGatherZ(r, block, f_send, f_recv, p, True) if p == 0 else GroupGather(r, block, f_send, f_recv, p)
        )
    half = panel_count // 2
    mine = pl.ds(pl.multiple_of(place.core * half, half), half)
    mine_field = pl.ds(pl.multiple_of(genes + place.core * half, half), half)
    disp_gather = GroupDirect(r, lambda o: field.at[o, mine_field, :], h_send, d_recv)
    spread = GroupDirect(r, lambda o: disp_block.at[o, mine, :], h_send, o_recv)
    swap_halves = remote(
        disp_block.at[:, mine, :], disp_block.at[:, mine, :], h_send.at[0], o_recv.at[0], "gene", place.other_core
    )

    def decode(p):
        at = pl.ds(p * step, step)
        logits[...] = lax.dot_general(w_mean[at, :], hidden[...], DN_T, preferred_element_type=F32)
        lane = lax.broadcasted_iota(jnp.int32, (step, 3 * panel_count), 1)
        pick = (panel_col[at, 0:1] == lax.rem(lane, panel_count).astype(F32)).astype(F32).astype(BF16)
        thetas[...] = jnp.dot(pick, tables, preferred_element_type=F32)

        def chunk(i, lost):
            rows = pl.ds(pl.multiple_of(i * few, few), few)
            there = pl.ds(pl.multiple_of(p * step + i * few, few), few)
            nll, d_logit, d_theta = terms(
                counts[there, :].astype(F32), thetas[rows, :], logits[rows, :], rate_scale, norm_scale, 12
            )
            field[r, there, :] = d_logit.astype(BF16)
            thetas[rows, :] = d_theta
            return lost + jnp.sum(nll, axis=0, keepdims=True)

        loss[...] += lax.fori_loop(0, step // few, chunk, jnp.zeros_like(loss))
        d_theta = thetas[...]
        if p < parts - 1:
            field_gather[p].start()
        row = lax.broadcasted_iota(jnp.int32, (step, 128), 1)
        wanted = jnp.where(lax.rem(row, 8) < 4, (row // 8) * 4 + lax.rem(row, 8), -1)
        pick_t = (panel_col[at, :] == wanted.astype(F32)).astype(F32).astype(BF16)
        upper = d_theta.astype(BF16)
        lower = (d_theta - upper.astype(F32)).astype(BF16)
        panel_part[...] += lax.dot_general(pick_t, upper, DN_0, preferred_element_type=F32) + lax.dot_general(
            pick_t, lower, DN_0, preferred_element_type=F32
        )

    for copy in into:
        copy.wait_recv()
    v_gather.start()
    decode(0)
    v_gather.second()
    decode(1)
    field_gather[0].second()
    v_gather.third()
    decode(2)
    field_gather[1].second()
    field_gather[0].third()
    decode(3)

    row = lax.broadcasted_iota(jnp.int32, (128, cells), 0)
    both = jnp.where(lax.rem(row, 8) == 4, loss[...], panel_part[...])
    tile[...] = both.reshape(NG, 8, cells)
    first = Swap(place, lambda t: tile.at[t], slots, s_send, s_recv, 0)
    first.start()
    field_gather[3].start()
    slots[place.g] = tile[place.g]
    field_gather[2].second()
    field_gather[1].third()
    first.finish()
    summed = total_of(slots)
    back[place.g] = summed
    second = Swap(place, lambda t: back.at[place.g], back, s_send, s_recv, 1)
    second.start()
    cell_loss[...] = summed[4:5] / genes_all
    field_gather[3].second()
    field_gather[2].third()
    v_gather.finish()
    second.finish()
    d_panel = jnp.concatenate([back[k, 0:4] for k in range(NG)], axis=0)
    tail = jnp.exp(-jnp.abs(disp))
    d_disp = d_panel * (jnp.where(disp >= 0, 1.0, tail) / (1.0 + tail)) * norm_scale
    field[r, pl.ds(genes, panel_count), :] = d_disp.astype(BF16)
    for copy in out:
        copy.wait_send()
    disp_gather.start()

    def contract(at, size):
        total = jnp.zeros((size, columns.shape[2]), F32)
        for k in range(NR):
            total = total + jnp.dot(field[k, at, :], columns[k], preferred_element_type=F32)
        return total

    def gradient_of(p):
        field_gather[p].finish()
        gradient[pl.ds(p * step, step), :] = contract(pl.ds(p * step, step), step)

    gradient_of(0)
    gradient_of(1)
    field_gather[3].third()
    disp_gather.finish()
    disp_block[r, mine, :] = contract(mine_field, half)
    disp_gather.drain()
    spread.start()
    gradient_of(2)
    gradient_of(3)
    spread.finish()
    swap_halves.start()
    swap_halves.wait()
    for one in [v_gather, first, second, spread] + field_gather:
        one.drain()


def finish_kernel(gradient, disp_block, loss, cell_loss, grad_mean, grad_disp):
    share = grad_mean.shape[0]
    cell_loss[...] = loss[...]
    grad_mean[...] = gradient[...].T[0:share]
    for k in range(NR):
        grad_disp[:, k * share:(k + 1) * share] = disp_block[k, :, 0:share]


def hbm():
    return pl.BlockSpec(memory_space=pl.ANY)


def whole():
    return pl.BlockSpec(memory_space=pltpu.VMEM)


def params(number):
    return pltpu.CompilerParams(collective_id=number, has_side_effects=True, vmem_limit_bytes=LIMIT)


def shards(counts, panels, membership, w_proj, w_qkv_within, w_out_within, w_qkv_cross, w_out_cross, w_mean, w_disp):
    cells, genes = counts.shape
    width = w_qkv_within.shape[0]
    head = w_out_within.shape[1]
    genes_all = genes * NG
    cells_all = cells * NR
    panel_count = w_disp.shape[1]
    counts_t = counts.T
    swap_sems = [pltpu.SemaphoreType.DMA((2, NG))] * 2
    first_part = encoder_scratch(width, genes, cells, head)
    cell_loss, gradient, disp_block = pl.pallas_call(
        functools.partial(network_kernel, head, genes_all, cells_all, panel_count, len(first_part)),
        name="network",
        out_shape=(
            jax.ShapeDtypeStruct((1, cells), F32),
            jax.ShapeDtypeStruct((genes, 256), F32),
            jax.ShapeDtypeStruct((NR, panel_count, 256), F32),
        ),
        in_specs=[hbm(), whole()] + [hbm()] * 5 + [whole(), hbm(), whole()],
        out_specs=(whole(), whole(), whole()),
        scratch_shapes=first_part + [
            pltpu.VMEM((genes, cells), jnp.int32),
            pltpu.VMEM((cells, width), BF16),
            pltpu.VMEM((8, cells), F32),
            pltpu.VMEM((genes, width), BF16),
            pltpu.VMEM((NG, 8, cells), F32),
            pltpu.VMEM((NG, 8, cells), F32),
            pltpu.VMEM((NG, 8, cells), F32),
            pltpu.VMEM((NR, ROWS, 256), BF16),
            pltpu.VMEM((NR, cells, 256), BF16),
            pltpu.VMEM((NR, genes + panel_count, cells), BF16),
            pltpu.VMEM((128, cells), F32),
            pltpu.VMEM((1, cells), F32),
            pltpu.VMEM((genes, 128), F32),
            pltpu.VMEM((genes // 4, cells), F32),
            pltpu.VMEM((genes // 4, cells), F32),
            pltpu.SemaphoreType.DMA((2,)),
        ] + swap_sems + [
            pltpu.SemaphoreType.DMA((NR,)),
            pltpu.SemaphoreType.DMA((NR,)),
            pltpu.SemaphoreType.DMA((1, WideGather.SLOTS)),
            pltpu.SemaphoreType.DMA((1, WideGather.SLOTS)),
            pltpu.SemaphoreType.DMA((4, GroupGather.SLOTS)),
            pltpu.SemaphoreType.DMA((4, GroupGather.SLOTS)),
            pltpu.SemaphoreType.DMA((NR,)),
            pltpu.SemaphoreType.DMA((NR,)),
        ],
        compiler_params=params(0),
    )(
        counts_t, membership, w_proj, jnp.transpose(w_qkv_within, (2, 1, 0)), jnp.transpose(w_qkv_cross, (2, 1, 0)),
        jnp.transpose(w_out_within, (1, 0, 2)), jnp.transpose(w_out_cross, (1, 0, 2)),
        panels[None, :], w_mean.T, w_disp.T,
    )
    cell_loss, grad_mean, grad_disp = pl.pallas_call(
        finish_kernel,
        name="finish",
        out_shape=(
            jax.ShapeDtypeStruct((1, cells), F32),
            jax.ShapeDtypeStruct((width // NR, genes), F32),
            jax.ShapeDtypeStruct((panel_count, width), F32),
        ),
        in_specs=[whole()] * 3,
        out_specs=(whole(), whole(), whole()),
    )(gradient, disp_block, cell_loss)
    return cell_loss[0], grad_mean, grad_disp.T


def solution(mesh):
    return jax.shard_map(
        shards,
        mesh=mesh,
        in_specs=(
            P("grp", "gene"),
            P("gene"),
            P("grp", None),
            P("gene", None),
            P(None, "gene", None),
            P("gene", None, None),
            P(None, "gene", None),
            P("gene", None, None),
            P(None, "gene"),
            P(),
        ),
        out_specs=(P("grp"), P("grp", "gene"), P()),
        check_vma=False,
    )
```

```python
import functools
import math

import jax
import jax.numpy as jnp
from jax import lax
from jax.experimental import pallas as pl
from jax.experimental.pallas import tpu as pltpu
from jax.sharding import PartitionSpec as P

EPS = 1e-06
FLOOR = 0.3
TARGET = 10000.0
DISP_BASE = 0.5
MESH = pl.DeviceIdType.MESH
F32 = jnp.float32
BF16 = jnp.bfloat16

NX = 4
NY = 2
NG = 16
NCHIP = 8
NR = 8
NZ = 4
NM = 4
ROWS = 16
LIMIT = 64 * 1024 * 1024 - 256 * 1024
DN_T = (((1,), (1,)), ((), ()))
DN_0 = (((0,), (0,)), ((), ()))


def remote(src, dst, send, recv, axis, to):
    return pltpu.make_async_remote_copy(
        src_ref=src, dst_ref=dst, send_sem=send, recv_sem=recv, device_id={axis: to}, device_id_type=MESH
    )


class Place:
    def __init__(self):
        self.g = lax.axis_index("gene")
        self.core = lax.rem(self.g, 2)
        self.x = lax.rem(self.g // 2, NX)
        self.y = self.g // (2 * NX)
        self.right = self.at(self.y, self.shift(1), self.core)
        self.left = self.at(self.y, self.shift(3), self.core)
        self.other_y = self.at(1 - self.y, self.x, self.core)
        self.other_core = self.at(self.y, self.x, 1 - self.core)

    def shift(self, by):
        return lax.rem(self.x + by, NX)

    def at(self, y, x, core):
        return (y * NX + x) * 2 + core

    def chip(self, y, x):
        return y * NX + x


def greet(axis_peers, meanwhile):
    barrier = pltpu.get_barrier_semaphore()
    for axis, to in axis_peers:
        pl.semaphore_signal(barrier, inc=1, device_id={axis: to}, device_id_type=MESH)
    meanwhile()
    pl.semaphore_wait(barrier, len(axis_peers))


def everyone(place):
    return [("gene", lax.rem(place.g + k, NG)) for k in range(1, NG)]


def rms(values):
    return values * lax.rsqrt(jnp.mean(values * values, axis=-1, keepdims=True) + EPS)


class Scatter:
    @staticmethod
    def scratch(width, sends):
        return [
            pltpu.VMEM((NM, NCHIP, ROWS, width), BF16),
            pltpu.VMEM((NM, 3, ROWS, width), BF16),
            pltpu.VMEM((NM, 3, ROWS, width), BF16),
            pltpu.VMEM((NM, 2, ROWS, width), BF16),
            pltpu.VMEM((NM, ROWS, width), BF16),
            pltpu.VMEM((NM, ROWS, width), BF16),
            pltpu.VMEM((NM, ROWS, width), F32),
            pltpu.VMEM((2, NX, ROWS, width), BF16),
            pltpu.SemaphoreType.DMA((NM, 7)),
        ] + [pltpu.SemaphoreType.DMA((NM, 7))] * sends

    def __init__(self, place, refs):
        (self.chip, self.from_left, self.from_right, self.relay, self.y_out, self.y_in, self.mine, four, recv, send) = refs
        self.send, self.recv = send, recv
        p = self.place = place
        ahead, behind, across = p.shift(1), p.shift(3), p.shift(2)
        self.copies, self.turned = [], {}
        for m in range(NM):
            if m % 2 == 0:
                self.turned[m] = ScatterY(self, m, four.at[m // 2], 1 if m == 0 else -1)
                self.copies.append(self.turned[m].c)
                continue

            def go(slot, src, dst, to):
                return remote(src, dst, send.at[m, slot], recv.at[m, slot], "gene", to)
            self.copies.append([
                go(0, self.chip.at[m, p.chip(0, across)], self.from_left.at[m, 0], p.right),
                go(1, self.chip.at[m, p.chip(1, across)], self.from_right.at[m, 0], p.left),
                go(2, self.chip.at[m, p.chip(1, ahead)], self.from_left.at[m, 2], p.right),
                go(3, self.chip.at[m, p.chip(0, behind)], self.from_right.at[m, 2], p.left),
                go(4, self.relay.at[m, 0], self.from_left.at[m, 1], p.right),
                go(5, self.relay.at[m, 1], self.from_right.at[m, 1], p.left),
                go(6, self.y_out.at[m], self.y_in.at[m], p.other_y),
            ])

    def spread(self, m):
        if m in self.turned:
            return self.turned[m].spread()
        for k in (0, 1, 2, 3):
            self.copies[m][k].start()

    def forward(self, m):
        if m in self.turned:
            return self.turned[m].forward()
        p = self.place
        self.copies[m][0].wait_recv()
        self.relay[m, 0] = (
            self.chip[m, p.chip(0, p.shift(1))].astype(F32) + self.from_left[m, 0].astype(F32)
        ).astype(BF16)
        self.copies[m][4].start()
        self.copies[m][1].wait_recv()
        self.relay[m, 1] = (
            self.chip[m, p.chip(1, p.shift(3))].astype(F32) + self.from_right[m, 0].astype(F32)
        ).astype(BF16)
        self.copies[m][5].start()

    def cross(self, m):
        if m in self.turned:
            return self.turned[m].cross()
        p = self.place
        for k in (2, 3, 4, 5):
            self.copies[m][k].wait_recv()
        self.y_out[m] = (
            self.chip[m, p.chip(1 - p.y, p.x)].astype(F32)
            + self.from_left[m, 2 - p.y].astype(F32)
            + self.from_right[m, 1 + p.y].astype(F32)
        ).astype(BF16)
        self.copies[m][6].start()
        self.mine[m] = (
            self.chip[m, p.chip(p.y, p.x)].astype(F32)
            + self.from_left[m, 1 + p.y].astype(F32)
            + self.from_right[m, 2 - p.y].astype(F32)
        )

    def take(self, m):
        if m in self.turned:
            return self.turned[m].take()
        self.copies[m][6].wait_recv()
        return self.mine[m] + self.y_in[m].astype(F32)

    def drain(self):
        for row in self.copies:
            for copy in row:
                copy.wait_send()


class ScatterY:
    def __init__(self, base, m, y_four, way):
        p = base.place
        self.base, self.m, self.four = base, m, y_four
        to, back = (p.right, p.left) if way > 0 else (p.left, p.right)
        ahead, behind = (p.shift(1), p.shift(3)) if way > 0 else (p.shift(3), p.shift(1))
        self.order = (p.shift(2), behind, ahead)
        self.outgoing = (base.relay.at[m, 0], base.relay.at[m, 1], base.y_out.at[m])
        self.incoming = (base.from_left.at[m, 0], base.from_right.at[m, 0], base.from_left.at[m, 1])

        def go(slot, src, dst, device):
            return remote(src, dst, base.send.at[m, slot], base.recv.at[m, slot], "gene", device)

        self.c = [
            go(k, base.chip.at[m, p.chip(1 - p.y, x)], y_four.at[x], p.other_y)
            for k, x in enumerate(self.order + (p.x,))
        ] + [go(4 + k, self.outgoing[k], self.incoming[k], (to, back, to)[k]) for k in range(3)]

    def spread(self):
        for k in range(4):
            self.c[k].start()

    def total(self, k):
        p = self.base.place
        x = p.x if k == 3 else self.order[k]
        self.c[k].wait_recv()
        return self.base.chip[self.m, p.chip(p.y, x)].astype(F32) + self.four[x].astype(F32)

    def forward(self):
        for k in (0, 1):
            self.outgoing[k][...] = self.total(k).astype(BF16)
            self.c[4 + k].start()

    def cross(self):
        value = self.total(2)
        self.c[4].wait_recv()
        self.outgoing[2][...] = (value + self.incoming[0][...].astype(F32)).astype(BF16)
        self.c[6].start()
        self.base.mine[self.m] = self.total(3)

    def take(self):
        self.c[5].wait_recv()
        self.c[6].wait_recv()
        return self.base.mine[self.m] + self.incoming[1][...].astype(F32) + self.incoming[2][...].astype(F32)


def run_pipeline(steps, count=NM):
    for t in range(count + len(steps) - 1):
        for lag, step in enumerate(steps):
            if 0 <= t - lag < count:
                step(t - lag)


class Gather:
    SLOTS = 7

    def __init__(self, place, block, send, recv, index, send_index=None):
        p = place
        send_index = index if send_index is None else send_index
        ahead, behind, across = p.shift(1), p.shift(3), p.shift(2)
        y, z, x = p.y, 1 - p.y, p.x

        def go(slot, owner, to):
            ref = block(owner)
            return remote(ref, ref, send.at[send_index, slot], recv.at[index, slot], "gene", to)

        own, paired = p.chip(y, x), p.chip(z, x)
        self.c = [
            go(0, own, p.other_y),
            go(1, own, p.right),
            go(2, own, p.left),
            go(3, paired, p.right),
            go(4, paired, p.left),
            go(5, p.chip(y, behind), p.right),
            go(6, p.chip(z, ahead), p.left),
        ]

    def start(self):
        for k in (1, 2, 0):
            self.c[k].start()

    def second(self):
        c = self.c
        c[1].wait_recv()
        c[5].start()
        c[0].wait_recv()
        c[3].start()
        c[4].start()

    def third(self):
        self.c[4].wait_recv()
        self.c[6].start()

    def finish(self):
        for k in (2, 3, 5, 6):
            self.c[k].wait_recv()

    def drain(self):
        for copy in self.c:
            copy.wait_send()


class GatherX:
    def __init__(self, place, block, send, recv, index, send_index, rightward):
        p = place
        ahead, behind, across = p.shift(1), p.shift(3), p.shift(2)
        y, x = p.y, p.x
        self.rightward = rightward

        def go(slot, owner, to):
            ref = block(owner)
            return remote(ref, ref, send.at[send_index, slot], recv.at[index, slot], "gene", to)

        self.c = [
            go(0, p.chip(y, x), p.right),
            go(1, p.chip(y, x), p.left),
            go(2, p.chip(y, behind), p.right) if rightward else go(2, p.chip(y, ahead), p.left),
            go(3, p.chip(y, x), p.other_y),
            go(4, p.chip(y, behind), p.other_y),
            go(5, p.chip(y, ahead), p.other_y),
            go(6, p.chip(y, across), p.other_y),
        ]

    def start(self):
        for k in (0, 1, 3):
            self.c[k].start()

    def second(self):
        c = self.c
        for k in (0, 1):
            c[k].wait_recv()
            if self.rightward == (k == 0):
                c[2].start()
            c[4 + k].start()

    def third(self):
        self.c[2].wait_recv()
        self.c[6].start()

    def finish(self):
        for k in (3, 4, 5, 6):
            self.c[k].wait_recv()

    def drain(self):
        for copy in self.c:
            copy.wait_send()


def lead(gathers):
    for one in gathers:
        one.second()
    for one in gathers[:2]:
        one.third()


class WideGather:
    SLOTS = 15

    def __init__(self, place, block, send, recv, index):
        p = place
        core, x, y, z = p.core, p.x, p.y, 1 - p.y
        ahead, behind, across = p.shift(1), p.shift(3), p.shift(2)
        self.far = Gather(place, lambda q: block(2 * q + core), send, recv, index)
        held = [p.chip(y, x), p.chip(z, x), p.chip(y, behind), p.chip(y, ahead), p.chip(z, behind), p.chip(z, ahead),
                p.chip(y, across), p.chip(z, across)]
        self.near = []
        for k, q in enumerate(held):
            ref = block(2 * q + core)
            self.near.append(remote(ref, ref, send.at[index, 7 + k], recv.at[index, 7 + k], "gene", p.other_core))

    def start(self):
        self.far.start()
        self.near[0].start()

    def second(self):
        self.far.second()
        self.near[1].start()
        self.near[2].start()

    def third(self):
        self.far.third()
        self.near[5].start()

    def finish(self):
        self.far.finish()
        for k in (3, 4, 6, 7):
            self.near[k].start()
        for copy in self.near:
            copy.wait_recv()

    def drain(self):
        self.far.drain()
        for copy in self.near:
            copy.wait_send()


class DirectSum:
    def __init__(self, place, shares, slots, send, recv):
        p = place
        self.shares, self.slots = shares, slots
        self.chip = p.chip(p.y, p.x)
        self.c = []
        for k in range(1, NCHIP):
            to = lax.rem(self.chip + k, NCHIP)
            self.c.append(remote(shares.at[to], slots.at[k], send.at[k], recv.at[k], "gene", to * 2 + p.core))

    def start(self):
        for copy in self.c:
            copy.start()

    def take(self):
        total = self.shares[self.chip].astype(F32)
        for k in range(1, NCHIP):
            self.c[k - 1].wait_recv()
            total = total + self.slots[k].astype(F32)
        return total

    def drain(self):
        for copy in self.c:
            copy.wait_send()


class Direct:
    def __init__(self, place, block, send, recv, index):
        p = place
        chip = p.chip(p.y, p.x)
        own = block(p.g)
        self.out, self.pair = [], []
        for k in range(NCHIP):
            to, frm = lax.rem(chip + k, NCHIP) * 2 + p.core, lax.rem(chip + NCHIP - k, NCHIP) * 2 + p.core
            ref = block(frm)
            if k:
                self.out.append(remote(own, own, send.at[index, k], recv.at[index, k], "gene", to))
            self.pair.append(remote(ref, ref, send.at[index, 7 + k if k else 0], recv.at[index, 7 + k if k else 0], "gene", p.other_core))

    def start(self):
        for copy in self.out + self.pair[:1]:
            copy.start()

    def finish(self):
        for k in range(1, NCHIP):
            self.out[k - 1].wait_recv()
            self.pair[k].start()
        for copy in self.pair:
            copy.wait_recv()

    def drain(self):
        for copy in self.out + self.pair:
            copy.wait_send()


class Swap:
    def __init__(self, place, source, slots, send, recv, index):
        self.out, self.into = [], []
        for k in range(1, NG):
            to, frm = lax.rem(place.g + k, NG), lax.rem(place.g + NG - k, NG)
            self.out.append(remote(source(to), slots.at[place.g], send.at[index, k], recv.at[index, place.g], "gene", to))
            self.into.append(remote(source(frm), slots.at[frm], send.at[index, k], recv.at[index, frm], "gene", frm))

    def start(self):
        for copy in self.out:
            copy.start()

    def finish(self):
        for copy in self.into:
            copy.wait_recv()

    def drain(self):
        for copy in self.out:
            copy.wait_send()


def total_of(slots):
    total = slots[0]
    for k in range(1, NG):
        total = total + slots[k]
    return total


def group_sum(values):
    high = values.astype(BF16)
    low = (values - high.astype(F32)).astype(BF16)
    shape = (values.shape[1], values.shape[1])
    row = lax.broadcasted_iota(jnp.int32, shape, 0) // 64
    col = lax.broadcasted_iota(jnp.int32, shape, 1) // 64
    ones = (row == col).astype(F32).astype(BF16)
    return jnp.dot(high, ones, preferred_element_type=F32) + jnp.dot(low, ones, preferred_element_type=F32)


def heads_of(rows, weights, head):
    parts = [jnp.dot(rows, weights[k], preferred_element_type=F32) for k in range(3)]
    for k in range(2):
        mean = group_sum(parts[k] * parts[k]) / head
        parts[k] = (parts[k] * lax.rsqrt(jnp.maximum(mean, FLOOR))).astype(BF16)
    parts[2] = parts[2].astype(BF16)
    return parts


def turned(values, by):
    if by == 0:
        return values
    row = lax.rem(lax.broadcasted_iota(jnp.int32, values.shape, 0), ROWS)
    count = values.shape[0]
    return jnp.where(row < by, pltpu.roll(values, count - ROWS + by, 0), pltpu.roll(values, by, 0))


def within_mix(query, keys, values, head):
    q, k, v = (part.astype(F32) for part in (query, keys, values))
    count = q.shape[0]
    scores = group_sum(jnp.concatenate([q * turned(k, 4 * d) for d in range(NM)], axis=0))
    weights = [jnp.exp(scores[d * count:(d + 1) * count] * head ** (-0.5)) for d in range(NM)]
    total = weights[0] + weights[1] + weights[2] + weights[3]
    mixed = None
    for d in range(NM):
        term = (weights[d] / total).astype(BF16).astype(F32) * turned(v, 4 * d)
        mixed = term if mixed is None else mixed + term
    return mixed.astype(BF16)


def cross_mix(query, keys, values, same, head):
    lane = lax.broadcasted_iota(jnp.int32, query.shape, 1) // 64
    q = query.astype(F32)
    mixed = jnp.zeros(query.shape, F32)
    for h in range(query.shape[1] // 64):
        one = jnp.where(lane == h, q, 0.0).astype(BF16)
        scores = lax.dot_general(one, keys, DN_T, preferred_element_type=F32) * head ** (-0.5)
        weights = jnp.where(same, jnp.exp(scores), 0.0)
        probs = (weights / jnp.sum(weights, axis=-1, keepdims=True)).astype(BF16)
        mixed = jnp.where(lane == h, jnp.dot(probs, values, preferred_element_type=F32), mixed)
    return mixed.astype(BF16)


def encoder_scratch(width, genes, cells, head):
    half = cells // 2
    raw = [pltpu.VMEM((3 * head, 2, width), BF16), pltpu.VMEM((head, 2, width), BF16)]
    layer = [
        pltpu.VMEM((3, width, 256), BF16),
        pltpu.VMEM((256, width), BF16),
        pltpu.VMEM((NM, NCHIP, ROWS, width), BF16),
    ]
    return (
        [
            pltpu.VMEM((cells, genes), BF16),
            pltpu.VMEM((NM, genes, 1664), BF16),
            pltpu.VMEM((8, cells), F32),
            pltpu.VMEM((NG, 8, cells), F32),
            pltpu.VMEM((NM, NCHIP, 2, ROWS, width), BF16),
            pltpu.VMEM((NM, NCHIP, ROWS, width), BF16),
            pltpu.VMEM((128, width), F32),
            pltpu.VMEM((2, 3 * head, width), F32),
            pltpu.VMEM((NM, ROWS, width), F32),
            pltpu.VMEM((NM, ROWS, width), F32),
            pltpu.VMEM((NM, 2, 2, half, 256), BF16),
            pltpu.VMEM((NM, half, 256), BF16),
            pltpu.VMEM((cells, 128), F32),
            pltpu.SemaphoreType.DMA((NM + 4,)),
        ]
        + raw * 2
        + layer * 2
        + [pltpu.SemaphoreType.DMA((1, NG))] * 2
        + [pltpu.SemaphoreType.DMA((NM,))] * 2
        + [pltpu.SemaphoreType.DMA((NM,))] * 2
        + [pltpu.SemaphoreType.DMA((NM,))] * 2
        + [pltpu.SemaphoreType.DMA((NM, Gather.SLOTS)), pltpu.SemaphoreType.DMA((2 * NM, Gather.SLOTS))]
        + [pltpu.SemaphoreType.DMA((1, 16))] * 2
        + Scatter.scratch(width, 1)
        + Scatter.scratch(width, 0)
        + [
            pltpu.VMEM((half, width), F32),
            pltpu.VMEM((NCHIP, ROWS, width), BF16),
            pltpu.VMEM((NCHIP, ROWS, width), BF16),
            pltpu.SemaphoreType.DMA((NCHIP,)),
            pltpu.SemaphoreType.DMA((NCHIP,)),
        ]
    )


def encode(head, meet, after, counts, groups, w_hbm, q1_hbm, q2_hbm, o1_hbm, o2_hbm, hidden, library, *refs):
    (scaled, w_proj, tile, slots, halves, pair, padded, split, tokens, resid, kv, queries, spot, load_sem) = refs[:14]
    raws, layers = refs[14:18], refs[18:24]
    (s_send, s_recv, w_send, w_recv, p_send, p_recv, k_send, k_recv, a_send, a_recv, d_send, d_recv) = refs[24:36]
    sums, (gathered, shares, share_in, z_send, z_recv) = refs[36:-5], refs[-5:]
    place = Place()
    width = resid.shape[-1]
    wide = w_proj.shape[-1]
    core, here = place.core, place.chip(place.y, place.x)
    scatter = [Scatter(place, sums[0:10]), Scatter(place, sums[10:19] + sums[9:10])]
    weights, outs, blocks = layers[0::3], layers[1::3], layers[2::3]

    small = [
        pltpu.make_async_copy(src, dst, load_sem.at[NM + k])
        for k, (src, dst) in enumerate(zip((q1_hbm, o1_hbm, q2_hbm, o2_hbm), raws))
    ]
    loads = [
        pltpu.make_async_copy(w_hbm.at[:, pl.ds((m * width) // 128 * 128, wide)], w_proj.at[m], load_sem.at[m])
        for m in range(NM)
    ]

    def first():
        for load in small[:2] + loads + small[2:]:
            load.start()

    def second():
        tile[...] = jnp.broadcast_to(jnp.sum(counts[...].astype(F32), axis=0, keepdims=True), tile.shape)

    meet(first, second)
    swap = Swap(place, lambda t: tile, slots, s_send, s_recv, 0)
    swap.start()
    slots[place.g] = tile[...]

    lanes = pl.ds(pl.multiple_of(core * 128, 128), 128)
    share = []
    for k in range(2):
        share.append([
            remote(weights[k].at[:, :, lanes], weights[k].at[:, :, lanes], w_send.at[2 * k], w_recv.at[2 * k], "gene", place.other_core),
            remote(outs[k].at[lanes, :], outs[k].at[lanes, :], w_send.at[2 * k + 1], w_recv.at[2 * k + 1], "gene", place.other_core),
        ])

    def prepare(k):
        padded[...] = jnp.zeros_like(padded)
        small[2 * k].wait()
        for h in range(2):
            split[h] = raws[2 * k][:, h, :].astype(F32)
        for a in range(3):
            for h in range(2):
                padded[64 * h:64 * h + head, :] = split[h, a * head:(a + 1) * head, :]
            weights[k][a, :, lanes] = padded[...].T.astype(BF16)
        share[k][0].start()
        small[2 * k + 1].wait()
        for h in range(2):
            padded[64 * h:64 * h + head, :] = raws[2 * k + 1][:, h, :].astype(F32)
        outs[k][lanes, :] = padded[...].astype(BF16)
        share[k][1].start()

    prepare(0)
    swap.finish()
    total = 1.0 + total_of(slots)
    library[...] = total
    scaled[...] = jnp.log1p(counts[...].astype(F32) * (TARGET / total[0:1])).T.astype(BF16)

    pairs = [
        remote(halves.at[m, :, 1 - core], pair.at[m], p_send.at[m], p_recv.at[m], "gene", place.other_core)
        for m in range(NM)
    ]

    def project(m):
        loads[m].wait()
        skip = (m * width) % 128
        out = jnp.dot(scaled[...], w_proj[m], preferred_element_type=F32)[:, skip:skip + width]
        halves[m] = out.astype(BF16).reshape(NCHIP, 2, ROWS, width)
        pairs[m].start()

    def join(m):
        pairs[m].wait_recv()
        for q in range(NCHIP):
            scatter[0].chip[m, q] = (halves[m, q, core].astype(F32) + pair[m, q].astype(F32)).astype(BF16)
        scatter[0].spread(m)

    def keep(m):
        scatter[0].mine[m] = scatter[0].take(m)

    run_pipeline([project, join, scatter[0].forward, scatter[0].cross, keep])
    scatter[0].drain()

    gathers = [
        [
            GatherX(place, lambda q, k=k, m=m: blocks[k].at[m, q], a_send, a_recv, k * NM + m, m, m == 0)
            if m % 2 == 0
            else Gather(place, lambda q, k=k, m=m: blocks[k].at[m, q], a_send, a_recv, k * NM + m, m)
            for m in range(NM)
        ]
        for k in range(2)
    ]
    for s in range(NM):
        for m in range(NM):
            tokens[s, 4 * m:4 * m + 4, :] = scatter[0].mine[m, 4 * s:4 * s + 4, :]
        blocks[0][s, here] = rms(tokens[s]).astype(BF16)
        gathers[0][s].start()

    prepare(1)
    cells = 2 * kv.shape[3]
    at = lax.broadcasted_iota(jnp.int32, (cells, cells), 1)
    source = 32 * (lax.rem(at, 128) // ROWS) + ROWS * (at // 128) + lax.rem(at, ROWS)
    order = (lax.broadcasted_iota(jnp.int32, (cells, cells), 0) == source).astype(F32).astype(BF16)
    row = jnp.dot(
        jnp.broadcast_to(groups[...].astype(F32), (128, cells)).astype(BF16), order, preferred_element_type=F32
    )
    spot[...] = row.T
    same = jnp.broadcast_to(spot[lanes, 0:1], (128, cells)) == row
    for copy in share[0]:
        copy.wait_recv()

    lead(gathers[0])

    def within(s):
        gathers[0][s].finish()
        if s + 2 < NM:
            gathers[0][s + 2].third()
        rows = blocks[0][s].reshape(NCHIP * ROWS, width)
        mixed = within_mix(*heads_of(rows, weights[0], head), head)
        out = jnp.dot(mixed, outs[0][...], preferred_element_type=F32)
        scatter[1].chip[s] = out.astype(BF16).reshape(NCHIP, ROWS, width)
        scatter[1].spread(s)

    def add_within(s):
        tokens[s] = tokens[s] + scatter[1].take(s)

    run_pipeline([within, scatter[1].forward, scatter[1].cross, add_within])
    for one in gathers[0]:
        one.drain()

    for m in range(NM):
        for s in range(NM):
            resid[m, 4 * s:4 * s + 4, :] = tokens[s, 4 * m:4 * m + 4, :]
        blocks[1][m, here] = rms(resid[m]).astype(BF16)
        gathers[1][m].start()
    for copy in share[1]:
        copy.wait_recv()
    trade = [
        remote(kv.at[m, core], kv.at[m, core], k_send.at[m], k_recv.at[m], "gene", place.other_core)
        for m in range(NM)
    ]

    lead(gathers[1])

    def look(m):
        if m + 2 < NM:
            gathers[1][m + 2].third()
        gathers[1][m].finish()
        rows = blocks[1][m].reshape(NCHIP * ROWS, width)
        queries[m], kv[m, core, 0], kv[m, core, 1] = heads_of(rows, weights[1], head)
        trade[m].start()

    def attend(m):
        trade[m].wait_recv()
        keys = jnp.concatenate([kv[m, 0, 0], kv[m, 1, 0]], axis=0)
        values = jnp.concatenate([kv[m, 0, 1], kv[m, 1, 1]], axis=0)
        mixed = cross_mix(queries[m], keys, values, same, head)
        out = jnp.dot(mixed, outs[1][...], preferred_element_type=F32)
        gathered[...] = gathered[...] + out if m else out

    run_pipeline([look, attend])

    shares[...] = gathered[...].astype(BF16).reshape(NCHIP, ROWS, width)
    final = DirectSum(place, shares, share_in, z_send, z_recv)
    final.start()
    pooled = (resid[0] + resid[1] + resid[2] + resid[3] + final.take()) * (1.0 / NM)
    hidden[pl.ds(pl.multiple_of(place.g * ROWS, ROWS), ROWS), :] = rms(pooled).astype(BF16)
    last = Direct(
        place, lambda o: hidden.at[pl.ds(pl.multiple_of(o * ROWS, ROWS), ROWS), :], d_send, d_recv, 0
    )
    last.start()
    after()
    last.finish()
    for one in scatter[1:] + gathers[1] + [swap, final, last]:
        one.drain()
    for copy in share[0] + share[1] + pairs + trade:
        copy.wait_send()


class GroupGather:
    SLOTS = 7

    def __init__(self, r, block, send, recv, index):
        z, h = lax.rem(r, NZ), r // NZ
        up, down = lax.rem(z + 1, NZ), lax.rem(z + 3, NZ)
        k = 1 - h

        def at(a, b):
            return a * NZ + b

        def go(slot, owner, to):
            ref = block(owner)
            return remote(ref, ref, send.at[index, slot], recv.at[index, slot], "grp", to)

        self.c = [
            go(0, at(h, z), at(k, z)),
            go(1, at(h, z), at(h, up)),
            go(2, at(h, z), at(h, down)),
            go(3, at(k, z), at(h, up)),
            go(4, at(k, z), at(h, down)),
            go(5, at(h, down), at(h, up)),
            go(6, at(k, up), at(h, down)),
        ]

    def start(self):
        for k in (1, 2, 0):
            self.c[k].start()

    def second(self):
        c = self.c
        c[1].wait_recv()
        c[5].start()
        c[0].wait_recv()
        c[3].start()
        c[4].start()

    def third(self):
        self.c[4].wait_recv()
        self.c[6].start()

    def finish(self):
        for k in (2, 3, 5, 6):
            self.c[k].wait_recv()

    def drain(self):
        for copy in self.c:
            copy.wait_send()


class GroupGatherZ:
    def __init__(self, r, block, send, recv, index, upward):
        z, h = lax.rem(r, NZ), r // NZ
        up, down, across = lax.rem(z + 1, NZ), lax.rem(z + 3, NZ), lax.rem(z + 2, NZ)
        k = 1 - h
        self.upward = upward

        def at(a, b):
            return a * NZ + b

        def go(slot, owner, to):
            ref = block(owner)
            return remote(ref, ref, send.at[index, slot], recv.at[index, slot], "grp", to)

        self.c = [
            go(0, at(h, z), at(h, up)),
            go(1, at(h, z), at(h, down)),
            go(2, at(h, down), at(h, up)) if upward else go(2, at(h, up), at(h, down)),
            go(3, at(h, z), at(k, z)),
            go(4, at(h, down), at(k, z)),
            go(5, at(h, up), at(k, z)),
            go(6, at(h, across), at(k, z)),
        ]

    def start(self):
        for k in (0, 1, 3):
            self.c[k].start()

    def second(self):
        c = self.c
        for k in (0, 1):
            c[k].wait_recv()
            if self.upward == (k == 0):
                c[2].start()
            c[4 + k].start()

    def third(self):
        self.c[2].wait_recv()
        self.c[6].start()

    def finish(self):
        for k in (3, 4, 5, 6):
            self.c[k].wait_recv()

    def drain(self):
        for copy in self.c:
            copy.wait_send()


class GroupDirect:
    def __init__(self, r, block, send, recv):
        self.out, self.into = [], []
        for k in range(1, NR):
            to, frm = lax.rem(r + k, NR), lax.rem(r + NR - k, NR)
            self.out.append(remote(block(r), block(r), send.at[k], recv.at[k], "grp", to))
            self.into.append(remote(block(r), block(frm), send.at[k], recv.at[k], "grp", frm))

    def start(self):
        for copy in self.out:
            copy.start()

    def finish(self):
        for copy in self.into:
            copy.wait_recv()

    def drain(self):
        for copy in self.out:
            copy.wait_send()


def log_factorials(count):
    return [math.log(math.factorial(k)) for k in range(count)]


def terms(x, theta, logit, rate_scale, norm_scale, most):
    tail = jnp.exp(-jnp.abs(logit))
    soft = jnp.maximum(logit, 0.0) + jnp.log1p(tail)
    sigmoid = jnp.where(logit >= 0, 1.0, tail) / (1.0 + tail)
    rate = rate_scale * soft
    product = jnp.ones_like(theta)
    slope = jnp.zeros_like(theta)
    log_factorial = jnp.zeros_like(theta)
    table = log_factorials(most + 1)
    for k in range(most):
        on = x > k
        term = theta + float(k)
        slope = jnp.where(on, slope * term + product, slope)
        product = jnp.where(on, product * term, product)
        if k:
            log_factorial = jnp.where(on, table[k + 1], log_factorial)
    total = theta + rate
    log_total = jnp.log(total)
    log_theta = jnp.log(theta)
    ratio = (theta + x) / total
    nll = -(
        jnp.log(product) - log_factorial
        + theta * (log_theta - log_total)
        + x * (jnp.log(rate) - log_total)
    )
    d_logit = (ratio - x / rate) * rate_scale * sigmoid * norm_scale
    d_theta = -(slope / product + log_theta + 1.0 - log_total - ratio)
    return nll, d_logit, d_theta


def network_kernel(
    head, genes_all, cells_all, panel_count, encoder_count,
    counts_hbm, groups, w_hbm, q1_hbm, q2_hbm, o1_hbm, o2_hbm, panel_row, w_mean_hbm, w_disp,
    cell_loss, gradient, disp_block, *refs,
):
    (
        counts, hidden, library, w_mean, tile, slots, back, piece, columns, field, panel_part, loss, panel_col, logits, thetas, mean_sem,
        s_send, s_recv, h_send, h_recv, v_send, v_recv, f_send, f_recv, d_recv, o_recv,
    ) = refs[encoder_count:]
    place = Place()
    r = lax.axis_index("grp")
    genes, cells = counts.shape
    width = hidden.shape[1]
    share = width // NR
    parts = 4
    few = 48
    sizes = [genes * k // 20 for k in (6, 6, 5, 3)]
    starts = [sum(sizes[:k]) for k in range(parts)]
    norm_scale = cells_all ** (-0.5)
    rows = pl.ds(pl.multiple_of(place.g * ROWS, ROWS), ROWS)
    out, into = [], []
    for k in range(1, NR):
        to, frm = lax.rem(r + k, NR), lax.rem(r + NR - k, NR)
        out.append(remote(piece.at[to], columns.at[r, rows], h_send.at[k], h_recv.at[r], "grp", to))
        into.append(remote(piece.at[frm], columns.at[frm, rows], h_send.at[k], h_recv.at[frm], "grp", frm))
    load_mean = pltpu.make_async_copy(w_mean_hbm, w_mean, mean_sem.at[0])
    load_counts = pltpu.make_async_copy(counts_hbm, counts, mean_sem.at[1])

    def early():
        panel_col[...] = jnp.broadcast_to(panel_row[...].astype(F32), (128, genes)).T
        piece[...] = jnp.zeros_like(piece)
        panel_part[...] = jnp.zeros_like(panel_part)
        loss[...] = jnp.zeros_like(loss)

    def after():
        own = hidden[rows, :].astype(F32)
        for k in range(NR):
            piece[k, :, 0:share] = own[:, k * share:(k + 1) * share].astype(BF16)
        for copy in out:
            copy.start()
        columns[r, rows] = piece[r]

    def meet(start, finish):
        def meanwhile():
            load_counts.start()
            start()
            load_mean.start()
            early()
            load_counts.wait()
            finish()

        greet(everyone(place) + [("grp", lax.rem(r + k, NR)) for k in range(1, NR)], meanwhile)

    encode(
        head, meet, after, counts, groups, w_hbm, q1_hbm, q2_hbm, o1_hbm, o2_hbm, hidden, library, *refs[:encoder_count]
    )
    load_mean.wait()
    disp = lax.dot_general(w_disp[...], hidden[...], DN_T, preferred_element_type=F32)
    table = DISP_BASE + (jnp.maximum(disp, 0.0) + jnp.log1p(jnp.exp(-jnp.abs(disp))))
    high = table.astype(BF16)
    rest = table - high.astype(F32)
    middle = rest.astype(BF16)
    low = (rest - middle.astype(F32)).astype(BF16)
    tables = jnp.concatenate([high, middle, low], axis=0)
    rate_scale = library[0:1] / genes_all

    v_gather = WideGather(
        place, lambda o: columns.at[:, pl.ds(pl.multiple_of(o * ROWS, ROWS), ROWS), :], v_send, v_recv, 0
    )
    field_gather = []
    for p in range(parts):
        block = lambda o, p=p: field.at[o, pl.ds(starts[p], sizes[p]), :]
        field_gather.append(
            GroupGatherZ(r, block, f_send, f_recv, p, True) if p == 0 else GroupGather(r, block, f_send, f_recv, p)
        )
    half = panel_count // 2
    mine = pl.ds(pl.multiple_of(place.core * half, half), half)
    mine_field = pl.ds(pl.multiple_of(genes + place.core * half, half), half)
    disp_gather = GroupDirect(r, lambda o: field.at[o, mine_field, :], h_send, d_recv)
    spread = GroupDirect(r, lambda o: disp_block.at[o, mine, :], h_send, o_recv)
    swap_halves = remote(
        disp_block.at[:, mine, :], disp_block.at[:, mine, :], h_send.at[0], o_recv.at[0], "gene", place.other_core
    )

    def decode(p):
        step = sizes[p]
        at = pl.ds(starts[p], step)
        logits[0:step, :] = lax.dot_general(w_mean[at, :], hidden[...], DN_T, preferred_element_type=F32)
        lane = lax.broadcasted_iota(jnp.int32, (step, 3 * panel_count), 1)
        pick = (panel_col[at, 0:1] == lax.rem(lane, panel_count).astype(F32)).astype(F32).astype(BF16)
        thetas[0:step, :] = jnp.dot(pick, tables, preferred_element_type=F32)

        def chunk(i, lost):
            rows = pl.ds(pl.multiple_of(i * few, few), few)
            there = pl.ds(pl.multiple_of(starts[p] + i * few, few), few)
            nll, d_logit, d_theta = terms(
                counts[there, :].astype(F32), thetas[rows, :], logits[rows, :], rate_scale, norm_scale, 12
            )
            field[r, there, :] = d_logit.astype(BF16)
            thetas[rows, :] = d_theta
            return lost + jnp.sum(nll, axis=0, keepdims=True)

        loss[...] += lax.fori_loop(0, step // few, chunk, jnp.zeros_like(loss))
        d_theta = thetas[0:step, :]
        if p < parts - 1:
            field_gather[p].start()
        row = lax.broadcasted_iota(jnp.int32, (step, 128), 1)
        wanted = jnp.where(lax.rem(row, 8) < 4, (row // 8) * 4 + lax.rem(row, 8), -1)
        pick_t = (panel_col[at, :] == wanted.astype(F32)).astype(F32).astype(BF16)
        upper = d_theta.astype(BF16)
        lower = (d_theta - upper.astype(F32)).astype(BF16)
        panel_part[...] += lax.dot_general(pick_t, upper, DN_0, preferred_element_type=F32) + lax.dot_general(
            pick_t, lower, DN_0, preferred_element_type=F32
        )

    for copy in into:
        copy.wait_recv()
    v_gather.start()
    decode(0)
    v_gather.second()
    decode(1)
    field_gather[0].second()
    v_gather.third()
    decode(2)
    field_gather[1].second()
    field_gather[0].third()
    decode(3)

    row = lax.broadcasted_iota(jnp.int32, (128, cells), 0)
    both = jnp.where(lax.rem(row, 8) == 4, loss[...], panel_part[...])
    tile[...] = both.reshape(NG, 8, cells)
    first = Swap(place, lambda t: tile.at[t], slots, s_send, s_recv, 0)
    first.start()
    field_gather[3].start()
    slots[place.g] = tile[place.g]
    field_gather[2].second()
    field_gather[1].third()
    first.finish()
    summed = total_of(slots)
    back[place.g] = summed
    second = Swap(place, lambda t: back.at[place.g], back, s_send, s_recv, 1)
    second.start()
    cell_loss[...] = summed[4:5] / genes_all
    field_gather[3].second()
    field_gather[2].third()
    v_gather.finish()
    second.finish()
    d_panel = jnp.concatenate([back[k, 0:4] for k in range(NG)], axis=0)
    tail = jnp.exp(-jnp.abs(disp))
    d_disp = d_panel * (jnp.where(disp >= 0, 1.0, tail) / (1.0 + tail)) * norm_scale
    field[r, pl.ds(genes, panel_count), :] = d_disp.astype(BF16)
    for copy in out:
        copy.wait_send()
    disp_gather.start()

    def contract(at, size):
        total = jnp.zeros((size, columns.shape[2]), F32)
        for k in range(NR):
            total = total + jnp.dot(field[k, at, :], columns[k], preferred_element_type=F32)
        return total

    def gradient_of(p):
        field_gather[p].finish()
        gradient[pl.ds(starts[p], sizes[p]), :] = contract(pl.ds(starts[p], sizes[p]), sizes[p])

    gradient_of(0)
    gradient_of(1)
    field_gather[3].third()
    disp_gather.finish()
    disp_block[r, mine, :] = contract(mine_field, half)
    disp_gather.drain()
    spread.start()
    gradient_of(2)
    gradient_of(3)
    spread.finish()
    swap_halves.start()
    swap_halves.wait()
    for one in [v_gather, first, second, spread] + field_gather:
        one.drain()


def finish_kernel(gradient, disp_block, loss, cell_loss, grad_mean, grad_disp):
    share = grad_mean.shape[0]
    cell_loss[...] = loss[...]
    grad_mean[...] = gradient[...].T[0:share]
    for k in range(NR):
        grad_disp[:, k * share:(k + 1) * share] = disp_block[k, :, 0:share]


def hbm():
    return pl.BlockSpec(memory_space=pl.ANY)


def whole():
    return pl.BlockSpec(memory_space=pltpu.VMEM)


def params(number):
    return pltpu.CompilerParams(collective_id=number, has_side_effects=True, vmem_limit_bytes=LIMIT)


def shards(counts, panels, membership, w_proj, w_qkv_within, w_out_within, w_qkv_cross, w_out_cross, w_mean, w_disp):
    cells, genes = counts.shape
    width = w_qkv_within.shape[0]
    head = w_out_within.shape[1]
    genes_all = genes * NG
    cells_all = cells * NR
    panel_count = w_disp.shape[1]
    counts_t = counts.T
    swap_sems = [pltpu.SemaphoreType.DMA((2, NG))] * 2
    first_part = encoder_scratch(width, genes, cells, head)
    cell_loss, gradient, disp_block = pl.pallas_call(
        functools.partial(network_kernel, head, genes_all, cells_all, panel_count, len(first_part)),
        name="network",
        out_shape=(
            jax.ShapeDtypeStruct((1, cells), F32),
            jax.ShapeDtypeStruct((genes, 256), F32),
            jax.ShapeDtypeStruct((NR, panel_count, 256), F32),
        ),
        in_specs=[hbm(), whole()] + [hbm()] * 5 + [whole(), hbm(), whole()],
        out_specs=(whole(), whole(), whole()),
        scratch_shapes=first_part + [
            pltpu.VMEM((genes, cells), jnp.int32),
            pltpu.VMEM((cells, width), BF16),
            pltpu.VMEM((8, cells), F32),
            pltpu.VMEM((genes, width), BF16),
            pltpu.VMEM((NG, 8, cells), F32),
            pltpu.VMEM((NG, 8, cells), F32),
            pltpu.VMEM((NG, 8, cells), F32),
            pltpu.VMEM((NR, ROWS, 256), BF16),
            pltpu.VMEM((NR, cells, 256), BF16),
            pltpu.VMEM((NR, genes + panel_count, cells), BF16),
            pltpu.VMEM((128, cells), F32),
            pltpu.VMEM((1, cells), F32),
            pltpu.VMEM((genes, 128), F32),
            pltpu.VMEM((genes * 6 // 20, cells), F32),
            pltpu.VMEM((genes * 6 // 20, cells), F32),
            pltpu.SemaphoreType.DMA((2,)),
        ] + swap_sems + [
            pltpu.SemaphoreType.DMA((NR,)),
            pltpu.SemaphoreType.DMA((NR,)),
            pltpu.SemaphoreType.DMA((1, WideGather.SLOTS)),
            pltpu.SemaphoreType.DMA((1, WideGather.SLOTS)),
            pltpu.SemaphoreType.DMA((4, GroupGather.SLOTS)),
            pltpu.SemaphoreType.DMA((4, GroupGather.SLOTS)),
            pltpu.SemaphoreType.DMA((NR,)),
            pltpu.SemaphoreType.DMA((NR,)),
        ],
        compiler_params=params(0),
    )(
        counts_t, membership, w_proj, jnp.transpose(w_qkv_within, (2, 1, 0)), jnp.transpose(w_qkv_cross, (2, 1, 0)),
        jnp.transpose(w_out_within, (1, 0, 2)), jnp.transpose(w_out_cross, (1, 0, 2)),
        panels[None, :], w_mean.T, w_disp.T,
    )
    cell_loss, grad_mean, grad_disp = pl.pallas_call(
        finish_kernel,
        name="finish",
        out_shape=(
            jax.ShapeDtypeStruct((1, cells), F32),
            jax.ShapeDtypeStruct((width // NR, genes), F32),
            jax.ShapeDtypeStruct((panel_count, width), F32),
        ),
        in_specs=[whole()] * 3,
        out_specs=(whole(), whole(), whole()),
    )(gradient, disp_block, cell_loss)
    return cell_loss[0], grad_mean, grad_disp.T


def solution(mesh):
    return jax.shard_map(
        shards,
        mesh=mesh,
        in_specs=(
            P("grp", "gene"),
            P("gene"),
            P("grp", None),
            P("gene", None),
            P(None, "gene", None),
            P("gene", None, None),
            P(None, "gene", None),
            P("gene", None, None),
            P(None, "gene"),
            P(),
        ),
        out_specs=(P("grp"), P("grp", "gene"), P()),
        check_vma=False,
    )
```
